32 devices in a mesh: dp: 16 (over z, x, core), tensor: 2 (over y).
Axes of the slice: x: 2, y: 2, z: 4, core: 2. Of those that a mesh axis runs over, the one named last changes fastest.
Arguments:
- tokens: bfloat16 [32768, 768], P(('dp', 'tensor')), may hold values from -6 to 6
- timesteps: int32 [32], replicated, may hold values from 0 to 999
- norm_gains: bfloat16 [2, 768], P(None, ('dp', 'tensor')), may hold values from 0.5 to 1.5
- biases: bfloat16 [5, 768], P(None, ('dp', 'tensor')), may hold values from -2 to 2
- second_shift: bfloat16 [768], P(('dp', 'tensor')), may hold values from -2 to 2
- hidden_bias: bfloat16 [3072], P(('dp', 'tensor')), may hold values from -3 to 3
- step_table: bfloat16 [1000, 768], P(None, ('dp', 'tensor')), may hold values from -3 to 3
- qkv_weight: bfloat16 [3, 768, 768], P(None, 'dp', 'tensor'), may hold values from -0.21875 to 0.21875
- out_weight: bfloat16 [768, 768], P('tensor', 'dp'), may hold values from -2 to 2
- up_weight: bfloat16 [768, 3072], P('dp', 'tensor'), may hold values from -0.21875 to 0.21875
- down_weight: bfloat16 [3072, 768], P('tensor', 'dp'), may hold values from -0.109375 to 0.109375
- cotangent: bfloat16 [32768, 768], P(('dp', 'tensor')), may hold values from -6 to 6
Outputs:
- layer_out: bfloat16 [32768, 768], P(('dp', 'tensor'))
- grad_tokens: float32 [32768, 768], P(('dp', 'tensor'))
- grad_gains: float32 [2, 768], P(None, ('dp', 'tensor'))
- grad_biases: float32 [5, 768], P(None, ('dp', 'tensor'))
- grad_second_shift: float32 [768], P(('dp', 'tensor'))
- grad_hidden: float32 [3072], P(('dp', 'tensor'))
- grad_table: float32 [1000, 768], P(None, ('dp', 'tensor'))
- grad_qkv: float32 [3, 768, 768], P(None, 'dp', 'tensor')
- grad_out: float32 [768, 768], P('tensor', 'dp')
- grad_up: float32 [768, 3072], P('dp', 'tensor')
- grad_down: float32 [3072, 768], P('tensor', 'dp')
The draws below stay inside these ranges and needn't reach their ends.
All inputs are finite; a program needn't handle non-finite values.
Results may differ from the reference program's by a relative error of at most 0.014.
Values may be sent and summed in bfloat16 or wider, within the bound.
A program may use at most 192 MiB of HBM per device.

```python
import jax
import jax.numpy as jnp
from jax import lax

D = 768
HEADS = 12
HEAD_DIM = 64
FF = 3072
TSTEPS = 1000
LEN = 1024
BLOCK = 256
SEQS = 32
TOKENS = 32768


def with_ends(values, key, least, high):
    extent = values.shape
    place = [jax.random.randint(jax.random.fold_in(key, axis), (), 0, extent[axis]) for axis in range(len(extent))]
    values = values.at[tuple(place)].set(least)
    longest = extent.index(max(extent))
    place[longest] = (place[longest] + 1) % extent[longest]
    return values.at[tuple(place)].set(high)


def spiked(values, own_key, source, target, blocks, factor):
    owner, partner = [(jnp.arange(values.shape[dim]) // (values.shape[dim] // blocks)).reshape([-1 if axis == dim else 1 for axis in range(values.ndim)]) for dim in (source, target)]
    chosen = jax.random.permutation(own_key, blocks)[partner]
    strong = (owner == chosen) | (owner == (partner + blocks // 2) % blocks)
    return jnp.where(strong, factor * values, values)


def levels(own_key, dims, cuts, least, largest):
    level, own = 1.0, jax.random.fold_in(own_key, 6)
    for dim, blocks in cuts:
        steps = jnp.exp(jax.random.uniform(jax.random.fold_in(own, dim), (blocks,), jnp.float32, least / len(cuts), largest / len(cuts)))
        level = level * jnp.repeat(steps, dims[dim] // blocks).reshape([-1 if axis == dim else 1 for axis in range(len(dims))])
    return level


def normal_values(rng, extent, width, limit, cuts=(), dtype=jnp.bfloat16):
    entries = width * jax.random.normal(rng, extent, jnp.float32)
    if cuts:
        entries = entries * levels(rng, extent, cuts, -0.22, 0.18)
    return jnp.clip(entries, -limit, limit).astype(dtype)


def heavy_noise(stream_key, extent, scale, limit, split, heavy, held_as=jnp.bfloat16):
    entries = scale * jax.random.normal(stream_key, extent, jnp.float32)
    if split:
        entries = entries * levels(stream_key, extent, split, -0.22, 0.18)
    return jnp.clip(spiked(entries, jax.random.fold_in(stream_key, 3), *heavy), -limit, limit).astype(held_as)


def setup_inputs(seed: int = 0) -> dict:
    keys = jax.random.split(jax.random.key(seed), 13)
    return {
        "tokens": heavy_noise(keys[0], (TOKENS, D), 1.0, 6.0, ((0, 32),), (0, 1, 32, 2.75)),
        "timesteps": with_ends(jax.random.randint(keys[1], (SEQS,), 0, TSTEPS), jax.random.fold_in(keys[1], 1), 0, TSTEPS - 1).astype(jnp.int32),
        "norm_gains": jnp.clip(1.0 + 0.1 * jax.random.normal(keys[2], (2, D), jnp.float32), 0.5, 1.5).astype(jnp.bfloat16),
        "biases": normal_values(keys[3], (5, D), 0.3, 2.0, ((1, 32),)),
        "second_shift": normal_values(keys[4], (D,), 0.3, 2.0, ((0, 32),)),
        "hidden_bias": normal_values(keys[5], (FF,), 0.5, 3.0, ((0, 32),)),
        "step_table": normal_values(keys[6], (TSTEPS, D), 0.5, 3.0, ((1, 32),)),
        "qkv_weight": normal_values(keys[7], (3, D, D), D ** -0.5, 0.21875, ((1, 16), (2, 2))),
        "out_weight": normal_values(keys[8], (D, D), (D // 96) ** -0.5, 2.0, ((0, 2), (1, 16))),
        "up_weight": normal_values(keys[9], (D, FF), D ** -0.5, 0.21875, ((0, 16), (1, 2))),
        "down_weight": normal_values(keys[10], (FF, D), FF ** -0.5, 0.109375, ((0, 2), (1, 16))),
        "cotangent": heavy_noise(keys[11], (TOKENS, D), 1.0, 6.0, ((0, 32),), (0, 1, 32, 2.75)),
    }


@jax.custom_vjp
def low(v):
    return lax.optimization_barrier(v.astype(jnp.bfloat16)).astype(jnp.float32)

@jax.custom_vjp
def low_back(v):
    return v

def low_keep(v):
    return (low(v), None)

def low_pass(kept, grad):
    return (grad,)

def back_keep(v):
    return (v, None)

def back_low(kept, grad):
    return (low(grad),)
low.defvjp(low_keep, low_pass)
low_back.defvjp(back_keep, back_low)
EPS = 1e-05
HIGH = lax.Precision.HIGHEST

def both_ways(value):
    return low_back(low(value))

def layer_norm(hidden, gain, shift):
    average = lax.optimization_barrier(jnp.mean(hidden, axis=-1, keepdims=True))
    centered = hidden - average
    variance = lax.optimization_barrier(jnp.mean(centered * centered, axis=-1, keepdims=True))
    return centered * lax.rsqrt(variance + EPS) * gain + shift

def matmul(left, right):
    return jnp.dot(left, right, precision=HIGH, preferred_element_type=jnp.float32)

def attend_one(triple):
    queries, keys_seq, values_seq = triple
    query_heads = queries.reshape(LEN, HEADS, HEAD_DIM)
    key_heads = keys_seq.reshape(LEN, HEADS, HEAD_DIM)
    value_heads = values_seq.reshape(LEN, HEADS, HEAD_DIM)
    scores = jnp.einsum('qhd,khd->hqk', query_heads, key_heads, precision=HIGH) * HEAD_DIM ** (-0.5)
    position = jnp.arange(LEN)
    allowed = position[:, None] // BLOCK >= position[None, :] // BLOCK
    scores = low_back(jnp.where(allowed[None], scores, -1e+30))
    chances = low(jax.nn.softmax(scores, axis=-1))
    mixed = jnp.einsum('hqk,khd->qhd', chances, value_heads, precision=HIGH)
    return mixed.reshape(LEN, D)

def forward(tokens, norm_gains, biases, second_shift, hidden_bias, step_table, qkv_weight, out_weight, up_weight, down_weight, timesteps):
    embed = step_table[timesteps]
    start = (tokens.reshape(SEQS, LEN, D) + embed[:, None, :]).reshape(SEQS * LEN, D)
    normed = low(layer_norm(start, norm_gains[0], biases[0]))
    queries = both_ways(matmul(normed, qkv_weight[0]) + biases[1])
    keys_all = both_ways(matmul(normed, qkv_weight[1]))
    values_all = both_ways(matmul(normed, qkv_weight[2]) + biases[2])
    mixed = lax.map(jax.checkpoint(attend_one), (queries.reshape(SEQS, LEN, D), keys_all.reshape(SEQS, LEN, D), values_all.reshape(SEQS, LEN, D)))
    mixed = both_ways(mixed.reshape(SEQS * LEN, D))
    attn_out = low_back(matmul(mixed, out_weight) + biases[3])
    middle = start + attn_out
    second = low(layer_norm(middle, norm_gains[1], second_shift))
    pre_act = low_back(matmul(second, up_weight) + hidden_bias)
    activated = low(jax.nn.gelu(pre_act))
    mlp_out = low_back(matmul(activated, down_weight) + biases[4])
    return middle + mlp_out

def reference(tokens, timesteps, norm_gains, biases, second_shift, hidden_bias, step_table, qkv_weight, out_weight, up_weight, down_weight, cotangent):
    floats = [array.astype(jnp.float32) for array in (tokens, norm_gains, biases, second_shift, hidden_bias, step_table, qkv_weight, out_weight, up_weight, down_weight)]

    def runner(*params):
        return forward(*params, timesteps)
    result, pullback = jax.vjp(runner, *floats)
    grads = pullback(cotangent.astype(jnp.float32))
    return (result.astype(jnp.bfloat16), grads[0], grads[1], grads[2], grads[3], grads[4], grads[5], grads[6], grads[7], grads[8], grads[9])
```

```python
import functools

import jax
import jax.numpy as jnp
from jax import lax
from jax.experimental import pallas as pl
from jax.experimental.pallas import tpu as pltpu
from jax.sharding import PartitionSpec as P

HEAD_DIM = 64
TSTEPS = 1000
LEN = 1024
BLOCK = 256
QBLK = 512


EPS = 1e-05
NEGATIVE = -1e30
HIGH = lax.Precision.HIGHEST
VMEM_LIMIT = 62 * 1024 * 1024


def layer_norm(hidden, gain, shift):
    average = jnp.mean(hidden, axis=-1, keepdims=True)
    centered = hidden - average
    variance = jnp.mean(centered * centered, axis=-1, keepdims=True)
    return centered * lax.rsqrt(variance + EPS) * gain + shift


def gather_rows(values):
    return lax.all_gather(values, "tensor", axis=0, tiled=True)


def sum_rows(values):
    return lax.psum_scatter(
        values.astype(jnp.bfloat16), "tensor", scatter_dimension=0, tiled=True
    ).astype(jnp.float32)


def fetch_attn(qkv_weight, out_weight):
    return (
        lax.all_gather(qkv_weight, "dp", axis=1, tiled=True),
        lax.all_gather(out_weight, "dp", axis=1, tiled=True),
    )


def fetch_mlp(up_weight, down_weight):
    return (
        lax.all_gather(up_weight, "dp", axis=0, tiled=True),
        lax.all_gather(down_weight, "dp", axis=1, tiled=True),
    )


def place_part(part, whole_len, offset):
    return lax.dynamic_update_slice_in_dim(jnp.zeros((whole_len,), jnp.float32), part, offset, 0)


def contract_rows(left, right):
    return lax.dot_general(
        left, right, (((0,), (0,)), ((), ())), preferred_element_type=jnp.float32
    )


def contract_cols(left, right):
    return lax.dot_general(
        left, right, (((1,), (1,)), ((), ())), preferred_element_type=jnp.float32
    )


def block_mask(start):
    query_pos = start + jnp.arange(QBLK)
    key_pos = jnp.arange(LEN)
    return query_pos[:, None] // BLOCK >= key_pos[None, :] // BLOCK


def split_heads(values):
    return values.reshape(values.shape[0], values.shape[1] // HEAD_DIM, HEAD_DIM)


def masked_scores(query_heads, key_heads, start, scale):
    scores = (
        jnp.einsum("qhd,khd->hqk", query_heads, key_heads, preferred_element_type=jnp.float32)
        * scale
    )
    return jnp.where(block_mask(start)[None], scores, NEGATIVE)


def block_slices(queries, keys_all, values_all, index):
    per_seq = LEN // QBLK
    seq_start = index // per_seq * LEN
    start = index % per_seq * QBLK
    query_blk = lax.dynamic_slice_in_dim(queries, seq_start + start, QBLK, 0)
    key_seq = lax.dynamic_slice_in_dim(keys_all, seq_start, LEN, 0)
    value_seq = lax.dynamic_slice_in_dim(values_all, seq_start, LEN, 0)
    return (seq_start, start, query_blk, key_seq, value_seq)


def run_attention(queries, keys_all, values_all, scale):
    total_rows = queries.shape[0]

    def run_advance(carry, index):
        seq_start, start, query_blk, key_seq, value_seq = block_slices(
            queries, keys_all, values_all, index
        )
        scores = masked_scores(split_heads(query_blk), split_heads(key_seq), start, scale)
        largest = jnp.max(scores, axis=-1, keepdims=True)
        expo = jnp.exp(scores - largest)
        totals = jnp.sum(expo, axis=-1, keepdims=True)
        chances = (expo / totals).astype(jnp.bfloat16)
        log_total = (largest + jnp.log(totals))[..., 0]
        mixed = jnp.einsum(
            "hqk,khd->qhd", chances, split_heads(value_seq), preferred_element_type=jnp.float32
        )
        return (carry, (mixed.reshape(QBLK, -1).astype(jnp.bfloat16), log_total))

    unused, (mixed, log_total) = lax.scan(run_advance, 0, jnp.arange(total_rows // QBLK))
    return (mixed.reshape(total_rows, -1), log_total)


def attention_back(queries, keys_all, values_all, grad_mixed, log_total, scale):
    total_rows = queries.shape[0]
    zeros = jnp.zeros(queries.shape, jnp.float32)

    def attention_advance(carry, inputs):
        grad_keys, grad_values = carry
        index, log_blk = inputs
        seq_start, start, query_blk, key_seq, value_seq = block_slices(
            queries, keys_all, values_all, index
        )
        grad_blk = lax.dynamic_slice_in_dim(grad_mixed, seq_start + start, QBLK, 0)
        query_heads = split_heads(query_blk)
        key_heads = split_heads(key_seq)
        grad_heads = split_heads(grad_blk)
        scores = masked_scores(query_heads, key_heads, start, scale)
        chances = jnp.exp(scores - log_blk[..., None])
        grad_probs = jnp.einsum(
            "qhd,khd->hqk", grad_heads, split_heads(value_seq), preferred_element_type=jnp.float32
        )
        inner = jnp.sum(chances * grad_probs, axis=-1, keepdims=True)
        grad_scores = (chances * (grad_probs - inner)).astype(jnp.bfloat16)
        grad_query = (
            jnp.einsum("hqk,khd->qhd", grad_scores, key_heads, preferred_element_type=jnp.float32)
            * scale
        )
        grad_key = (
            jnp.einsum("hqk,qhd->khd", grad_scores, query_heads, preferred_element_type=jnp.float32)
            * scale
        )
        grad_value = jnp.einsum(
            "hqk,qhd->khd",
            chances.astype(jnp.bfloat16),
            grad_heads,
            preferred_element_type=jnp.float32,
        )
        old_keys = lax.dynamic_slice_in_dim(grad_keys, seq_start, LEN, 0)
        old_values = lax.dynamic_slice_in_dim(grad_values, seq_start, LEN, 0)
        grad_keys = lax.dynamic_update_slice_in_dim(
            grad_keys, old_keys + grad_key.reshape(LEN, -1), seq_start, 0
        )
        grad_values = lax.dynamic_update_slice_in_dim(
            grad_values, old_values + grad_value.reshape(LEN, -1), seq_start, 0
        )
        return ((grad_keys, grad_values), grad_query.reshape(QBLK, -1))

    (grad_keys, grad_values), grad_queries = lax.scan(
        attention_advance, (zeros, zeros), (jnp.arange(total_rows // QBLK), log_total)
    )
    return (grad_queries.reshape(total_rows, -1), grad_keys, grad_values)


def shards(
    tokens,
    timesteps,
    norm_gains,
    biases,
    second_shift,
    hidden_bias,
    step_table,
    qkv_weight,
    out_weight,
    up_weight,
    down_weight,
    cotangent,
):
    width = tokens.shape[1]
    half_width = qkv_weight.shape[2]
    half_hidden = up_weight.shape[1]
    slot = lax.axis_index("tensor")
    device = lax.axis_index(("dp", "tensor"))
    scale = HEAD_DIM ** (-0.5)
    gains_all, biases_all, second_all, hidden_all, table_all = (
        lax.all_gather(norm_gains, ("dp", "tensor"), axis=1, tiled=True),
        lax.all_gather(biases, ("dp", "tensor"), axis=1, tiled=True),
        lax.all_gather(second_shift, ("dp", "tensor"), axis=0, tiled=True),
        lax.all_gather(hidden_bias, ("dp", "tensor"), axis=0, tiled=True),
        lax.all_gather(step_table, ("dp", "tensor"), axis=1, tiled=True),
    )
    gains_all = gains_all.astype(jnp.float32)
    biases_all = biases_all.astype(jnp.float32)
    second_all = second_all.astype(jnp.float32)
    hidden_local = lax.dynamic_slice_in_dim(
        hidden_all.astype(jnp.float32), slot * half_hidden, half_hidden, 0
    )
    query_bias = lax.dynamic_slice_in_dim(biases_all[1], slot * half_width, half_width, 0)
    value_bias = lax.dynamic_slice_in_dim(biases_all[2], slot * half_width, half_width, 0)
    step_id = lax.dynamic_slice_in_dim(timesteps, device, 1, 0)
    picker = (step_id[:, None] == jnp.arange(TSTEPS)[None, :]).astype(jnp.bfloat16)
    embed = jnp.dot(picker, table_all, preferred_element_type=jnp.float32)
    start_h = tokens.astype(jnp.float32) + embed
    qkv_full, out_full = fetch_attn(qkv_weight, out_weight)
    up_full, down_full = fetch_mlp(up_weight, down_weight)
    normed = gather_rows(layer_norm(start_h, gains_all[0], biases_all[0]).astype(jnp.bfloat16))
    projected = jnp.einsum("rd,jde->jre", normed, qkv_full, preferred_element_type=jnp.float32)
    queries = (projected[0] + query_bias).astype(jnp.bfloat16)
    keys_all = projected[1].astype(jnp.bfloat16)
    values_all = (projected[2] + value_bias).astype(jnp.bfloat16)
    mixed, log_total = run_attention(queries, keys_all, values_all, scale)
    attn_out = (
        sum_rows(jnp.dot(mixed, out_full, preferred_element_type=jnp.float32)) + biases_all[3]
    )
    middle = start_h + attn_out
    second = gather_rows(layer_norm(middle, gains_all[1], second_all).astype(jnp.bfloat16))
    pre_act = jnp.dot(second, up_full, preferred_element_type=jnp.float32) + hidden_local
    activated = jax.nn.gelu(pre_act).astype(jnp.bfloat16)
    mlp_out = (
        sum_rows(jnp.dot(activated, down_full, preferred_element_type=jnp.float32)) + biases_all[4]
    )
    layer_out = (middle + mlp_out).astype(jnp.bfloat16)
    grad_top = cotangent.astype(jnp.float32)
    up_full, down_full = fetch_mlp(up_weight, down_weight)
    grad_mlp_all = gather_rows(cotangent)
    grad_downw = contract_rows(activated, grad_mlp_all)
    grad_act = contract_cols(grad_mlp_all, down_full)
    unused, gelu_back = jax.vjp(jax.nn.gelu, pre_act)
    grad_pre = gelu_back(grad_act)[0].astype(jnp.bfloat16)
    grad_upw = contract_rows(second, grad_pre)
    grad_hidden_local = jnp.sum(grad_pre.astype(jnp.float32), axis=0)
    grad_second = sum_rows(contract_cols(grad_pre, up_full))
    unused, second_back = jax.vjp(layer_norm, middle, gains_all[1], second_all)
    grad_mid_part, grad_gain_two, grad_shift_two = second_back(grad_second)
    grad_middle = grad_top + grad_mid_part
    grad_up, grad_down = (
        lax.psum_scatter(grad_upw, "dp", scatter_dimension=0, tiled=True),
        lax.psum_scatter(grad_downw, "dp", scatter_dimension=1, tiled=True),
    )
    qkv_full, out_full = fetch_attn(qkv_weight, out_weight)
    grad_attn = grad_middle.astype(jnp.bfloat16)
    grad_attn_all = gather_rows(grad_attn)
    grad_outw = contract_rows(mixed, grad_attn_all)
    grad_mixed = contract_cols(grad_attn_all, out_full).astype(jnp.bfloat16)
    grad_queries, grad_keys, grad_values = attention_back(
        queries, keys_all, values_all, grad_mixed, log_total, scale
    )
    grad_rows = jnp.stack([grad_queries, grad_keys, grad_values]).astype(jnp.bfloat16)
    grad_qkvw = jnp.einsum("rd,jre->jde", normed, grad_rows, preferred_element_type=jnp.float32)
    grad_normed = sum_rows(
        jnp.einsum("jre,jde->rd", grad_rows, qkv_full, preferred_element_type=jnp.float32)
    )
    unused, first_back = jax.vjp(layer_norm, start_h, gains_all[0], biases_all[0])
    grad_start_part, grad_gain_one, grad_shift_one = first_back(grad_normed)
    grad_tokens = grad_middle + grad_start_part
    grad_qkv, grad_out = (
        lax.psum_scatter(grad_qkvw, "dp", scatter_dimension=1, tiled=True),
        lax.psum_scatter(grad_outw, "dp", scatter_dimension=1, tiled=True),
    )
    row_sums = jnp.sum(grad_rows.astype(jnp.float32), axis=1)
    gain_terms = jnp.stack([grad_gain_one, grad_gain_two])
    bias_terms = jnp.stack(
        [
            grad_shift_one,
            place_part(row_sums[0], width, slot * half_width),
            place_part(row_sums[2], width, slot * half_width),
            jnp.sum(grad_attn.astype(jnp.float32), axis=0),
            jnp.sum(grad_top, axis=0),
        ]
    )
    hidden_terms = place_part(
        grad_hidden_local,
        hidden_bias.shape[0] * lax.axis_size(("dp", "tensor")),
        slot * half_hidden,
    )
    seq_grad = jnp.sum(grad_tokens, axis=0, keepdims=True)
    table_terms = lax.dot_general(
        picker.astype(jnp.float32),
        seq_grad,
        (((0,), (0,)), ((), ())),
        precision=HIGH,
        preferred_element_type=jnp.float32,
    )
    grad_gains, grad_biases, grad_shift, grad_hidden, grad_table = (
        lax.psum_scatter(gain_terms, ("dp", "tensor"), scatter_dimension=1, tiled=True),
        lax.psum_scatter(bias_terms, ("dp", "tensor"), scatter_dimension=1, tiled=True),
        lax.psum_scatter(grad_shift_two, ("dp", "tensor"), scatter_dimension=0, tiled=True),
        lax.psum_scatter(hidden_terms, ("dp", "tensor"), scatter_dimension=0, tiled=True),
        lax.psum_scatter(table_terms, ("dp", "tensor"), scatter_dimension=1, tiled=True),
    )
    return (
        layer_out,
        grad_tokens,
        grad_gains,
        grad_biases,
        grad_shift,
        grad_hidden,
        grad_table,
        grad_qkv,
        grad_out,
        grad_up,
        grad_down,
    )


MESH_ID = pl.DeviceIdType.MESH
F32, BF16 = jnp.float32, jnp.bfloat16
NZ, NX, NC, NY = 4, 2, 2, 2
QB = 256
PACK_ROWS = 32
GELU_A, GELU_B = 0.7978845608028654, 0.044715


def nt(left, right):
    return lax.dot_general(left, right, (((1,), (1,)), ((), ())), preferred_element_type=F32)


def nn(left, right):
    return lax.dot_general(left, right, (((1,), (0,)), ((), ())), preferred_element_type=F32)


def tn(left, right):
    return lax.dot_general(left, right, (((0,), (0,)), ((), ())), preferred_element_type=F32)


def position():
    dp = lax.axis_index("dp")
    return (lax.axis_index("tensor"), dp // (NX * NC), lax.rem(dp // NC, NX), lax.rem(dp, NC))


def device_at(y, z, x, c):
    return (z * (NX * NC) + x * NC + c, y)


def greet(pos):
    y, z, x, c = pos
    peers = [device_at(y, lax.rem(z + k, NZ), x, c) for k in range(1, NZ)]
    peers += [device_at(y, z, 1 - x, c), device_at(1 - y, z, x, c), device_at(y, z, x, 1 - c)]
    barrier = pltpu.get_barrier_semaphore()
    for peer in peers:
        pl.semaphore_signal(barrier, inc=1, device_id=peer, device_id_type=MESH_ID)
    pl.semaphore_wait(barrier, len(peers))


def remote(src, dst, send, recv, index, peer):
    return pltpu.make_async_remote_copy(
        src_ref=src,
        dst_ref=dst,
        send_sem=send.at[index],
        recv_sem=recv.at[index],
        device_id=peer,
        device_id_type=MESH_ID,
    )


class Gather:
    def __init__(self, buf, cols, send, recv, pos):
        self.buf, self.cols, self.send, self.recv, self.pos = buf, cols, send, recv, pos

    def view(self, y, z, x, c):
        return self.buf.at[y, z, x, c, :, self.cols]

    def steps(self, step):
        y, z, x, c = self.pos
        lo, hi, both = pl.ds(0, 2), pl.ds(2, 2), pl.ds(0, 2)
        if step == 0:
            return [
                (k - 1, (y, z, x, c), (y, lax.rem(z + NZ - k, NZ), x, c), device_at(y, lax.rem(z + k, NZ), x, c))
                for k in range(1, NZ)
            ]
        x_peer, y_peer = device_at(y, z, 1 - x, c), device_at(1 - y, z, x, c)
        if step == 1:
            return [(3, (y, lo, x, c), (y, lo, 1 - x, c), x_peer), (4, (y, hi, x, c), (1 - y, hi, x, c), y_peer)]
        if step == 2:
            return [
                (5, (y, lo, both, c), (1 - y, lo, both, c), y_peer),
                (6, (both, hi, x, c), (both, hi, 1 - x, c), x_peer),
            ]
        return [(7, (both, pl.ds(0, NZ), both, c), (both, pl.ds(0, NZ), both, 1 - c), device_at(y, z, x, 1 - c))]

    def start(self, step):
        for sem, src, _, peer in self.steps(step):
            remote(self.view(*src), self.view(*src), self.send, self.recv, sem, peer).start()

    def wait(self, step):
        for sem, _, dst, peer in self.steps(step):
            remote(self.view(*dst), self.view(*dst), self.send, self.recv, sem, peer).wait_recv()

    def next(self, step):
        self.wait(step)
        self.start(step + 1)

    def drain(self):
        for step in range(4):
            for sem, src, _, peer in self.steps(step):
                remote(self.view(*src), self.view(*src), self.send, self.recv, sem, peer).wait_send()


def gelu_parts(v):
    square = v * v
    half = 0.5 + 0.5 * jnp.tanh(v * (GELU_A + (GELU_A * GELU_B) * square))
    act = v * half
    slope = half + (2.0 * act) * (1.0 - half) * (GELU_A + (3 * GELU_A * GELU_B) * square)
    return act, slope


def moments(hidden):
    average = jnp.mean(hidden, axis=-1, keepdims=True)
    centered = hidden - average
    variance = jnp.mean(centered * centered, axis=-1, keepdims=True)
    scale = lax.rsqrt(variance + EPS)
    return centered * scale, scale


def norm_back(xhat, scale, grad):
    return (grad - jnp.mean(grad, axis=-1, keepdims=True) - xhat * jnp.mean(grad * xhat, axis=-1, keepdims=True)) * scale


def row_block(index, size):
    return pl.ds(pl.multiple_of(index * size, size), size)


def sum_rows_of(values):
    return jnp.sum(values.astype(F32), axis=0, keepdims=True)


def blocks():
    for z in range(NZ):
        for x in range(NX):
            for c in range(NC):
                for y in range(NY):
                    yield (z * NX + x) * NC * NY + c * NY + y, (y, z, x, c)


def forward_kernel(
    dims,
    tokens,
    steps,
    gains,
    biases,
    shift2,
    hidden,
    table,
    qkv,
    outw,
    upw,
    downw,
    cot,
    q_out,
    k_out,
    v_out,
    mixed_out,
    normed_out,
    middle_out,
    gsec_out,
    small_out,
    lse_out,
    ghid_out,
    csum_out,
    layer_out,
    weights_out,
    grads_out,
    full,
    pack,
    stage,
    normed,
    queries,
    keys_all,
    values_all,
    mixed,
    middle,
    second,
    second_t,
    cot_t,
    result,
    gsec,
    act,
    gpre,
    gtile,
    hid,
    send,
    recv,
    local,
):
    rows, width, per, half, ffh, ft = dims
    pos = position()
    y, z, x, c = pos
    me = device_at(y, z, x, c)[0] * NY + y
    share = width // (NZ * NX * NC * NY)
    n_ff = ffh // ft
    greet(pos)

    names = ["pack", "q", "k", "v", "o"] + [f"m{i}" for i in range(n_ff)]
    col = {"pack": pl.ds(0, 128)}
    for i, name in enumerate(["q", "k", "v", "o"]):
        col[name] = pl.ds(i * half, half)
    for i in range(n_ff):
        col[f"m{i}"] = pl.ds(4 * half + 2 * ft * i, 2 * ft)
    flow = {
        name: Gather(pack if name == "pack" else full, col[name], send.at[i], recv.at[i], pos) for i, name in enumerate(names)
    }

    for i, name in enumerate(["q", "k", "v"]):
        full[y, z, x, c, :, col[name]] = qkv[i]
        if name == "q":
            flow["q"].start(0)
    stage[...] = jnp.zeros_like(stage)
    stage[0:2, 0:share] = gains[...].astype(F32)
    stage[2:7, 0:share] = biases[...].astype(F32)
    stage[7:8, 0:share] = shift2[...].astype(F32)
    picked = (steps[...] == lax.broadcasted_iota(jnp.int32, (steps.shape[0], table.shape[0]), 1)).astype(BF16)
    stage[32 : 32 + steps.shape[0], 0:share] = nn(picked, table[...])
    turned = stage[...].T
    pack[y, z, x, c, 0:share, :] = turned[0:share]
    hshare = hidden.shape[1]
    lane = lax.broadcasted_iota(jnp.int32, (hshare, NC * NY * hshare), 0) + hshare * (c * NY + y)
    place = (lane == lax.broadcasted_iota(jnp.int32, (hshare, NC * NY * hshare), 1)).astype(BF16)
    spread = nn(jnp.broadcast_to(hidden[...], (8, hshare)), place)
    for j in range(spread.shape[1] // 128):
        pack[y, z, x, c, share + j : share + j + 1, :] = spread[0:1, 128 * j : 128 * j + 128]
    flow["pack"].start(0)
    flow["k"].start(0)
    flow["v"].start(0)
    full[y, z, x, c, :, col["o"]] = outw[...].T
    flow["o"].start(0)
    for i in range(n_ff):
        full[y, z, x, c, :, pl.ds(4 * half + 2 * ft * i, ft)] = upw[:, ft * i : ft * i + ft]
        full[y, z, x, c, :, pl.ds(4 * half + 2 * ft * i + ft, ft)] = downw[ft * i : ft * i + ft, :].T
        flow[f"m{i}"].start(0)

    flow["pack"].next(0)
    flow["q"].next(0)
    flow["pack"].next(1)

    def turn_cot(i, total):
        rb = row_block(i, 256)
        block = cot[rb, :]
        cot_t[:, rb] = block.T
        return total + sum_rows_of(block)

    csum_out[...] = lax.fori_loop(0, rows // 256, turn_cot, jnp.zeros((1, width), F32))
    flow["q"].next(1)
    flow["pack"].next(2)
    flow["k"].next(0)
    flow["pack"].wait(3)

    for d, (by, bz, bx, bc) in blocks():
        middle[d * share : d * share + share, 0:128] = pack[by, bz, bx, bc, 0:share, :]
    small_out[...] = middle[0:width, 0:128].T
    for bz in range(NZ):
        for bx in range(NX):
            total = pack[0, bz, bx, 0, share : share + 8, :]
            for bc, by in ((0, 1), (1, 0), (1, 1)):
                total = total + pack[by, bz, bx, bc, share : share + 8, :]
            for j in range(NC * NY * hshare // 128):
                at = (bz * NX + bx) * NC * NY * hshare + 128 * j
                hid[0:1, at : at + 128] = total[j : j + 1]
    embed = small_out[pl.ds(32 + me, 1), :]

    def first_norm(i, _):
        rb = row_block(i, 128)
        xhat, _ = moments(tokens[rb, :].astype(F32) + embed)
        normed[rb, :] = (xhat * small_out[0:1, :] + small_out[2:3, :]).astype(BF16)
        return 0

    flow["q"].next(2)
    lax.fori_loop(0, rows // 128, first_norm, 0)

    def whole(cols):
        return jnp.concatenate([full[by, :, :, :, :, cols].reshape(width, half) for by in range(NY)], axis=1)

    def project(name, bias, factor, out):
        def body(i, _):
            rb = row_block(i, 512)
            value = nn(normed[rb, :], whole(col[name]))
            if bias is not None:
                value = value + small_out[bias : bias + 1, :]
            value = value.astype(BF16)
            out[rb, :] = value * jnp.asarray(factor, BF16) if factor != 1 else value
            return 0

        lax.fori_loop(0, rows // 512, body, 0)

    locals_ = []

    def save(src, dst, index):
        copy = pltpu.make_async_copy(src, dst, local.at[index])
        copy.start()
        locals_.append(copy)

    flow["k"].next(1)
    flow["v"].next(0)
    flow["q"].wait(3)
    project("q", 3, HEAD_DIM**-0.5, queries)
    flow["k"].next(2)
    flow["v"].next(1)
    flow["o"].next(0)
    flow["k"].wait(3)
    project("k", None, 1, keys_all)
    flow["v"].next(2)
    flow["o"].next(1)
    flow["m0"].next(0)
    flow["v"].wait(3)
    project("v", 4, 1, values_all)
    save(normed, normed_out, 0)
    save(queries, q_out, 1)
    save(keys_all, k_out, 2)
    save(values_all, v_out, 3)

    def attend(p, _):
        @pl.when(p == 0)
        def _():
            flow["o"].next(2)
            flow["m0"].next(1)

        @pl.when(p == 1)
        def _():
            flow["m1"].next(0)

        @pl.when(p == 3)
        def _():
            flow["m0"].next(2)
            flow["m2"].next(0)

        @pl.when(p == 4)
        def _():
            flow["m1"].next(1)

        cols = pl.ds(pl.multiple_of(p * 128, 128), 128)
        low = lax.broadcasted_iota(jnp.int32, (QB, 128), 1) < HEAD_DIM
        for i in range(rows // QB):
            n = (i + 1) * QB
            rb = slice(i * QB, n)
            key, value, query = keys_all[0:n, cols], values_all[0:n, cols], queries[rb, cols]
            outs = []
            for h in range(2):
                scores = nt(key, jnp.where(low == (h == 0), query, jnp.zeros_like(query)))
                top = jnp.max(scores, axis=0, keepdims=True)
                expo = jnp.exp(scores - top)
                total = jnp.sum(expo, axis=0, keepdims=True)
                lse_out[pl.ds(2 * p + h, 1), rb] = top + jnp.log(total)
                outs.append(tn((expo * (1.0 / total)).astype(BF16), value))
            mixed[rb, cols] = jnp.where(low, outs[0], outs[1]).astype(BF16)
        return 0

    lax.fori_loop(0, width // 128, attend, 0)
    flow["o"].wait(3)
    save(mixed, mixed_out, 4)
    for by in range(NY):
        save(full.at[by, :, :, :, :, pl.ds(0, 4 * half)], weights_out.at[by], 5 + by)

    def second_norm(i, _):
        rb = row_block(i, 256)
        start_h = tokens[rb, :].astype(F32) + embed
        value = start_h + (nt(mixed[rb, :], whole(col["o"])) + small_out[5:6, :])
        middle[rb, :] = value
        xhat, _ = moments(value)
        block = (xhat * small_out[1:2, :] + small_out[7:8, :]).astype(BF16)
        second[rb, :] = block
        second_t[:, rb] = block.T
        return 0

    lax.fori_loop(0, rows // 256, second_norm, 0)
    save(middle, middle_out, 7)
    flow["m1"].next(2)
    flow["m0"].wait(3)

    def tile_copy(t, slot):
        ty, tm = lax.rem(t, NY), t // NY
        return pltpu.make_async_copy(
            gtile.at[slot], grads_out.at[ty, :, pl.ds(pl.multiple_of(tm * 2 * ft, 128), 2 * ft)], local.at[8 + slot]
        )

    def tile(t, _):
        ty, tm = lax.rem(t, NY), t // NY
        slot = lax.rem(t, 2)

        @pl.when(t == 1)
        def _():
            flow["m2"].next(1)

        @pl.when(t == 2)
        def _():
            flow["m1"].wait(3)

        @pl.when(t == 3)
        def _():
            flow["m2"].next(2)

        @pl.when(t == 4)
        def _():
            flow["m2"].wait(3)

        up_at = pl.ds(pl.multiple_of(4 * half + tm * 2 * ft, 128), ft)
        down_at = pl.ds(pl.multiple_of(4 * half + tm * 2 * ft + ft, 128), ft)
        hid_at = pl.ds(pl.multiple_of(ty * ffh + tm * ft, 128), ft)

        def up():
            return full[ty, :, :, :, :, up_at].reshape(width, ft)

        def down():
            return full[ty, :, :, :, :, down_at].reshape(width, ft)

        pre = nn(second[...], up()) + hid[:, hid_at]
        gact = nn(cot[...], down())
        value, slope = gelu_parts(pre)
        act[...] = value.astype(BF16)
        grad = (gact * slope).astype(BF16)
        gpre[...] = grad
        ghid_out[:, hid_at] = sum_rows_of(grad)
        more = nt(act[...], down())
        gmore = nt(gpre[...], up())

        @pl.when(t == 0)
        def _():
            result[...] = more
            gsec[...] = gmore

        @pl.when(t > 0)
        def _():
            result[...] += more
            gsec[...] += gmore

        @pl.when(t >= 2)
        def _():
            tile_copy(t - 2, slot).wait()

        def weight_grad(i, _):
            rb = row_block(i, 256)
            gtile[slot, rb, 0:ft] = nn(second_t[rb, :], gpre[...]).astype(BF16)
            gtile[slot, rb, ft : 2 * ft] = nn(cot_t[rb, :], act[...]).astype(BF16)
            return 0

        lax.fori_loop(0, width // 256, weight_grad, 0)
        tile_copy(t, slot).start()
        return 0

    tiles = NY * n_ff
    lax.fori_loop(0, tiles, tile, 0)
    save(gsec, gsec_out, 10)

    def finish(i, _):
        rb = row_block(i, 256)
        layer_out[rb, :] = (middle[rb, :] + (result[rb, :] + small_out[6:7, :])).astype(BF16)
        return 0

    lax.fori_loop(0, rows // 256, finish, 0)
    tile_copy(tiles - 2, 0).wait()
    tile_copy(tiles - 1, 1).wait()
    for copy in locals_:
        copy.wait()
    for name in names:
        flow[name].drain()


class Scatter:
    def __init__(self, source, own, bufs, send, recv, pos, loaded):
        self.source, self.own, self.bufs = source, own, bufs
        self.send, self.recv, self.pos, self.loaded = send, recv, pos, loaded

    def copies(self, step):
        y, z, x, c = self.pos
        first, second_x, second_y, third_y, third_x, last = self.bufs
        own = self.own
        lo, hi, both = pl.ds(0, 2), pl.ds(2, 2), pl.ds(0, 2)
        x_peer, y_peer = device_at(y, z, 1 - x, c), device_at(1 - y, z, x, c)
        if step == 0:
            return [(0, self.source.at[both, pl.ds(0, NZ), both, 1 - c], first, device_at(y, z, x, 1 - c))]
        if step == 1:
            return [(1, own.at[both, lo, 1 - x], second_x, x_peer), (2, own.at[1 - y, hi, both], second_y, y_peer)]
        if step == 2:
            return [(3, own.at[1 - y, lo, x], third_y, y_peer), (4, own.at[y, hi, 1 - x], third_x, x_peer)]
        return [
            (4 + k, own.at[y, lax.rem(z + k, NZ), x], last.at[k - 1], device_at(y, lax.rem(z + k, NZ), x, c))
            for k in range(1, NZ)
        ]

    def start(self, step):
        for sem, src, dst, peer in self.copies(step):
            remote(src, dst, self.send, self.recv, sem, peer).start()

    def wait(self, step):
        for sem, src, dst, peer in self.copies(step):
            remote(src, dst, self.send, self.recv, sem, peer).wait_recv()

    def add(self, step):
        y, z, x, c = self.pos
        own, source = self.own, self.source
        first, second_x, second_y, third_y, third_x, last = self.bufs
        kind = own.dtype

        def plus(left, right):
            return (left.astype(F32) + right.astype(F32)).astype(kind)

        def each(count, body):
            def run(i, _):
                body(i)
                return 0

            lax.fori_loop(0, count, run, 0)

        if step == 0:

            def body(i):
                iy, iz, ix = i // (NZ * NX), lax.rem(i // NX, NZ), lax.rem(i, NX)
                mine = own[iy, iz, ix] if self.loaded else source[iy, iz, ix, c]
                own[iy, iz, ix] = plus(mine, first[iy, iz, ix])

            each(NY * NZ * NX, body)
        elif step == 1:

            def body(i):
                a, b = i // 2, lax.rem(i, 2)
                own[a, b, x] = plus(own[a, b, x], second_x[a, b])
                own[y, 2 + a, b] = plus(own[y, 2 + a, b], second_y[a, b])

            each(4, body)
        else:

            def body(i):
                own[y, i, x] = plus(own[y, i, x], third_y[i])
                own[y, 2 + i, x] = plus(own[y, 2 + i, x], third_x[i])

            each(2, body)

    def next(self, step):
        self.wait(step)
        self.add(step)
        self.start(step + 1)

    def final(self):
        y, z, x, c = self.pos
        last = self.bufs[5]
        self.wait(3)
        total = self.own[y, z, x].astype(F32)
        for k in range(NZ - 1):
            total = total + last[k].astype(F32)
        return total

    def drain(self):
        for step in range(4):
            for sem, src, dst, peer in self.copies(step):
                remote(src, dst, self.send, self.recv, sem, peer).wait_send()


def scatter_scratch(per, width, kind):
    return [
        pltpu.VMEM((NY, NZ, NX, per, width), kind),
        pltpu.VMEM((NY, NZ, NX, per, width), kind),
        pltpu.VMEM((2, 2, per, width), kind),
        pltpu.VMEM((2, 2, per, width), kind),
        pltpu.VMEM((2, per, width), kind),
        pltpu.VMEM((2, per, width), kind),
        pltpu.VMEM((NZ - 1, per, width), kind),
    ]


def backward_kernel(
    dims,
    tokens,
    cot,
    small,
    lse,
    ghid,
    csum,
    q_in,
    k_in,
    v_in,
    mixed_in,
    normed_in,
    middle_in,
    gsec_in,
    weights_in,
    grads_in,
    gup_out,
    gdown_out,
    gout_out,
    gqkv_out,
    gpack_out,
    gtok_out,
    queries,
    keys_all,
    values_all,
    mixed,
    normed,
    normed_t,
    middle,
    gsec,
    weights,
    gattn,
    gattn_t,
    gval,
    acc_k,
    acc_v,
    sums,
    gpack,
    gout,
    gqkv,
    *rest,
):
    rows, width, per, half, ffh, ft = dims
    pos = position()
    y, z, x, c = pos
    me = device_at(y, z, x, c)[0] * NY + y
    share = width // (NZ * NX * NC * NY)
    n_ff = ffh // ft
    n_groups = half // 128
    names = [f"m{i}" for i in range(n_ff)] + ["o"] + [f"q{i}" for i in range(n_groups)] + ["pack"]
    send, recv, local = rest[-3:]
    flow = {}
    for i, name in enumerate(names):
        own, first, *others = rest[7 * i : 7 * i + 7]
        if name[0] == "m":
            source = grads_in.at[:, :, :, :, :, pl.ds(2 * ft * i, 2 * ft)]
        else:
            source = {"o": gout, "p": gpack}.get(name[0], None)
            if source is None:
                source = gqkv.at[int(name[1:])]
        flow[name] = Scatter(source, own, [first] + others, send.at[i], recv.at[i], pos, name[0] == "m")

    copies = {}

    def load(name, src, dst, index):
        copies[name] = pltpu.make_async_copy(src, dst, local.at[index])
        copies[name].start()

    load("middle", middle_in, middle, 0)
    load("gsec", gsec_in, gsec, 1)
    for i in range(n_ff):
        name = f"m{i}"
        load(name, flow[name].source.at[:, :, :, c], flow[name].own, 2 + i)
    at = 2 + n_ff
    load("w", weights_in, weights, at)
    load("mixed", mixed_in, mixed, at + 1)
    load("normed", normed_in, normed, at + 2)
    load("q", q_in, queries, at + 3)
    load("k", k_in, keys_all, at + 4)
    load("v", v_in, values_all, at + 5)
    greet(pos)
    for i in range(n_ff):
        flow[f"m{i}"].start(0)
    copies["middle"].wait()
    copies["gsec"].wait()

    def second_back(i, totals):
        rb = row_block(i, 128)
        xhat, scale = moments(middle[rb, :])
        grad = gsec[rb, :]
        result = cot[rb, :].astype(F32) + norm_back(xhat, scale, grad * small[1:2, :])
        gsec[rb, :] = result
        low = result.astype(BF16)
        gattn[rb, :] = low
        gattn_t[:, rb] = low.T
        return (
            totals[0] + sum_rows_of(grad * xhat),
            totals[1] + sum_rows_of(grad),
            totals[2] + sum_rows_of(low),
        )

    zero = jnp.zeros((1, width), F32)
    ggain2, gshift2, gattn_sum = lax.fori_loop(0, rows // 128, second_back, (zero, zero, zero))
    sums[...] = jnp.zeros_like(sums)
    sums[1:2, :] = ggain2
    sums[5:6, :] = gattn_sum
    sums[6:7, :] = csum[...]
    sums[7:8, :] = gshift2
    copies["m0"].wait()
    flow["m0"].next(0)
    copies["w"].wait()
    copies["mixed"].wait()

    def whole(index):
        cols = pl.ds(index * half, half)
        return jnp.concatenate([weights[by, :, cols] for by in range(NY)], axis=1)

    for by in range(NY):
        def out_grad(i, _):
            rb = row_block(i, 384)
            part = nn(gattn_t[rb, :], mixed[:, by * half : by * half + half]).astype(BF16)
            gout[by, pl.ds(i * 2, 2)] = part.reshape(2, NX, NC, per, half)
            return 0

        lax.fori_loop(0, width // 384, out_grad, 0)
    flow["o"].start(0)

    def mixed_grad(i, _):
        rb = row_block(i, 512)
        mixed[rb, :] = nn(gattn[rb, :], whole(3)).astype(BF16)
        return 0

    lax.fori_loop(0, rows // 512, mixed_grad, 0)
    copies["m1"].wait()
    flow["m1"].next(0)
    copies["normed"].wait()

    def turn_normed(i, _):
        rb = row_block(i, 256)
        normed_t[:, rb] = normed[rb, :].T
        return 0

    lax.fori_loop(0, rows // 256, turn_normed, 0)
    copies["q"].wait()
    copies["k"].wait()
    copies["v"].wait()
    gq, gk, gv = gattn, normed, gval

    def attend_back(s, _):
        group, by = s // NY, lax.rem(s, NY)
        p = by * n_groups + group

        @pl.when(s == 1)
        def _():
            copies["m2"].wait()
            flow["m2"].next(0)
            flow["m0"].next(1)

        @pl.when(s == 2)
        def _():
            flow["o"].next(0)

        @pl.when(s == 3)
        def _():
            flow["m1"].next(1)
            flow["m0"].next(2)
            flow["q0"].next(0)

        @pl.when(s == 4)
        def _():
            flow["m2"].next(1)
            flow["o"].next(1)

        @pl.when(s == 5)
        def _():
            flow["q1"].next(0)
            flow["m1"].next(2)
            flow["q0"].next(1)

        cols = pl.ds(pl.multiple_of(p * 128, 128), 128)
        low = lax.broadcasted_iota(jnp.int32, (QB, 128), 1) < HEAD_DIM
        for i in range(rows // QB):
            n = (i + 1) * QB
            rb = slice(i * QB, n)
            key, value = keys_all[0:n, cols], values_all[0:n, cols]
            query, grad = queries[rb, cols], mixed[rb, cols]
            parts, dv, dk = [], None, None
            for h in range(2):
                sel = low == (h == 0)
                query_h = jnp.where(sel, query, jnp.zeros_like(query))
                grad_h = jnp.where(sel, grad, jnp.zeros_like(grad))
                probs = jnp.exp(nt(key, query_h) - lse[pl.ds(2 * p + h, 1), rb])
                gprobs = nt(value, grad_h)
                inner = jnp.sum(probs * gprobs, axis=0, keepdims=True)
                gscores = (probs * (gprobs - inner)).astype(BF16)
                pv, pk = nn(probs.astype(BF16), grad_h), nn(gscores, query_h)
                dv = pv if dv is None else dv + pv
                dk = pk if dk is None else dk + pk
                parts.append(tn(gscores, key))
            last = n - QB
            if last:
                acc_k[0:last] += dk[:last]
                acc_v[0:last] += dv[:last]
            acc_k[last:n] = dk[last:]
            acc_v[last:n] = dv[last:]
            gq[rb, cols] = (jnp.where(low, parts[0], parts[1]) * HEAD_DIM**-0.5).astype(BF16)
        gk[:, cols] = acc_k[...].astype(BF16)
        gv[:, cols] = acc_v[...].astype(BF16)

        @pl.when(by == NY - 1)
        def _():
            for piece, source in enumerate((gq, gk, gv)):
                pick = jnp.concatenate(
                    [source[:, pl.ds(pl.multiple_of((b * n_groups + group) * 128, 128), 128)] for b in range(NY)], axis=1
                )
                part = nn(normed_t[...], pick).astype(BF16)
                for b in range(NY):
                    gqkv[group, b, :, :, :, :, piece * 128 : piece * 128 + 128] = part[:, b * 128 : b * 128 + 128].reshape(
                        NZ, NX, NC, per, 128
                    )
            for g in range(n_groups):
                @pl.when(group == g)
                def _():
                    flow[f"q{g}"].start(0)

        return 0

    lax.fori_loop(0, NY * n_groups, attend_back, 0)
    flow["q0"].next(2)
    flow["m2"].next(2)
    flow["o"].next(2)
    flow["q1"].next(1)
    flow["q2"].next(0)
    embed = small[pl.ds(32 + me, 1), :]

    def first_back(i, totals):
        rb = row_block(i, 256)
        xhat, scale = moments(tokens[rb, :].astype(F32) + embed)
        q_rows, k_rows, v_rows = gq[rb, :], gk[rb, :], gv[rb, :]
        grad = nt(q_rows, whole(0)) + nt(k_rows, whole(1)) + nt(v_rows, whole(2))
        result = gsec[rb, :] + norm_back(xhat, scale, grad * small[0:1, :])
        middle[rb, :] = result

        @pl.when(i == 1)
        def _():
            flow["q1"].next(2)
            flow["q2"].next(1)

        return (
            totals[0] + sum_rows_of(grad * xhat),
            totals[1] + sum_rows_of(grad),
            totals[2] + sum_rows_of(q_rows),
            totals[3] + sum_rows_of(v_rows),
            totals[4] + sum_rows_of(result),
        )

    ggain1, gshift1, q_sum, v_sum, seq_sum = lax.fori_loop(0, rows // 256, first_back, (zero,) * 5)
    sums[0:1, :] = ggain1
    sums[2:3, :] = gshift1
    sums[3:4, :] = q_sum
    sums[4:5, :] = v_sum
    sums[pl.ds(32 + me, 1), :] = seq_sum
    gtok = pltpu.make_async_copy(middle, gtok_out, local.at[at + 6])
    gtok.start()
    turned = sums[...].T
    hgroup = ghid.shape[1] // (NZ * NX)
    for d, (by, bz, bx, bc) in blocks():
        gpack[by, bz, bx, bc, 0:share, :] = turned[d * share : d * share + share]
        for j in range(hgroup // 128):
            start = (bz * NX + bx) * hgroup + 128 * j
            gpack[by, bz, bx, bc, share + j : share + j + 1, :] = ghid[:, start : start + 128]
        gpack[by, bz, bx, bc, share + hgroup // 128 :, :] = jnp.zeros((PACK_ROWS - share - hgroup // 128, 128), F32)
    flow["pack"].start(0)
    for i in range(n_ff):
        total = flow[f"m{i}"].final()
        gup_out[:, ft * i : ft * i + ft] = total[:, 0:ft]
        gdown_out[:, ft * i : ft * i + ft] = total[:, ft:]
    flow["pack"].next(0)
    flow["q2"].next(2)
    flow["pack"].next(1)
    gout_out[...] = flow["o"].final()
    for g in range(n_groups - 1):
        total = flow[f"q{g}"].final()
        for piece in range(3):
            gqkv_out[piece, :, 128 * g : 128 * g + 128] = total[:, 128 * piece : 128 * piece + 128]
    flow["pack"].next(2)
    g = n_groups - 1
    total = flow[f"q{g}"].final()
    for piece in range(3):
        gqkv_out[piece, :, 128 * g : 128 * g + 128] = total[:, 128 * piece : 128 * piece + 128]
    gpack_out[...] = flow["pack"].final()
    gtok.wait()
    for name in names:
        flow[name].drain()


def fast_shards(
    tokens,
    timesteps,
    norm_gains,
    biases,
    second_shift,
    hidden_bias,
    step_table,
    qkv_weight,
    out_weight,
    up_weight,
    down_weight,
    cotangent,
):
    rows, width = tokens.shape
    _, per, half = qkv_weight.shape
    ffh = up_weight.shape[1]
    ft = 512
    dims = (rows, width, per, half, ffh, ft)
    n_ff, n_groups = ffh // ft, half // 128
    total = 4 * half + 2 * ffh
    vmem, anywhere = pl.BlockSpec(memory_space=pltpu.VMEM), pl.BlockSpec(memory_space=pl.ANY)
    shape = jax.ShapeDtypeStruct
    low, wide = shape((rows, width), BF16), shape((rows, width), F32)
    vm = pltpu.VMEM
    hshare = hidden_bias.shape[0]
    n_chunks = 5 + n_ff
    outs = pl.pallas_call(
        functools.partial(forward_kernel, dims),
        in_specs=[vmem] * 12,
        out_specs=[anywhere] * 7 + [vmem] * 5 + [anywhere] * 2,
        out_shape=[
            low,
            low,
            low,
            low,
            low,
            wide,
            wide,
            shape((128, width), F32),
            shape((16, rows), F32),
            shape((1, NY * ffh), F32),
            shape((1, width), F32),
            low,
            shape((NY, NZ, NX, NC, per, 4 * half), BF16),
            shape((NY, width, 2 * ffh), BF16),
        ],
        scratch_shapes=[
            vm((NY, NZ, NX, NC, per, total), BF16),
            vm((NY, NZ, NX, NC, PACK_ROWS, 128), F32),
            vm((128, 128), F32),
            vm((rows, width), BF16),
            vm((rows, width), BF16),
            vm((rows, width), BF16),
            vm((rows, width), BF16),
            vm((rows, width), BF16),
            vm((rows, width), F32),
            vm((rows, width), BF16),
            vm((width, rows), BF16),
            vm((width, rows), BF16),
            vm((rows, width), F32),
            vm((rows, width), F32),
            vm((rows, ft), BF16),
            vm((rows, ft), BF16),
            vm((2, width, 2 * ft), BF16),
            vm((1, NY * ffh), F32),
            pltpu.SemaphoreType.DMA((n_chunks, 8)),
            pltpu.SemaphoreType.DMA((n_chunks, 8)),
            pltpu.SemaphoreType.DMA((11,)),
        ],
        compiler_params=pltpu.CompilerParams(collective_id=0, has_side_effects=True, vmem_limit_bytes=VMEM_LIMIT),
        name="layer_forward",
    )(
        tokens,
        timesteps.reshape(-1, 1),
        norm_gains,
        biases,
        second_shift.reshape(1, -1),
        hidden_bias.reshape(1, -1),
        step_table,
        qkv_weight,
        out_weight,
        up_weight,
        down_weight,
        cotangent,
    )
    q, k, v, mixed, normed, middle, gsec, small, lse, ghid, csum, layer_out, weights, grads = outs
    chunks = [2 * ft] * n_ff + [half] * (1 + n_groups)
    scratch = []
    for cols in chunks:
        scratch += scatter_scratch(per, cols, BF16)
    scratch += scatter_scratch(PACK_ROWS, 128, F32)
    n_local = 2 + n_ff + 7
    gup, gdown, gout, gqkv, gpack, gtok = pl.pallas_call(
        functools.partial(backward_kernel, dims),
        in_specs=[vmem] * 6 + [anywhere] * 9,
        out_specs=[vmem] * 5 + [anywhere],
        out_shape=[
            shape((per, ffh), F32),
            shape((per, ffh), F32),
            shape((per, half), F32),
            shape((3, per, half), F32),
            shape((PACK_ROWS, 128), F32),
            wide,
        ],
        scratch_shapes=[
            vm((rows, width), BF16),
            vm((rows, width), BF16),
            vm((rows, width), BF16),
            vm((rows, width), BF16),
            vm((rows, width), BF16),
            vm((width, rows), BF16),
            vm((rows, width), F32),
            vm((rows, width), F32),
            vm((NY, width, 4 * half), BF16),
            vm((rows, width), BF16),
            vm((width, rows), BF16),
            vm((rows, width), BF16),
            vm((rows, 128), F32),
            vm((rows, 128), F32),
            vm((128, width), F32),
            vm((NY, NZ, NX, NC, PACK_ROWS, 128), F32),
            vm((NY, NZ, NX, NC, per, half), BF16),
            vm((n_groups, NY, NZ, NX, NC, per, 3 * 128), BF16),
            *scratch,
            pltpu.SemaphoreType.DMA((len(chunks) + 1, 8)),
            pltpu.SemaphoreType.DMA((len(chunks) + 1, 8)),
            pltpu.SemaphoreType.DMA((n_local,)),
        ],
        compiler_params=pltpu.CompilerParams(collective_id=1, has_side_effects=True, vmem_limit_bytes=VMEM_LIMIT),
        name="layer_backward",
    )(
        tokens,
        cotangent,
        small,
        lse,
        ghid,
        csum,
        q,
        k,
        v,
        mixed,
        normed,
        middle,
        gsec,
        weights.reshape(NY, width, 4 * half),
        grads.reshape(NY, NZ, NX, NC, per, 2 * ffh),
    )
    share = norm_gains.shape[1]
    rows_small = gpack[:share, :8].T
    hid_rows = gpack[share : share + NC * NY * hshare // 128].reshape(-1)
    slot = lax.rem(lax.axis_index("dp"), NC) * NY + lax.axis_index("tensor")
    grad_hidden = lax.dynamic_slice_in_dim(hid_rows, slot * hshare, hshare, 0)
    n_seq = timesteps.shape[0]
    picker = (jnp.arange(step_table.shape[0])[:, None] == timesteps[None, :]).astype(F32)
    grad_table = lax.dot_general(
        picker, gpack[:share, 32 : 32 + n_seq], (((1,), (1,)), ((), ())), precision=HIGH, preferred_element_type=F32
    )
    return (
        layer_out,
        gtok,
        rows_small[0:2],
        rows_small[2:7],
        rows_small[7],
        grad_hidden,
        grad_table,
        gqkv,
        gout.T,
        gup,
        gdown.T,
    )


def solution(mesh):
    in_specs = (
        P(("dp", "tensor"), None),
        P(),
        P(None, ("dp", "tensor")),
        P(None, ("dp", "tensor")),
        P(("dp", "tensor")),
        P(("dp", "tensor")),
        P(None, ("dp", "tensor")),
        P(None, "dp", "tensor"),
        P("tensor", "dp"),
        P("dp", "tensor"),
        P("tensor", "dp"),
        P(("dp", "tensor"), None),
    )
    out_specs = (
        P(("dp", "tensor"), None),
        P(("dp", "tensor"), None),
        P(None, ("dp", "tensor")),
        P(None, ("dp", "tensor")),
        P(("dp", "tensor")),
        P(("dp", "tensor")),
        P(None, ("dp", "tensor")),
        P(None, "dp", "tensor"),
        P("tensor", "dp"),
        P("dp", "tensor"),
        P("tensor", "dp"),
    )
    fast = mesh.shape["dp"] == NZ * NX * NC and mesh.shape["tensor"] == NY
    return jax.shard_map(fast_shards if fast else shards, mesh=mesh, in_specs=in_specs, out_specs=out_specs, check_vma=False)
```

```python
import functools

import jax
import jax.numpy as jnp
from jax import lax
from jax.experimental import pallas as pl
from jax.experimental.pallas import tpu as pltpu
from jax.sharding import PartitionSpec as P

HEAD_DIM = 64
TSTEPS = 1000
LEN = 1024
BLOCK = 256
QBLK = 512


EPS = 1e-05
NEGATIVE = -1e30
HIGH = lax.Precision.HIGHEST
VMEM_LIMIT = 62 * 1024 * 1024


def layer_norm(hidden, gain, shift):
    average = jnp.mean(hidden, axis=-1, keepdims=True)
    centered = hidden - average
    variance = jnp.mean(centered * centered, axis=-1, keepdims=True)
    return centered * lax.rsqrt(variance + EPS) * gain + shift


def gather_rows(values):
    return lax.all_gather(values, "tensor", axis=0, tiled=True)


def sum_rows(values):
    return lax.psum_scatter(
        values.astype(jnp.bfloat16), "tensor", scatter_dimension=0, tiled=True
    ).astype(jnp.float32)


def fetch_attn(qkv_weight, out_weight):
    return (
        lax.all_gather(qkv_weight, "dp", axis=1, tiled=True),
        lax.all_gather(out_weight, "dp", axis=1, tiled=True),
    )


def fetch_mlp(up_weight, down_weight):
    return (
        lax.all_gather(up_weight, "dp", axis=0, tiled=True),
        lax.all_gather(down_weight, "dp", axis=1, tiled=True),
    )


def place_part(part, whole_len, offset):
    return lax.dynamic_update_slice_in_dim(jnp.zeros((whole_len,), jnp.float32), part, offset, 0)


def contract_rows(left, right):
    return lax.dot_general(
        left, right, (((0,), (0,)), ((), ())), preferred_element_type=jnp.float32
    )


def contract_cols(left, right):
    return lax.dot_general(
        left, right, (((1,), (1,)), ((), ())), preferred_element_type=jnp.float32
    )


def block_mask(start):
    query_pos = start + jnp.arange(QBLK)
    key_pos = jnp.arange(LEN)
    return query_pos[:, None] // BLOCK >= key_pos[None, :] // BLOCK


def split_heads(values):
    return values.reshape(values.shape[0], values.shape[1] // HEAD_DIM, HEAD_DIM)


def masked_scores(query_heads, key_heads, start, scale):
    scores = (
        jnp.einsum("qhd,khd->hqk", query_heads, key_heads, preferred_element_type=jnp.float32)
        * scale
    )
    return jnp.where(block_mask(start)[None], scores, NEGATIVE)


def block_slices(queries, keys_all, values_all, index):
    per_seq = LEN // QBLK
    seq_start = index // per_seq * LEN
    start = index % per_seq * QBLK
    query_blk = lax.dynamic_slice_in_dim(queries, seq_start + start, QBLK, 0)
    key_seq = lax.dynamic_slice_in_dim(keys_all, seq_start, LEN, 0)
    value_seq = lax.dynamic_slice_in_dim(values_all, seq_start, LEN, 0)
    return (seq_start, start, query_blk, key_seq, value_seq)


def run_attention(queries, keys_all, values_all, scale):
    total_rows = queries.shape[0]

    def run_advance(carry, index):
        seq_start, start, query_blk, key_seq, value_seq = block_slices(
            queries, keys_all, values_all, index
        )
        scores = masked_scores(split_heads(query_blk), split_heads(key_seq), start, scale)
        largest = jnp.max(scores, axis=-1, keepdims=True)
        expo = jnp.exp(scores - largest)
        totals = jnp.sum(expo, axis=-1, keepdims=True)
        chances = (expo / totals).astype(jnp.bfloat16)
        log_total = (largest + jnp.log(totals))[..., 0]
        mixed = jnp.einsum(
            "hqk,khd->qhd", chances, split_heads(value_seq), preferred_element_type=jnp.float32
        )
        return (carry, (mixed.reshape(QBLK, -1).astype(jnp.bfloat16), log_total))

    unused, (mixed, log_total) = lax.scan(run_advance, 0, jnp.arange(total_rows // QBLK))
    return (mixed.reshape(total_rows, -1), log_total)


def attention_back(queries, keys_all, values_all, grad_mixed, log_total, scale):
    total_rows = queries.shape[0]
    zeros = jnp.zeros(queries.shape, jnp.float32)

    def attention_advance(carry, inputs):
        grad_keys, grad_values = carry
        index, log_blk = inputs
        seq_start, start, query_blk, key_seq, value_seq = block_slices(
            queries, keys_all, values_all, index
        )
        grad_blk = lax.dynamic_slice_in_dim(grad_mixed, seq_start + start, QBLK, 0)
        query_heads = split_heads(query_blk)
        key_heads = split_heads(key_seq)
        grad_heads = split_heads(grad_blk)
        scores = masked_scores(query_heads, key_heads, start, scale)
        chances = jnp.exp(scores - log_blk[..., None])
        grad_probs = jnp.einsum(
            "qhd,khd->hqk", grad_heads, split_heads(value_seq), preferred_element_type=jnp.float32
        )
        inner = jnp.sum(chances * grad_probs, axis=-1, keepdims=True)
        grad_scores = (chances * (grad_probs - inner)).astype(jnp.bfloat16)
        grad_query = (
            jnp.einsum("hqk,khd->qhd", grad_scores, key_heads, preferred_element_type=jnp.float32)
            * scale
        )
        grad_key = (
            jnp.einsum("hqk,qhd->khd", grad_scores, query_heads, preferred_element_type=jnp.float32)
            * scale
        )
        grad_value = jnp.einsum(
            "hqk,qhd->khd",
            chances.astype(jnp.bfloat16),
            grad_heads,
            preferred_element_type=jnp.float32,
        )
        old_keys = lax.dynamic_slice_in_dim(grad_keys, seq_start, LEN, 0)
        old_values = lax.dynamic_slice_in_dim(grad_values, seq_start, LEN, 0)
        grad_keys = lax.dynamic_update_slice_in_dim(
            grad_keys, old_keys + grad_key.reshape(LEN, -1), seq_start, 0
        )
        grad_values = lax.dynamic_update_slice_in_dim(
            grad_values, old_values + grad_value.reshape(LEN, -1), seq_start, 0
        )
        return ((grad_keys, grad_values), grad_query.reshape(QBLK, -1))

    (grad_keys, grad_values), grad_queries = lax.scan(
        attention_advance, (zeros, zeros), (jnp.arange(total_rows // QBLK), log_total)
    )
    return (grad_queries.reshape(total_rows, -1), grad_keys, grad_values)


def shards(
    tokens,
    timesteps,
    norm_gains,
    biases,
    second_shift,
    hidden_bias,
    step_table,
    qkv_weight,
    out_weight,
    up_weight,
    down_weight,
    cotangent,
):
    width = tokens.shape[1]
    half_width = qkv_weight.shape[2]
    half_hidden = up_weight.shape[1]
    slot = lax.axis_index("tensor")
    device = lax.axis_index(("dp", "tensor"))
    scale = HEAD_DIM ** (-0.5)
    gains_all, biases_all, second_all, hidden_all, table_all = (
        lax.all_gather(norm_gains, ("dp", "tensor"), axis=1, tiled=True),
        lax.all_gather(biases, ("dp", "tensor"), axis=1, tiled=True),
        lax.all_gather(second_shift, ("dp", "tensor"), axis=0, tiled=True),
        lax.all_gather(hidden_bias, ("dp", "tensor"), axis=0, tiled=True),
        lax.all_gather(step_table, ("dp", "tensor"), axis=1, tiled=True),
    )
    gains_all = gains_all.astype(jnp.float32)
    biases_all = biases_all.astype(jnp.float32)
    second_all = second_all.astype(jnp.float32)
    hidden_local = lax.dynamic_slice_in_dim(
        hidden_all.astype(jnp.float32), slot * half_hidden, half_hidden, 0
    )
    query_bias = lax.dynamic_slice_in_dim(biases_all[1], slot * half_width, half_width, 0)
    value_bias = lax.dynamic_slice_in_dim(biases_all[2], slot * half_width, half_width, 0)
    step_id = lax.dynamic_slice_in_dim(timesteps, device, 1, 0)
    picker = (step_id[:, None] == jnp.arange(TSTEPS)[None, :]).astype(jnp.bfloat16)
    embed = jnp.dot(picker, table_all, preferred_element_type=jnp.float32)
    start_h = tokens.astype(jnp.float32) + embed
    qkv_full, out_full = fetch_attn(qkv_weight, out_weight)
    up_full, down_full = fetch_mlp(up_weight, down_weight)
    normed = gather_rows(layer_norm(start_h, gains_all[0], biases_all[0]).astype(jnp.bfloat16))
    projected = jnp.einsum("rd,jde->jre", normed, qkv_full, preferred_element_type=jnp.float32)
    queries = (projected[0] + query_bias).astype(jnp.bfloat16)
    keys_all = projected[1].astype(jnp.bfloat16)
    values_all = (projected[2] + value_bias).astype(jnp.bfloat16)
    mixed, log_total = run_attention(queries, keys_all, values_all, scale)
    attn_out = (
        sum_rows(jnp.dot(mixed, out_full, preferred_element_type=jnp.float32)) + biases_all[3]
    )
    middle = start_h + attn_out
    second = gather_rows(layer_norm(middle, gains_all[1], second_all).astype(jnp.bfloat16))
    pre_act = jnp.dot(second, up_full, preferred_element_type=jnp.float32) + hidden_local
    activated = jax.nn.gelu(pre_act).astype(jnp.bfloat16)
    mlp_out = (
        sum_rows(jnp.dot(activated, down_full, preferred_element_type=jnp.float32)) + biases_all[4]
    )
    layer_out = (middle + mlp_out).astype(jnp.bfloat16)
    grad_top = cotangent.astype(jnp.float32)
    up_full, down_full = fetch_mlp(up_weight, down_weight)
    grad_mlp_all = gather_rows(cotangent)
    grad_downw = contract_rows(activated, grad_mlp_all)
    grad_act = contract_cols(grad_mlp_all, down_full)
    unused, gelu_back = jax.vjp(jax.nn.gelu, pre_act)
    grad_pre = gelu_back(grad_act)[0].astype(jnp.bfloat16)
    grad_upw = contract_rows(second, grad_pre)
    grad_hidden_local = jnp.sum(grad_pre.astype(jnp.float32), axis=0)
    grad_second = sum_rows(contract_cols(grad_pre, up_full))
    unused, second_back = jax.vjp(layer_norm, middle, gains_all[1], second_all)
    grad_mid_part, grad_gain_two, grad_shift_two = second_back(grad_second)
    grad_middle = grad_top + grad_mid_part
    grad_up, grad_down = (
        lax.psum_scatter(grad_upw, "dp", scatter_dimension=0, tiled=True),
        lax.psum_scatter(grad_downw, "dp", scatter_dimension=1, tiled=True),
    )
    qkv_full, out_full = fetch_attn(qkv_weight, out_weight)
    grad_attn = grad_middle.astype(jnp.bfloat16)
    grad_attn_all = gather_rows(grad_attn)
    grad_outw = contract_rows(mixed, grad_attn_all)
    grad_mixed = contract_cols(grad_attn_all, out_full).astype(jnp.bfloat16)
    grad_queries, grad_keys, grad_values = attention_back(
        queries, keys_all, values_all, grad_mixed, log_total, scale
    )
    grad_rows = jnp.stack([grad_queries, grad_keys, grad_values]).astype(jnp.bfloat16)
    grad_qkvw = jnp.einsum("rd,jre->jde", normed, grad_rows, preferred_element_type=jnp.float32)
    grad_normed = sum_rows(
        jnp.einsum("jre,jde->rd", grad_rows, qkv_full, preferred_element_type=jnp.float32)
    )
    unused, first_back = jax.vjp(layer_norm, start_h, gains_all[0], biases_all[0])
    grad_start_part, grad_gain_one, grad_shift_one = first_back(grad_normed)
    grad_tokens = grad_middle + grad_start_part
    grad_qkv, grad_out = (
        lax.psum_scatter(grad_qkvw, "dp", scatter_dimension=1, tiled=True),
        lax.psum_scatter(grad_outw, "dp", scatter_dimension=1, tiled=True),
    )
    row_sums = jnp.sum(grad_rows.astype(jnp.float32), axis=1)
    gain_terms = jnp.stack([grad_gain_one, grad_gain_two])
    bias_terms = jnp.stack(
        [
            grad_shift_one,
            place_part(row_sums[0], width, slot * half_width),
            place_part(row_sums[2], width, slot * half_width),
            jnp.sum(grad_attn.astype(jnp.float32), axis=0),
            jnp.sum(grad_top, axis=0),
        ]
    )
    hidden_terms = place_part(
        grad_hidden_local,
        hidden_bias.shape[0] * lax.axis_size(("dp", "tensor")),
        slot * half_hidden,
    )
    seq_grad = jnp.sum(grad_tokens, axis=0, keepdims=True)
    table_terms = lax.dot_general(
        picker.astype(jnp.float32),
        seq_grad,
        (((0,), (0,)), ((), ())),
        precision=HIGH,
        preferred_element_type=jnp.float32,
    )
    grad_gains, grad_biases, grad_shift, grad_hidden, grad_table = (
        lax.psum_scatter(gain_terms, ("dp", "tensor"), scatter_dimension=1, tiled=True),
        lax.psum_scatter(bias_terms, ("dp", "tensor"), scatter_dimension=1, tiled=True),
        lax.psum_scatter(grad_shift_two, ("dp", "tensor"), scatter_dimension=0, tiled=True),
        lax.psum_scatter(hidden_terms, ("dp", "tensor"), scatter_dimension=0, tiled=True),
        lax.psum_scatter(table_terms, ("dp", "tensor"), scatter_dimension=1, tiled=True),
    )
    return (
        layer_out,
        grad_tokens,
        grad_gains,
        grad_biases,
        grad_shift,
        grad_hidden,
        grad_table,
        grad_qkv,
        grad_out,
        grad_up,
        grad_down,
    )


MESH_ID = pl.DeviceIdType.MESH
F32, BF16 = jnp.float32, jnp.bfloat16
NZ, NX, NC, NY = 4, 2, 2, 2
QB = 256
LINE = 40
GELU_A, GELU_B = 0.7978845608028654, 0.044715


def nt(left, right):
    return lax.dot_general(left, right, (((1,), (1,)), ((), ())), preferred_element_type=F32)


def nn(left, right):
    return lax.dot_general(left, right, (((1,), (0,)), ((), ())), preferred_element_type=F32)


def tn(left, right):
    return lax.dot_general(left, right, (((0,), (0,)), ((), ())), preferred_element_type=F32)


def position():
    dp = lax.axis_index("dp")
    return (lax.axis_index("tensor"), dp // (NX * NC), lax.rem(dp // NC, NX), lax.rem(dp, NC))


def device_at(y, z, x, c):
    return (z * (NX * NC) + x * NC + c, y)


def plane_peers(pos):
    y, z, x, c = pos
    for flip in range(1, NY * NX * NC):
        to = (1 - y if flip & 4 else y, z, 1 - x if flip & 2 else x, 1 - c if flip & 1 else c)
        yield flip - 1, to


def greet(pos):
    y, z, x, c = pos
    peers = [device_at(y, lax.rem(z + k, NZ), x, c) for k in range(1, NZ)]
    peers += [device_at(*to) for _, to in plane_peers(pos)]
    barrier = pltpu.get_barrier_semaphore()
    for peer in peers:
        pl.semaphore_signal(barrier, inc=1, device_id=peer, device_id_type=MESH_ID)
    return lambda: pl.semaphore_wait(barrier, len(peers))


def at_step(index, events):
    for step, names in events.items():

        @pl.when(index == step)
        def _():
            for name in names:
                name()


def remote(src, dst, send, recv, index, peer):
    return pltpu.make_async_remote_copy(
        src_ref=src,
        dst_ref=dst,
        send_sem=send.at[index],
        recv_sem=recv.at[index],
        device_id=peer,
        device_id_type=MESH_ID,
    )


class Gather:
    def __init__(self, buf, cols, send, recv, pos):
        self.buf, self.cols, self.send, self.recv, self.pos = buf, cols, send, recv, pos

    def view(self, y, z, x, c):
        return self.buf.at[y, z, x, c, :, self.cols]

    def steps(self, step):
        y, z, x, c = self.pos
        lo, hi, both = pl.ds(0, 2), pl.ds(2, 2), pl.ds(0, 2)
        if step == 0:
            return [
                (k - 1, (y, z, x, c), (y, lax.rem(z + NZ - k, NZ), x, c), device_at(y, lax.rem(z + k, NZ), x, c))
                for k in range(1, NZ)
            ]
        x_peer, y_peer = device_at(y, z, 1 - x, c), device_at(1 - y, z, x, c)
        if step == 1:
            return [(3, (y, lo, x, c), (y, lo, 1 - x, c), x_peer), (4, (y, hi, x, c), (1 - y, hi, x, c), y_peer)]
        if step == 2:
            return [
                (5, (y, lo, both, c), (1 - y, lo, both, c), y_peer),
                (6, (both, hi, x, c), (both, hi, 1 - x, c), x_peer),
            ]
        return [(7, (both, pl.ds(0, NZ), both, c), (both, pl.ds(0, NZ), both, 1 - c), device_at(y, z, x, 1 - c))]

    def start(self, step):
        for sem, src, _, peer in self.steps(step):
            remote(self.view(*src), self.view(*src), self.send, self.recv, sem, peer).start()

    def wait(self, step):
        for sem, _, dst, peer in self.steps(step):
            remote(self.view(*dst), self.view(*dst), self.send, self.recv, sem, peer).wait_recv()

    def next(self, step):
        self.wait(step)
        self.start(step + 1)

    def drain(self, count):
        for step in range(count):
            for sem, src, _, peer in self.steps(step):
                remote(self.view(*src), self.view(*src), self.send, self.recv, sem, peer).wait_send()


class SmallGather(Gather):
    def __init__(self, buf, send, recv, pos):
        super().__init__(buf, None, send, recv, pos)

    def view(self, y, z, x, c):
        return self.buf.at[y, z, x, c]

    def steps(self, step):
        y, z, x, c = self.pos
        if step == 0:
            return super().steps(0)
        every = pl.ds(0, NZ)
        return [
            (3 + flip, (y, every, x, c), (to[0], every, to[2], to[3]), device_at(*to)) for flip, to in plane_peers(self.pos)
        ]


class SmallScatter:
    def __init__(self, source, acc, first, last, send, recv, pos):
        self.source, self.acc, self.first, self.last = source, acc, first, last
        self.send, self.recv, self.pos = send, recv, pos

    def copies(self, step):
        y, z, x, c = self.pos
        every = pl.ds(0, NZ)
        if step == 0:
            return [
                remote(
                    self.source.at[to[0], every, to[2], to[3]],
                    self.first.at[flip],
                    self.send,
                    self.recv,
                    3 + flip,
                    device_at(*to),
                )
                for flip, to in plane_peers(self.pos)
            ]
        return [
            remote(
                self.acc.at[lax.rem(z + k, NZ)],
                self.last.at[k - 1],
                self.send,
                self.recv,
                k - 1,
                device_at(y, lax.rem(z + k, NZ), x, c),
            )
            for k in range(1, NZ)
        ]

    def start(self, step):
        for copy in self.copies(step):
            copy.start()

    def next(self):
        y, z, x, c = self.pos
        total = self.source[y, :, x, c]
        for flip, copy in enumerate(self.copies(0)):
            copy.wait_recv()
            total = total + self.first[flip]
        self.acc[...] = total
        self.start(1)

    def final(self):
        total = self.acc[self.pos[1]]
        for k, copy in enumerate(self.copies(1)):
            copy.wait_recv()
            total = total + self.last[k]
        return total

    def drain(self, _):
        for step in range(2):
            for copy in self.copies(step):
                copy.wait_send()


def small_scratch():
    tile = (8, 128)
    return [
        pltpu.VMEM((NY, NZ, NX, NC, *tile), F32),
        pltpu.VMEM((NZ, *tile), F32),
        pltpu.VMEM((NY * NX * NC - 1, NZ, *tile), F32),
        pltpu.VMEM((NZ - 1, *tile), F32),
    ]


def fold(values):
    return values[0:8] + pltpu.roll(values[8:16], LINE, 1) + pltpu.roll(values[16:24], 2 * LINE, 1)


def unfold(tile):
    return jnp.concatenate([tile, pltpu.roll(tile, 128 - LINE, 1), pltpu.roll(tile, 128 - 2 * LINE, 1)], axis=0)


def gelu_parts(v):
    square = v * v
    half = 0.5 + 0.5 * jnp.tanh(v * (GELU_A + (GELU_A * GELU_B) * square))
    act = v * half
    slope = half + (2.0 * act) * (1.0 - half) * (GELU_A + (3 * GELU_A * GELU_B) * square)
    return act, slope


def moments(hidden):
    average = jnp.mean(hidden, axis=-1, keepdims=True)
    centered = hidden - average
    variance = jnp.mean(centered * centered, axis=-1, keepdims=True)
    scale = lax.rsqrt(variance + EPS)
    return centered * scale, scale


def norm_back(xhat, scale, grad):
    return (grad - jnp.mean(grad, axis=-1, keepdims=True) - xhat * jnp.mean(grad * xhat, axis=-1, keepdims=True)) * scale


def row_block(index, size):
    return pl.ds(pl.multiple_of(index * size, size), size)


def sum_rows_of(values):
    return jnp.sum(values.astype(F32), axis=0, keepdims=True)


def blocks():
    for z in range(NZ):
        for x in range(NX):
            for c in range(NC):
                for y in range(NY):
                    yield (z * NX + x) * NC * NY + c * NY + y, (y, z, x, c)


def forward_kernel(
    dims,
    steps,
    gains,
    biases,
    shift2,
    hidden,
    table_t,
    tokens_in,
    qkv_in,
    outw_t,
    upw_in,
    downw_t,
    cot_in,
    q_out,
    k_out,
    v_out,
    mixed_out,
    normed_out,
    middle_out,
    gsec_out,
    small_out,
    lse_out,
    ghid_out,
    csum_out,
    layer_out,
    weights_out,
    grads_out,
    part_out,
    full,
    pack,
    lines,
    stage,
    tokens,
    cot,
    normed,
    queries,
    keys_all,
    values_all,
    mixed,
    middle,
    second,
    second_t,
    cot_t,
    result,
    gsec,
    act,
    gpre,
    gtile,
    hid,
    *rest,
):
    rows, width, per, half, ffh, ft = dims
    pos = position()
    y, z, x, c = pos
    me = device_at(y, z, x, c)[0] * NY + y
    share = width // (NZ * NX * NC * NY)
    n_ff = ffh // ft
    scatter_bufs, (send, recv, local) = rest[:-3], rest[-3:]

    n_groups = half // 128
    groups = [f"g{i}" for i in range(n_groups)]
    names = ["pack", "hid", *groups, "o"] + [f"m{i}" for i in range(n_ff)]
    col = {"o": pl.ds(3 * half, half)}
    for i in range(n_groups):
        col[f"g{i}"] = pl.ds(i * 384, 384)
    for i in range(n_ff):
        col[f"m{i}"] = pl.ds(4 * half + 2 * ft * i, 2 * ft)
    flow = {}
    for i, name in enumerate(names):
        if name in col:
            flow[name] = Gather(full, col[name], send.at[i], recv.at[i], pos)
        else:
            flow[name] = SmallGather({"pack": pack, "hid": lines}[name], send.at[i], recv.at[i], pos)
    ready = greet(pos)
    copies = {}

    def copy(name, src, dst):
        copies[name] = pltpu.make_async_copy(src, dst, local.at[len(copies)])
        copies[name].start()

    def own(start, size):
        return full.at[y, z, x, c, :, pl.ds(start, size)]

    parts = {"pack": [], "hid": []}
    for g in range(n_groups):
        parts[f"g{g}"] = [f"g{g}{i}" for i in range(3)]
        for i in range(3):
            copy(f"g{g}{i}", qkv_in.at[i, :, pl.ds(128 * g, 128)], own(384 * g + 128 * i, 128))
    copy("cot", cot_in, cot)
    copy("tokens", tokens_in, tokens)
    copy("o", outw_t, own(3 * half, half))
    parts["o"] = ["o"]
    for i in range(n_ff):
        copy(f"u{i}", upw_in.at[:, pl.ds(ft * i, ft)], own(4 * half + 2 * ft * i, ft))
        copy(f"d{i}", downw_t.at[:, pl.ds(ft * i, ft)], own(4 * half + 2 * ft * i + ft, ft))
        parts[f"m{i}"] = [f"u{i}", f"d{i}"]

    def launch(name):
        for key in parts[name]:
            copies[key].wait()
        flow[name].start(0)

    stage[...] = jnp.zeros_like(stage)
    stage[0:2, 0:share] = gains[...].astype(F32)
    stage[2:7, 0:share] = biases[...].astype(F32)
    stage[7:8, 0:share] = shift2[...].astype(F32)
    n_steps, n_seq = table_t.shape[1], steps.shape[1]
    wanted = jnp.concatenate([steps[...], jnp.full((1, 128 - n_seq), -1, jnp.int32)], axis=1)
    picked = (wanted == lax.broadcasted_iota(jnp.int32, (n_steps, 128), 0)).astype(BF16)
    pack[y, z, x, c] = fold(stage[...].T[0:share] + pltpu.roll(nn(table_t[...], picked), 8, 1))
    hshare = hidden.shape[1]
    lane = lax.broadcasted_iota(jnp.int32, (hshare, NC * NY * hshare), 0) + hshare * (c * NY + y)
    place = (lane == lax.broadcasted_iota(jnp.int32, (hshare, NC * NY * hshare), 1)).astype(BF16)
    spread = nn(jnp.broadcast_to(hidden[...], (8, hshare)), place)
    n_hid = NC * NY * hshare // 128
    pieces = [spread[0:1, 128 * j : 128 * j + 128] for j in range(n_hid)]
    lines[y, z, x, c] = jnp.concatenate([*pieces, jnp.zeros((8 - n_hid, 128), F32)], axis=0)

    ready()
    launch("pack")
    launch("g0")
    copies["cot"].wait()

    def turn_cot(i, total):
        rb = row_block(i, 256)
        block = cot[rb, :]
        cot_t[:, rb] = block.T
        return total + sum_rows_of(block)

    csum_out[...] = lax.fori_loop(0, rows // 256, turn_cot, jnp.zeros((1, width), F32))
    flow["pack"].next(0)
    flow["g0"].next(0)
    launch("g1")
    flow["g0"].next(1)
    flow["pack"].wait(1)
    flow["g1"].next(0)
    launch("g2")
    launch("hid")
    launch("o")

    for d, (by, bz, bx, bc) in blocks():
        middle[d * share : d * share + share, 0:128] = unfold(pack[by, bz, bx, bc])
    small_out[...] = middle[0:width, 0:128].T
    embed = small_out[pl.ds(8 + me, 1), :]
    copies["tokens"].wait()
    flow["g0"].next(2)

    def first_norm(i, _):
        rb = row_block(i, 128)
        xhat, _ = moments(tokens[rb, :].astype(F32) + embed)
        normed[rb, :] = (xhat * small_out[0:1, :] + small_out[2:3, :]).astype(BF16)
        return 0

    lax.fori_loop(0, rows // 128, first_norm, 0)
    copy("normed", normed, normed_out)
    flow["g1"].next(1)
    flow["g2"].next(0)
    launch("m0")

    def whole(cols, size):
        return jnp.concatenate([full[by, :, :, :, :, cols].reshape(width, size) for by in range(NY)], axis=1)

    def project(group):
        cols = pl.ds(pl.multiple_of(group * 384, 128), 384)

        def body(i, _):
            rb = row_block(i, 512)
            value = nn(normed[rb, :], whole(cols, 384))
            for by in range(NY):
                to = pl.ds(pl.multiple_of((by * n_groups + group) * 128, 128), 128)
                piece = [value[:, by * 384 + 128 * j : by * 384 + 128 * j + 128] for j in range(3)]
                queries[rb, to] = (piece[0] + small_out[3:4, to]).astype(BF16) * jnp.asarray(HEAD_DIM**-0.5, BF16)
                keys_all[rb, to] = piece[1].astype(BF16)
                values_all[rb, to] = (piece[2] + small_out[4:5, to]).astype(BF16)
            return 0

        lax.fori_loop(0, rows // 512, body, 0)

    def then(name, step):
        return lambda: flow[name].next(step)

    def arrived(name):
        return lambda: flow[name].wait(3)

    def off(name):
        return lambda: launch(name)

    events = {
        (0, 1): [then("o", 0), then("hid", 0)],
        (0, 2): [then("g1", 2)],
        (0, 3): [then("g2", 1), off("m1")],
        (1, 2): [then("m0", 0)],
        (1, 3): [then("o", 1)],
        (2, 0): [then("g2", 2)],
        (2, 2): [off("m2")],
        (3, 0): [then("o", 2), then("m1", 0)],
        (3, 2): [then("m0", 1)],
        (5, 0): [then("m2", 0), then("m1", 1)],
    }

    def attend(s, _):
        group, by = s // NY, lax.rem(s, NY)
        p = by * n_groups + group

        @pl.when(by == 0)
        def _():
            at_step(group, {g: [arrived(f"g{g}")] for g in range(n_groups)})
            project(group)

        cols = pl.ds(pl.multiple_of(p * 128, 128), 128)
        low = lax.broadcasted_iota(jnp.int32, (QB, 128), 1) < HEAD_DIM
        for i in range(rows // QB):
            at_step(s, {key[0]: names for key, names in events.items() if key[1] == i})
            n = (i + 1) * QB
            rb = slice(i * QB, n)
            key, value, query = keys_all[0:n, cols], values_all[0:n, cols], queries[rb, cols]
            outs, scales = [], []
            for h in range(2):
                scores = nt(key, jnp.where(low == (h == 0), query, jnp.zeros_like(query)))
                top = jnp.max(scores, axis=0, keepdims=True)
                expo = jnp.exp(scores - top)
                total = jnp.sum(expo, axis=0, keepdims=True)
                lse_out[pl.ds(2 * p + h, 1), rb] = top + jnp.log(total)
                scales.append(jnp.broadcast_to(1.0 / total, (HEAD_DIM, QB)))
                outs.append(tn(expo.astype(BF16), value))
            scale = jnp.concatenate(scales, axis=0).T
            mixed[rb, cols] = (jnp.where(low, outs[0], outs[1]) * scale).astype(BF16)
        return 0

    lax.fori_loop(0, width // 128, attend, 0)
    copy("queries", queries, q_out)
    copy("keys", keys_all, k_out)
    copy("values", values_all, v_out)
    flow["o"].wait(3)
    flow["m0"].next(2)
    flow["hid"].wait(1)
    for bz in range(NZ):
        for bx in range(NX):
            total = lines[0, bz, bx, 0] + lines[0, bz, bx, 1] + lines[1, bz, bx, 0] + lines[1, bz, bx, 1]
            for j in range(n_hid):
                at = ((bz * NX + bx) * n_hid + j) * 128
                hid[0:1, at : at + 128] = total[j : j + 1]
    copy("mixed", mixed, mixed_out)
    for by in range(NY):
        copy(f"w{by}", full.at[by, :, :, :, :, pl.ds(0, 4 * half)], weights_out.at[by])

    def second_norm(i, _):
        rb = row_block(i, 256)
        start_h = tokens[rb, :].astype(F32) + embed
        value = start_h + (nt(mixed[rb, :], whole(col["o"], half)) + small_out[5:6, :])
        middle[rb, :] = value
        xhat, _ = moments(value)
        block = (xhat * small_out[1:2, :] + small_out[7:8, :]).astype(BF16)
        second[rb, :] = block
        second_t[:, rb] = block.T
        return 0

    lax.fori_loop(0, rows // 256, second_norm, 0)
    copy("middle", middle, middle_out)
    flow["m0"].wait(3)
    at = len(copies)

    def tile_copy(t, slot):
        ty, tm = lax.rem(t, NY), t // NY
        return pltpu.make_async_copy(
            gtile.at[slot],
            grads_out.at[ty, :, :, :, :, pl.ds(pl.multiple_of(tm * 2 * ft, 128), 2 * ft)],
            local.at[at + slot],
        )

    part = Scatter(
        grads_out.at[:, :, :, :, :, pl.ds(0, 2 * ft)],
        scatter_bufs[0],
        scatter_bufs[1:],
        send.at[len(names)],
        recv.at[len(names)],
        pos,
        True,
    )
    part_load = pltpu.make_async_copy(part.source.at[:, :, :, c], part.own, local.at[at + 2])
    tiles = NY * n_ff

    def tile(t, _):
        ty, tm = lax.rem(t, NY), t // NY
        slot = lax.rem(t, 2)

        def load_part():
            part_load.wait()
            part.next(0)

        at_step(t, {2: [arrived("m1")], 3: [then("m2", 2), load_part], 4: [arrived("m2")]})
        up_at = pl.ds(pl.multiple_of(4 * half + tm * 2 * ft, 128), ft)
        down_at = pl.ds(pl.multiple_of(4 * half + tm * 2 * ft + ft, 128), ft)
        hid_at = pl.ds(pl.multiple_of(ty * ffh + tm * ft, 128), ft)

        def up():
            return full[ty, :, :, :, :, up_at].reshape(width, ft)

        def down():
            return full[ty, :, :, :, :, down_at].reshape(width, ft)

        pre = nn(second[...], up()) + hid[:, hid_at]
        gact = nn(cot[...], down())
        value, slope = gelu_parts(pre)
        act[...] = value.astype(BF16)
        grad = (gact * slope).astype(BF16)
        gpre[...] = grad
        ghid_out[:, hid_at] = sum_rows_of(grad)
        more = nt(act[...], down())
        gmore = nt(gpre[...], up())

        @pl.when(t == 0)
        def _():
            result[...] = more
            gsec[...] = gmore

        @pl.when(t > 0)
        def _():
            result[...] += more
            gsec[...] += gmore

        @pl.when(t > 0)
        def _():
            tile_copy(t - 1, 1 - slot).wait()

        def start_part():
            part_load.start()
            part.start(0)

        at_step(
            t,
            {
                0: [then("m2", 1)],
                1: [then("m1", 2)],
                2: [start_part],
                4: [lambda: part.next(1)],
            },
        )

        def weight_grad(i, _):
            rb = row_block(i, 384)
            gz = pl.ds(i * 2, 2)
            gtile[slot, gz, :, :, :, 0:ft] = nn(second_t[rb, :], gpre[...]).astype(BF16).reshape(2, NX, NC, per, ft)
            gtile[slot, gz, :, :, :, ft : 2 * ft] = nn(cot_t[rb, :], act[...]).astype(BF16).reshape(2, NX, NC, per, ft)
            return 0

        @pl.when(t == tiles - 1)
        def _():
            def finish(i, _):
                rb = row_block(i, 128)
                normed[rb, :] = (middle[rb, :] + (result[rb, :] + small_out[6:7, :])).astype(BF16)
                return 0

            copies["normed"].wait()
            lax.fori_loop(0, rows // 128, finish, 0)
            last_copies[0].start()
            last_copies[1].start()

        lax.fori_loop(0, width // 384, weight_grad, 0)
        tile_copy(t, slot).start()
        return 0

    last_copies = [
        pltpu.make_async_copy(normed, layer_out, local.at[at + 3]),
        pltpu.make_async_copy(gsec, gsec_out, local.at[at + 4]),
    ]
    lax.fori_loop(0, tiles, tile, 0)
    part.wait(2)
    part.add(2)
    part_save = pltpu.make_async_copy(part.own.at[y, :, x], part_out, local.at[at + 5])
    part_save.start()
    tile_copy(tiles - 1, (tiles - 1) % 2).wait()
    for key in ["queries", "keys", "values", "mixed", "middle"] + [f"w{by}" for by in range(NY)]:
        copies[key].wait()
    for last in last_copies:
        last.wait()
    for name in names:
        flow[name].drain(4 if name in col else 2)
    part.drain(3)
    part_save.wait()


class Scatter:
    def __init__(self, source, own, bufs, send, recv, pos, loaded):
        self.source, self.own, self.bufs = source, own, bufs
        self.send, self.recv, self.pos, self.loaded = send, recv, pos, loaded

    def copies(self, step):
        y, z, x, c = self.pos
        first, second_x, second_y, third_y, third_x, last = self.bufs
        own = self.own
        lo, hi, both = pl.ds(0, 2), pl.ds(2, 2), pl.ds(0, 2)
        x_peer, y_peer = device_at(y, z, 1 - x, c), device_at(1 - y, z, x, c)
        if step == 0:
            return [(0, self.source.at[both, pl.ds(0, NZ), both, 1 - c], first, device_at(y, z, x, 1 - c))]
        if step == 1:
            return [(1, own.at[both, lo, 1 - x], second_x, x_peer), (2, own.at[1 - y, hi, both], second_y, y_peer)]
        if step == 2:
            return [(3, own.at[1 - y, lo, x], third_y, y_peer), (4, own.at[y, hi, 1 - x], third_x, x_peer)]
        return [
            (4 + k, own.at[y, lax.rem(z + k, NZ), x], last.at[k - 1], device_at(y, lax.rem(z + k, NZ), x, c))
            for k in range(1, NZ)
        ]

    def start(self, step):
        for sem, src, dst, peer in self.copies(step):
            remote(src, dst, self.send, self.recv, sem, peer).start()

    def wait(self, step):
        for sem, src, dst, peer in self.copies(step):
            remote(src, dst, self.send, self.recv, sem, peer).wait_recv()

    def add(self, step):
        y, z, x, c = self.pos
        own, source = self.own, self.source
        first, second_x, second_y, third_y, third_x, last = self.bufs
        kind = own.dtype

        def plus(left, right):
            return (left.astype(F32) + right.astype(F32)).astype(kind)

        def each(count, body):
            def run(i, _):
                body(i)
                return 0

            lax.fori_loop(0, count, run, 0)

        if step == 0:

            def body(i):
                iy, iz, ix = i // (NZ * NX), lax.rem(i // NX, NZ), lax.rem(i, NX)
                mine = own[iy, iz, ix] if self.loaded else source[iy, iz, ix, c]
                own[iy, iz, ix] = plus(mine, first[iy, iz, ix])

            each(NY * NZ * NX, body)
        elif step == 1:

            def body(i):
                a, b = i // 2, lax.rem(i, 2)
                own[a, b, x] = plus(own[a, b, x], second_x[a, b])
                own[y, 2 + a, b] = plus(own[y, 2 + a, b], second_y[a, b])

            each(4, body)
        else:

            def body(i):
                own[y, i, x] = plus(own[y, i, x], third_y[i])
                own[y, 2 + i, x] = plus(own[y, 2 + i, x], third_x[i])

            each(2, body)

    def next(self, step):
        self.wait(step)
        self.add(step)
        self.start(step + 1)

    def final(self):
        y, z, x, c = self.pos
        last = self.bufs[5]
        self.wait(3)
        total = self.own[y, z, x].astype(F32)
        for k in range(NZ - 1):
            total = total + last[k].astype(F32)
        return total

    def drain(self, count, first=0):
        for step in range(first, count):
            for sem, src, dst, peer in self.copies(step):
                remote(src, dst, self.send, self.recv, sem, peer).wait_send()


def scatter_scratch(per, width, kind):
    return [
        pltpu.VMEM((NY, NZ, NX, per, width), kind),
        pltpu.VMEM((NY, NZ, NX, per, width), kind),
        pltpu.VMEM((2, 2, per, width), kind),
        pltpu.VMEM((2, 2, per, width), kind),
        pltpu.VMEM((2, per, width), kind),
        pltpu.VMEM((2, per, width), kind),
        pltpu.VMEM((NZ - 1, per, width), kind),
    ]


def backward_kernel(
    dims,
    small,
    lse,
    ghid,
    csum,
    tokens_in,
    cot_in,
    q_in,
    k_in,
    v_in,
    mixed_in,
    normed_in,
    middle_in,
    gsec_in,
    weights_in,
    grads_in,
    part_in,
    gup_out,
    gdown_out,
    gout_out,
    gqkv_out,
    gpack_out,
    gtok_out,
    tokens,
    cot,
    part_own,
    part_last,
    queries,
    keys_all,
    values_all,
    mixed,
    normed,
    normed_t,
    middle,
    gsec,
    weights,
    gattn,
    gattn_t,
    gval,
    gmixed,
    acc,
    inner,
    sums,
    gout,
    gqkv,
    *rest,
):
    rows, width, per, half, ffh, ft = dims
    pos = position()
    y, z, x, c = pos
    me = device_at(y, z, x, c)[0] * NY + y
    share = width // (NZ * NX * NC * NY)
    n_ff = ffh // ft
    n_groups = half // 128
    names = [f"m{i}" for i in range(n_ff)] + ["o"] + [f"q{i}" for i in range(n_groups)] + ["pack", "hid"]
    send, recv, local = rest[-3:]
    flow = {}
    for i, name in enumerate(names):
        if name == "m0":
            continue
        if name in ("pack", "hid"):
            at = -11 if name == "pack" else -7
            flow[name] = SmallScatter(*rest[at : at + 4], send.at[i], recv.at[i], pos)
            continue
        own, first, *others = rest[7 * i - 7 : 7 * i]
        if name[0] == "m":
            source = grads_in.at[:, :, :, :, :, pl.ds(2 * ft * i, 2 * ft)]
        else:
            source = gout if name == "o" else gqkv.at[int(name[1:])]
        flow[name] = Scatter(source, own, [first] + others, send.at[i], recv.at[i], pos, name[0] == "m")

    copies = {}

    def load(name, src, dst):
        copies[name] = pltpu.make_async_copy(src, dst, local.at[len(copies)])
        copies[name].start()

    ready = greet(pos)
    n_hid = ghid.shape[1] // (NZ * NX * 128)
    for d, (by, bz, bx, bc) in blocks():
        start = (bz * NX + bx) * n_hid
        pieces = [ghid[:, 128 * (start + j) : 128 * (start + j + 1)] for j in range(n_hid)]
        flow["hid"].source[by, bz, bx, bc] = jnp.concatenate([*pieces, jnp.zeros((8 - n_hid, 128), F32)], axis=0)
    load("part", part_in, part_own)
    for i in range(4):
        rb = pl.ds(i * (rows // 4), rows // 4)
        load(f"middle{i}", middle_in.at[rb], middle.at[rb])
        load(f"gsec{i}", gsec_in.at[rb], gsec.at[rb])
        load(f"cot{i}", cot_in.at[rb], cot.at[rb])
    for i in range(1, n_ff):
        load(f"m{i}", flow[f"m{i}"].source.at[:, :, :, c], flow[f"m{i}"].own)
    load("mixed", mixed_in, mixed)
    load("w", weights_in, weights)
    load("normed", normed_in, normed)
    load("q", q_in, queries)
    load("k", k_in, keys_all)
    load("v", v_in, values_all)
    load("tokens", tokens_in, tokens)

    def part_copies():
        m0 = names.index("m0")
        return [
            remote(
                part_own.at[lax.rem(z + k, NZ)],
                part_last.at[k - 1],
                send.at[m0],
                recv.at[m0],
                k,
                device_at(y, lax.rem(z + k, NZ), x, c),
            )
            for k in range(1, NZ)
        ]

    def second_back(i, totals):
        arrive = [lambda i=i: [copies[f"{name}{i}"].wait() for name in ("middle", "gsec", "cot")] for i in range(4)]
        at_step(i, {rows // 512 * k: [arrive[k]] for k in range(4)})
        rb = row_block(i, 128)
        xhat, scale = moments(middle[rb, :])
        grad = gsec[rb, :]
        result = cot[rb, :].astype(F32) + norm_back(xhat, scale, grad * small[1:2, :])
        gsec[rb, :] = result
        low = result.astype(BF16)
        gattn[rb, :] = low
        gattn_t[:, rb] = low.T
        return (
            totals[0] + sum_rows_of(grad * xhat),
            totals[1] + sum_rows_of(grad),
            totals[2] + sum_rows_of(low),
        )

    zero = jnp.zeros((1, width), F32)
    totals = lax.fori_loop(0, rows // 256, second_back, (zero, zero, zero))
    ready()
    for i in range(1, n_ff):
        flow[f"m{i}"].start(0)
    copies["part"].wait()
    for copy in part_copies():
        copy.start()
    flow["hid"].start(0)
    ggain2, gshift2, gattn_sum = lax.fori_loop(rows // 256, rows // 128, second_back, totals)
    sums[...] = jnp.zeros_like(sums)
    sums[1:2, :] = ggain2
    sums[5:6, :] = gattn_sum
    sums[6:7, :] = csum[...]
    sums[7:8, :] = gshift2
    copies["m1"].wait()
    flow["m1"].next(0)
    copies["w"].wait()
    copies["mixed"].wait()

    def whole(index):
        if index == 3:
            return jnp.concatenate([weights[by, :, pl.ds(3 * half, half)] for by in range(NY)], axis=1)
        picks = [weights[by, :, pl.ds(384 * g + 128 * index, 128)] for by in range(NY) for g in range(n_groups)]
        return jnp.concatenate(picks, axis=1)

    for by in range(NY):
        def out_grad(i, _):
            rb = row_block(i, 384)
            part = nn(gattn_t[rb, :], mixed[:, by * half : by * half + half]).astype(BF16)
            gout[by, pl.ds(i * 2, 2)] = part.reshape(2, NX, NC, per, half)
            return 0

        lax.fori_loop(0, width // 384, out_grad, 0)
    flow["o"].start(0)

    def mixed_grad(i, _):
        rb = row_block(i, 512)
        gmixed[rb, :] = nn(gattn[rb, :], whole(3)).astype(BF16)
        return 0

    lax.fori_loop(0, rows // 512, mixed_grad, 0)
    copies["m2"].wait()
    flow["m2"].next(0)
    flow["o"].next(0)
    copies["normed"].wait()

    def turn_normed(i, _):
        rb = row_block(i, 256)
        normed_t[:, rb] = normed[rb, :].T
        return 0

    lax.fori_loop(0, rows // 256, turn_normed, 0)
    copies["q"].wait()
    copies["k"].wait()
    copies["v"].wait()
    gq, gk, gv = gattn, normed, gval

    def then(name, step):
        return lambda: flow[name].next(step)

    events = {
        (2, 0): [then("m1", 1)],
        (2, 1): [then("q0", 0)],
        (2, 2): [then("m2", 1)],
        (3, 0): [then("o", 1), flow["hid"].next],
        (4, 0): [then("m1", 2)],
        (4, 1): [then("q1", 0)],
        (4, 2): [then("q0", 1)],
        (5, 0): [then("m2", 2)],
        (5, 1): [then("o", 2)],
        (5, 2): [then("q0", 2)],
    }

    def attend_back(s, _):
        group, by = s // NY, lax.rem(s, NY)
        p = by * n_groups + group

        cols = pl.ds(pl.multiple_of(p * 128, 128), 128)
        dots = (gmixed[:, cols].astype(F32) * mixed[:, cols].astype(F32)).T
        for h in range(2):
            inner[h : h + 1, :] = jnp.sum(dots[HEAD_DIM * h : HEAD_DIM * (h + 1)], axis=0, keepdims=True)
        for j in range(rows // QB):
            at_step(s, {key[0]: names for key, names in events.items() if key[1] == j})
            kb, first = slice(j * QB, (j + 1) * QB), j * QB
            later = rows - first
            key, value = keys_all[kb, cols], values_all[kb, cols]
            low = lax.broadcasted_iota(jnp.int32, (later, 128), 1) < HEAD_DIM

            def two(block):
                none = jnp.zeros_like(block)
                return jnp.concatenate([jnp.where(low, block, none), jnp.where(low, none, block)], axis=0)

            query, grad = two(queries[first:rows, cols]), two(gmixed[first:rows, cols])
            logs = jnp.concatenate([lse[pl.ds(2 * p + h, 1), first:rows] for h in range(2)], axis=1)
            inners = jnp.concatenate([inner[h : h + 1, first:rows] for h in range(2)], axis=1)
            probs = jnp.exp(nt(key, query) - logs)
            gscores = (probs * (nt(value, grad) - inners)).astype(BF16)
            gv[kb, cols] = nn(probs.astype(BF16), grad).astype(BF16)
            gk[kb, cols] = nn(gscores, query).astype(BF16)
            both = tn(gscores, key)
            more = jnp.where(low, both[:later], both[later:])
            if j == 0:
                acc[...] = more
            else:
                acc[first:rows] += more
        gq[:, cols] = (acc[...] * HEAD_DIM**-0.5).astype(BF16)

        @pl.when(by == NY - 1)
        def _():
            for piece, source in enumerate((gq, gk, gv)):
                pick = jnp.concatenate(
                    [source[:, pl.ds(pl.multiple_of((b * n_groups + group) * 128, 128), 128)] for b in range(NY)], axis=1
                )
                part = nn(normed_t[...], pick).astype(BF16)
                for b in range(NY):
                    gqkv[group, b, :, :, :, :, piece * 128 : piece * 128 + 128] = part[:, b * 128 : b * 128 + 128].reshape(
                        NZ, NX, NC, per, 128
                    )
            for g in range(n_groups):
                @pl.when(group == g)
                def _():
                    flow[f"q{g}"].start(0)

        return 0

    lax.fori_loop(0, NY * n_groups, attend_back, 0)
    copies["tokens"].wait()
    embed = small[pl.ds(8 + me, 1), :]

    def first_back(i, totals):
        rb = row_block(i, 256)
        xhat, scale = moments(tokens[rb, :].astype(F32) + embed)
        q_rows, k_rows, v_rows = gq[rb, :], gk[rb, :], gv[rb, :]
        grad = nt(q_rows, whole(0)) + nt(k_rows, whole(1)) + nt(v_rows, whole(2))
        result = gsec[rb, :] + norm_back(xhat, scale, grad * small[0:1, :])
        middle[rb, :] = result

        at_step(
            i,
            {0: [then("q1", 1)], 1: [then("q2", 0)], 2: [then("q1", 2)], 3: [then("q2", 1)]},
        )
        return (
            totals[0] + sum_rows_of(grad * xhat),
            totals[1] + sum_rows_of(grad),
            totals[2] + sum_rows_of(q_rows),
            totals[3] + sum_rows_of(v_rows),
            totals[4] + sum_rows_of(result),
        )

    ggain1, gshift1, q_sum, v_sum, seq_sum = lax.fori_loop(0, rows // 256, first_back, (zero,) * 5)
    sums[0:1, :] = ggain1
    sums[2:3, :] = gshift1
    sums[3:4, :] = q_sum
    sums[4:5, :] = v_sum
    sums[pl.ds(8 + me, 1), :] = seq_sum
    gtok = pltpu.make_async_copy(middle, gtok_out, local.at[len(copies)])
    gtok.start()
    turned = sums[...].T
    for d, (by, bz, bx, bc) in blocks():
        flow["pack"].source[by, bz, bx, bc] = fold(turned[d * share : d * share + share])
    flow["pack"].start(0)
    flow["q2"].next(2)
    total = part_own[z].astype(F32)
    for k, copy in enumerate(part_copies()):
        copy.wait_recv()
        total = total + part_last[k].astype(F32)
    gup_out[:, 0:ft] = total[:, 0:ft]
    gdown_out[:, 0:ft] = total[:, ft:]
    for i in range(1, n_ff):
        total = flow[f"m{i}"].final()
        gup_out[:, ft * i : ft * i + ft] = total[:, 0:ft]
        gdown_out[:, ft * i : ft * i + ft] = total[:, ft:]
    flow["pack"].next()
    gout_out[...] = flow["o"].final()
    gpack_out[8:16] = flow["hid"].final()

    def qkv_final(g):
        total = flow[f"q{g}"].final()
        for piece in range(3):
            gqkv_out[piece, :, 128 * g : 128 * g + 128] = total[:, 128 * piece : 128 * piece + 128]

    for g in range(n_groups):
        qkv_final(g)
    gpack_out[0:8] = flow["pack"].final()
    gtok.wait()
    for copy in part_copies():
        copy.wait_send()
    for name in names[1:]:
        flow[name].drain(4)


def finish_kernel(slots, count, steps, gpack, *refs):
    large, (gains_out, biases_out, shift_out, hidden_out, table_out) = refs[:count], refs[count : count + 5]
    outs, bufs, (load_sem, save_sem) = refs[count + 5 : 2 * count + 5], refs[2 * count + 5 : 3 * count + 5], refs[-2:]
    pieces = []
    for src, buf, out in zip(large, bufs, outs):
        cut = 4 if src.shape[0] % 512 == 0 else 1
        size = src.shape[0] // cut
        for k in range(cut):
            at, n = pl.ds(k * size, size), len(pieces)
            pieces.append(
                (
                    pltpu.make_async_copy(src.at[at], buf.at[at], load_sem.at[n]),
                    pltpu.make_async_copy(buf.at[at], out.at[at], save_sem.at[n]),
                )
            )
    for load, _ in pieces:
        load.start()
    share, hshare = gains_out.shape[1], hidden_out.shape[1]
    features = unfold(gpack[0:8, :])
    turned = jnp.concatenate([features, jnp.zeros((128 - share, 128), F32)], axis=0).T
    gains_out[...] = turned[0:2, 0:share]
    biases_out[...] = turned[2:7, 0:share]
    shift_out[...] = turned[7:8, 0:share]
    slot = lax.rem(lax.axis_index("dp"), NC) * NY + lax.axis_index("tensor")
    line = jnp.concatenate([gpack[8 + j : 9 + j, :] for j in range(slots * hshare // 128)], axis=1)
    value = line[:, 0:hshare]
    for k in range(1, slots):
        value = jnp.where(slot == k, line[:, hshare * k : hshare * k + hshare], value)
    hidden_out[...] = value
    n_steps, n_seq = table_out.shape[1], steps.shape[1]
    picked = (steps[...] == lax.broadcasted_iota(jnp.int32, (n_steps, n_seq), 0)).astype(F32)
    table_out[...] = lax.dot_general(
        features[:, 8 : 8 + n_seq], picked, (((1,), (1,)), ((), ())), precision=HIGH, preferred_element_type=F32
    )
    for load, save in pieces:
        load.wait()
        save.start()
    for _, save in pieces:
        save.wait()


def fast_shards(
    tokens,
    timesteps,
    norm_gains,
    biases,
    second_shift,
    hidden_bias,
    step_table,
    qkv_weight,
    out_weight,
    up_weight,
    down_weight,
    cotangent,
):
    rows, width = tokens.shape
    _, per, half = qkv_weight.shape
    ffh = up_weight.shape[1]
    ft = 512
    dims = (rows, width, per, half, ffh, ft)
    n_ff, n_groups = ffh // ft, half // 128
    total = 4 * half + 2 * ffh
    vmem, anywhere = pl.BlockSpec(memory_space=pltpu.VMEM), pl.BlockSpec(memory_space=pl.ANY)
    shape = jax.ShapeDtypeStruct
    low, wide = shape((rows, width), BF16), shape((rows, width), F32)
    vm = pltpu.VMEM
    hshare = hidden_bias.shape[0]
    n_chunks = 3 + n_groups + n_ff
    steps = timesteps.reshape(1, -1)
    outs = pl.pallas_call(
        functools.partial(forward_kernel, dims),
        in_specs=[vmem] * 6 + [anywhere] * 6,
        out_specs=[anywhere] * 7 + [vmem] * 4 + [anywhere] * 4,
        out_shape=[
            low,
            low,
            low,
            low,
            low,
            wide,
            wide,
            shape((128, width), F32),
            shape((16, rows), F32),
            shape((1, NY * ffh), F32),
            shape((1, width), F32),
            low,
            shape((NY, NZ, NX, NC, per, 4 * half), BF16),
            shape((NY, NZ, NX, NC, per, 2 * ffh), BF16),
            shape((NZ, per, 2 * ft), BF16),
        ],
        scratch_shapes=[
            vm((NY, NZ, NX, NC, per, total), BF16),
            vm((NY, NZ, NX, NC, 8, 128), F32),
            vm((NY, NZ, NX, NC, 8, 128), F32),
            vm((128, 128), F32),
            vm((rows, width), BF16),
            vm((rows, width), BF16),
            vm((rows, width), BF16),
            vm((rows, width), BF16),
            vm((rows, width), BF16),
            vm((rows, width), BF16),
            vm((rows, width), BF16),
            vm((rows, width), F32),
            vm((rows, width), BF16),
            vm((width, rows), BF16),
            vm((width, rows), BF16),
            vm((rows, width), F32),
            vm((rows, width), F32),
            vm((rows, ft), BF16),
            vm((rows, ft), BF16),
            vm((2, NZ, NX, NC, per, 2 * ft), BF16),
            vm((1, NY * ffh), F32),
            *scatter_scratch(per, 2 * ft, BF16),
            pltpu.SemaphoreType.DMA((n_chunks + 1, 10)),
            pltpu.SemaphoreType.DMA((n_chunks + 1, 10)),
            pltpu.SemaphoreType.DMA((18 + 3 * n_groups + 2 * n_ff,)),
        ],
        compiler_params=pltpu.CompilerParams(collective_id=0, has_side_effects=True, vmem_limit_bytes=VMEM_LIMIT),
        name="layer_forward",
    )(
        steps,
        norm_gains,
        biases,
        second_shift.reshape(1, -1),
        hidden_bias.reshape(1, -1),
        step_table.T,
        tokens,
        qkv_weight,
        out_weight.T,
        up_weight,
        down_weight.T,
        cotangent,
    )
    q, k, v, mixed, normed, middle, gsec, small, lse, ghid, csum, layer, weights, grads, part = outs
    chunks = [2 * ft] * (n_ff - 1) + [half] * (1 + n_groups)
    scratch = []
    for cols in chunks:
        scratch += scatter_scratch(per, cols, BF16)
    scratch += small_scratch() + small_scratch()
    gup, gdown, gout, gqkv, gpack, gtok = pl.pallas_call(
        functools.partial(backward_kernel, dims),
        in_specs=[vmem] * 4 + [anywhere] * 12,
        out_specs=[vmem] * 5 + [anywhere],
        out_shape=[
            shape((per, ffh), F32),
            shape((per, ffh), F32),
            shape((per, half), F32),
            shape((3, per, half), F32),
            shape((16, 128), F32),
            wide,
        ],
        scratch_shapes=[
            vm((rows, width), BF16),
            vm((rows, width), BF16),
            vm((NZ, per, 2 * ft), BF16),
            vm((NZ - 1, per, 2 * ft), BF16),
            vm((rows, width), BF16),
            vm((rows, width), BF16),
            vm((rows, width), BF16),
            vm((rows, width), BF16),
            vm((rows, width), BF16),
            vm((width, rows), BF16),
            vm((rows, width), F32),
            vm((rows, width), F32),
            vm((NY, width, 4 * half), BF16),
            vm((rows, width), BF16),
            vm((width, rows), BF16),
            vm((rows, width), BF16),
            vm((rows, width), BF16),
            vm((rows, 128), F32),
            vm((8, rows), F32),
            vm((128, width), F32),
            vm((NY, NZ, NX, NC, per, half), BF16),
            vm((n_groups, NY, NZ, NX, NC, per, 3 * 128), BF16),
            *scratch,
            pltpu.SemaphoreType.DMA((len(chunks) + 3, 10)),
            pltpu.SemaphoreType.DMA((len(chunks) + 3, 10)),
            pltpu.SemaphoreType.DMA((20 + n_ff,)),
        ],
        compiler_params=pltpu.CompilerParams(collective_id=1, has_side_effects=True, vmem_limit_bytes=VMEM_LIMIT),
        name="layer_backward",
    )(
        small,
        lse,
        ghid,
        csum,
        tokens,
        cotangent,
        q,
        k,
        v,
        mixed,
        normed,
        middle,
        gsec,
        weights.reshape(NY, width, 4 * half),
        grads,
        part,
    )
    share, n_steps = norm_gains.shape[1], step_table.shape[0]
    large = (gtok, layer, gqkv, gout, gup, gdown)
    pieces = sum(4 if array.shape[0] % 512 == 0 else 1 for array in large)
    small_shapes = [(2, share), (5, share), (1, share), (1, hshare), (share, n_steps)]
    large_shapes = [shape(array.shape, array.dtype) for array in large]
    grad_gains, grad_biases, grad_shift, grad_hidden, grad_table, gtok, layer, gqkv, gout, gup, gdown = pl.pallas_call(
        functools.partial(finish_kernel, NC * NY, len(large)),
        in_specs=[vmem] * 2 + [anywhere] * len(large),
        out_specs=[vmem] * 5 + [anywhere] * len(large),
        out_shape=[shape(dims, F32) for dims in small_shapes] + large_shapes,
        scratch_shapes=[vm(array.shape, array.dtype) for array in large] + [pltpu.SemaphoreType.DMA((pieces,))] * 2,
        name="finish",
    )(steps, gpack, *large)
    return (
        layer,
        gtok,
        grad_gains,
        grad_biases,
        grad_shift.reshape(share),
        grad_hidden.reshape(hshare),
        grad_table.T,
        gqkv,
        gout.T,
        gup,
        gdown.T,
    )


def solution(mesh):
    in_specs = (
        P(("dp", "tensor"), None),
        P(),
        P(None, ("dp", "tensor")),
        P(None, ("dp", "tensor")),
        P(("dp", "tensor")),
        P(("dp", "tensor")),
        P(None, ("dp", "tensor")),
        P(None, "dp", "tensor"),
        P("tensor", "dp"),
        P("dp", "tensor"),
        P("tensor", "dp"),
        P(("dp", "tensor"), None),
    )
    out_specs = (
        P(("dp", "tensor"), None),
        P(("dp", "tensor"), None),
        P(None, ("dp", "tensor")),
        P(None, ("dp", "tensor")),
        P(("dp", "tensor")),
        P(("dp", "tensor")),
        P(None, ("dp", "tensor")),
        P(None, "dp", "tensor"),
        P("tensor", "dp"),
        P("dp", "tensor"),
        P("tensor", "dp"),
    )
    fast = mesh.shape["dp"] == NZ * NX * NC and mesh.shape["tensor"] == NY
    return jax.shard_map(fast_shards if fast else shards, mesh=mesh, in_specs=in_specs, out_specs=out_specs, check_vma=False)
```

```python
import functools

import jax
import jax.numpy as jnp
from jax import lax
from jax.experimental import pallas as pl
from jax.experimental.pallas import tpu as pltpu
from jax.sharding import PartitionSpec as P

HEAD_DIM = 64
TSTEPS = 1000
LEN = 1024
BLOCK = 256
QBLK = 512


EPS = 1e-05
NEGATIVE = -1e30
HIGH = lax.Precision.HIGHEST
VMEM_LIMIT = 62 * 1024 * 1024


def layer_norm(hidden, gain, shift):
    average = jnp.mean(hidden, axis=-1, keepdims=True)
    centered = hidden - average
    variance = jnp.mean(centered * centered, axis=-1, keepdims=True)
    return centered * lax.rsqrt(variance + EPS) * gain + shift


def gather_rows(values):
    return lax.all_gather(values, "tensor", axis=0, tiled=True)


def sum_rows(values):
    return lax.psum_scatter(
        values.astype(jnp.bfloat16), "tensor", scatter_dimension=0, tiled=True
    ).astype(jnp.float32)


def fetch_attn(qkv_weight, out_weight):
    return (
        lax.all_gather(qkv_weight, "dp", axis=1, tiled=True),
        lax.all_gather(out_weight, "dp", axis=1, tiled=True),
    )


def fetch_mlp(up_weight, down_weight):
    return (
        lax.all_gather(up_weight, "dp", axis=0, tiled=True),
        lax.all_gather(down_weight, "dp", axis=1, tiled=True),
    )


def place_part(part, whole_len, offset):
    return lax.dynamic_update_slice_in_dim(jnp.zeros((whole_len,), jnp.float32), part, offset, 0)


def contract_rows(left, right):
    return lax.dot_general(
        left, right, (((0,), (0,)), ((), ())), preferred_element_type=jnp.float32
    )


def contract_cols(left, right):
    return lax.dot_general(
        left, right, (((1,), (1,)), ((), ())), preferred_element_type=jnp.float32
    )


def block_mask(start):
    query_pos = start + jnp.arange(QBLK)
    key_pos = jnp.arange(LEN)
    return query_pos[:, None] // BLOCK >= key_pos[None, :] // BLOCK


def split_heads(values):
    return values.reshape(values.shape[0], values.shape[1] // HEAD_DIM, HEAD_DIM)


def masked_scores(query_heads, key_heads, start, scale):
    scores = (
        jnp.einsum("qhd,khd->hqk", query_heads, key_heads, preferred_element_type=jnp.float32)
        * scale
    )
    return jnp.where(block_mask(start)[None], scores, NEGATIVE)


def block_slices(queries, keys_all, values_all, index):
    per_seq = LEN // QBLK
    seq_start = index // per_seq * LEN
    start = index % per_seq * QBLK
    query_blk = lax.dynamic_slice_in_dim(queries, seq_start + start, QBLK, 0)
    key_seq = lax.dynamic_slice_in_dim(keys_all, seq_start, LEN, 0)
    value_seq = lax.dynamic_slice_in_dim(values_all, seq_start, LEN, 0)
    return (seq_start, start, query_blk, key_seq, value_seq)


def run_attention(queries, keys_all, values_all, scale):
    total_rows = queries.shape[0]

    def run_advance(carry, index):
        seq_start, start, query_blk, key_seq, value_seq = block_slices(
            queries, keys_all, values_all, index
        )
        scores = masked_scores(split_heads(query_blk), split_heads(key_seq), start, scale)
        largest = jnp.max(scores, axis=-1, keepdims=True)
        expo = jnp.exp(scores - largest)
        totals = jnp.sum(expo, axis=-1, keepdims=True)
        chances = (expo / totals).astype(jnp.bfloat16)
        log_total = (largest + jnp.log(totals))[..., 0]
        mixed = jnp.einsum(
            "hqk,khd->qhd", chances, split_heads(value_seq), preferred_element_type=jnp.float32
        )
        return (carry, (mixed.reshape(QBLK, -1).astype(jnp.bfloat16), log_total))

    unused, (mixed, log_total) = lax.scan(run_advance, 0, jnp.arange(total_rows // QBLK))
    return (mixed.reshape(total_rows, -1), log_total)


def attention_back(queries, keys_all, values_all, grad_mixed, log_total, scale):
    total_rows = queries.shape[0]
    zeros = jnp.zeros(queries.shape, jnp.float32)

    def attention_advance(carry, inputs):
        grad_keys, grad_values = carry
        index, log_blk = inputs
        seq_start, start, query_blk, key_seq, value_seq = block_slices(
            queries, keys_all, values_all, index
        )
        grad_blk = lax.dynamic_slice_in_dim(grad_mixed, seq_start + start, QBLK, 0)
        query_heads = split_heads(query_blk)
        key_heads = split_heads(key_seq)
        grad_heads = split_heads(grad_blk)
        scores = masked_scores(query_heads, key_heads, start, scale)
        chances = jnp.exp(scores - log_blk[..., None])
        grad_probs = jnp.einsum(
            "qhd,khd->hqk", grad_heads, split_heads(value_seq), preferred_element_type=jnp.float32
        )
        inner = jnp.sum(chances * grad_probs, axis=-1, keepdims=True)
        grad_scores = (chances * (grad_probs - inner)).astype(jnp.bfloat16)
        grad_query = (
            jnp.einsum("hqk,khd->qhd", grad_scores, key_heads, preferred_element_type=jnp.float32)
            * scale
        )
        grad_key = (
            jnp.einsum("hqk,qhd->khd", grad_scores, query_heads, preferred_element_type=jnp.float32)
            * scale
        )
        grad_value = jnp.einsum(
            "hqk,qhd->khd",
            chances.astype(jnp.bfloat16),
            grad_heads,
            preferred_element_type=jnp.float32,
        )
        old_keys = lax.dynamic_slice_in_dim(grad_keys, seq_start, LEN, 0)
        old_values = lax.dynamic_slice_in_dim(grad_values, seq_start, LEN, 0)
        grad_keys = lax.dynamic_update_slice_in_dim(
            grad_keys, old_keys + grad_key.reshape(LEN, -1), seq_start, 0
        )
        grad_values = lax.dynamic_update_slice_in_dim(
            grad_values, old_values + grad_value.reshape(LEN, -1), seq_start, 0
        )
        return ((grad_keys, grad_values), grad_query.reshape(QBLK, -1))

    (grad_keys, grad_values), grad_queries = lax.scan(
        attention_advance, (zeros, zeros), (jnp.arange(total_rows // QBLK), log_total)
    )
    return (grad_queries.reshape(total_rows, -1), grad_keys, grad_values)


def shards(
    tokens,
    timesteps,
    norm_gains,
    biases,
    second_shift,
    hidden_bias,
    step_table,
    qkv_weight,
    out_weight,
    up_weight,
    down_weight,
    cotangent,
):
    width = tokens.shape[1]
    half_width = qkv_weight.shape[2]
    half_hidden = up_weight.shape[1]
    slot = lax.axis_index("tensor")
    device = lax.axis_index(("dp", "tensor"))
    scale = HEAD_DIM ** (-0.5)
    gains_all, biases_all, second_all, hidden_all, table_all = (
        lax.all_gather(norm_gains, ("dp", "tensor"), axis=1, tiled=True),
        lax.all_gather(biases, ("dp", "tensor"), axis=1, tiled=True),
        lax.all_gather(second_shift, ("dp", "tensor"), axis=0, tiled=True),
        lax.all_gather(hidden_bias, ("dp", "tensor"), axis=0, tiled=True),
        lax.all_gather(step_table, ("dp", "tensor"), axis=1, tiled=True),
    )
    gains_all = gains_all.astype(jnp.float32)
    biases_all = biases_all.astype(jnp.float32)
    second_all = second_all.astype(jnp.float32)
    hidden_local = lax.dynamic_slice_in_dim(
        hidden_all.astype(jnp.float32), slot * half_hidden, half_hidden, 0
    )
    query_bias = lax.dynamic_slice_in_dim(biases_all[1], slot * half_width, half_width, 0)
    value_bias = lax.dynamic_slice_in_dim(biases_all[2], slot * half_width, half_width, 0)
    step_id = lax.dynamic_slice_in_dim(timesteps, device, 1, 0)
    picker = (step_id[:, None] == jnp.arange(TSTEPS)[None, :]).astype(jnp.bfloat16)
    embed = jnp.dot(picker, table_all, preferred_element_type=jnp.float32)
    start_h = tokens.astype(jnp.float32) + embed
    qkv_full, out_full = fetch_attn(qkv_weight, out_weight)
    up_full, down_full = fetch_mlp(up_weight, down_weight)
    normed = gather_rows(layer_norm(start_h, gains_all[0], biases_all[0]).astype(jnp.bfloat16))
    projected = jnp.einsum("rd,jde->jre", normed, qkv_full, preferred_element_type=jnp.float32)
    queries = (projected[0] + query_bias).astype(jnp.bfloat16)
    keys_all = projected[1].astype(jnp.bfloat16)
    values_all = (projected[2] + value_bias).astype(jnp.bfloat16)
    mixed, log_total = run_attention(queries, keys_all, values_all, scale)
    attn_out = (
        sum_rows(jnp.dot(mixed, out_full, preferred_element_type=jnp.float32)) + biases_all[3]
    )
    middle = start_h + attn_out
    second = gather_rows(layer_norm(middle, gains_all[1], second_all).astype(jnp.bfloat16))
    pre_act = jnp.dot(second, up_full, preferred_element_type=jnp.float32) + hidden_local
    activated = jax.nn.gelu(pre_act).astype(jnp.bfloat16)
    mlp_out = (
        sum_rows(jnp.dot(activated, down_full, preferred_element_type=jnp.float32)) + biases_all[4]
    )
    layer_out = (middle + mlp_out).astype(jnp.bfloat16)
    grad_top = cotangent.astype(jnp.float32)
    up_full, down_full = fetch_mlp(up_weight, down_weight)
    grad_mlp_all = gather_rows(cotangent)
    grad_downw = contract_rows(activated, grad_mlp_all)
    grad_act = contract_cols(grad_mlp_all, down_full)
    unused, gelu_back = jax.vjp(jax.nn.gelu, pre_act)
    grad_pre = gelu_back(grad_act)[0].astype(jnp.bfloat16)
    grad_upw = contract_rows(second, grad_pre)
    grad_hidden_local = jnp.sum(grad_pre.astype(jnp.float32), axis=0)
    grad_second = sum_rows(contract_cols(grad_pre, up_full))
    unused, second_back = jax.vjp(layer_norm, middle, gains_all[1], second_all)
    grad_mid_part, grad_gain_two, grad_shift_two = second_back(grad_second)
    grad_middle = grad_top + grad_mid_part
    grad_up, grad_down = (
        lax.psum_scatter(grad_upw, "dp", scatter_dimension=0, tiled=True),
        lax.psum_scatter(grad_downw, "dp", scatter_dimension=1, tiled=True),
    )
    qkv_full, out_full = fetch_attn(qkv_weight, out_weight)
    grad_attn = grad_middle.astype(jnp.bfloat16)
    grad_attn_all = gather_rows(grad_attn)
    grad_outw = contract_rows(mixed, grad_attn_all)
    grad_mixed = contract_cols(grad_attn_all, out_full).astype(jnp.bfloat16)
    grad_queries, grad_keys, grad_values = attention_back(
        queries, keys_all, values_all, grad_mixed, log_total, scale
    )
    grad_rows = jnp.stack([grad_queries, grad_keys, grad_values]).astype(jnp.bfloat16)
    grad_qkvw = jnp.einsum("rd,jre->jde", normed, grad_rows, preferred_element_type=jnp.float32)
    grad_normed = sum_rows(
        jnp.einsum("jre,jde->rd", grad_rows, qkv_full, preferred_element_type=jnp.float32)
    )
    unused, first_back = jax.vjp(layer_norm, start_h, gains_all[0], biases_all[0])
    grad_start_part, grad_gain_one, grad_shift_one = first_back(grad_normed)
    grad_tokens = grad_middle + grad_start_part
    grad_qkv, grad_out = (
        lax.psum_scatter(grad_qkvw, "dp", scatter_dimension=1, tiled=True),
        lax.psum_scatter(grad_outw, "dp", scatter_dimension=1, tiled=True),
    )
    row_sums = jnp.sum(grad_rows.astype(jnp.float32), axis=1)
    gain_terms = jnp.stack([grad_gain_one, grad_gain_two])
    bias_terms = jnp.stack(
        [
            grad_shift_one,
            place_part(row_sums[0], width, slot * half_width),
            place_part(row_sums[2], width, slot * half_width),
            jnp.sum(grad_attn.astype(jnp.float32), axis=0),
            jnp.sum(grad_top, axis=0),
        ]
    )
    hidden_terms = place_part(
        grad_hidden_local,
        hidden_bias.shape[0] * lax.axis_size(("dp", "tensor")),
        slot * half_hidden,
    )
    seq_grad = jnp.sum(grad_tokens, axis=0, keepdims=True)
    table_terms = lax.dot_general(
        picker.astype(jnp.float32),
        seq_grad,
        (((0,), (0,)), ((), ())),
        precision=HIGH,
        preferred_element_type=jnp.float32,
    )
    grad_gains, grad_biases, grad_shift, grad_hidden, grad_table = (
        lax.psum_scatter(gain_terms, ("dp", "tensor"), scatter_dimension=1, tiled=True),
        lax.psum_scatter(bias_terms, ("dp", "tensor"), scatter_dimension=1, tiled=True),
        lax.psum_scatter(grad_shift_two, ("dp", "tensor"), scatter_dimension=0, tiled=True),
        lax.psum_scatter(hidden_terms, ("dp", "tensor"), scatter_dimension=0, tiled=True),
        lax.psum_scatter(table_terms, ("dp", "tensor"), scatter_dimension=1, tiled=True),
    )
    return (
        layer_out,
        grad_tokens,
        grad_gains,
        grad_biases,
        grad_shift,
        grad_hidden,
        grad_table,
        grad_qkv,
        grad_out,
        grad_up,
        grad_down,
    )


MESH_ID = pl.DeviceIdType.MESH
F32, BF16 = jnp.float32, jnp.bfloat16
NZ, NX, NC, NY = 4, 2, 2, 2
QB = 256
LINE = 40
GELU_A, GELU_B = 0.7978845608028654, 0.044715


def nt(left, right):
    return lax.dot_general(left, right, (((1,), (1,)), ((), ())), preferred_element_type=F32)


def nn(left, right):
    return lax.dot_general(left, right, (((1,), (0,)), ((), ())), preferred_element_type=F32)


def tn(left, right):
    return lax.dot_general(left, right, (((0,), (0,)), ((), ())), preferred_element_type=F32)


def position():
    dp = lax.axis_index("dp")
    return (lax.axis_index("tensor"), dp // (NX * NC), lax.rem(dp // NC, NX), lax.rem(dp, NC))


def device_at(y, z, x, c):
    return (z * (NX * NC) + x * NC + c, y)


def plane_peers(pos):
    y, z, x, c = pos
    for flip in range(1, NY * NX * NC):
        to = (1 - y if flip & 4 else y, z, 1 - x if flip & 2 else x, 1 - c if flip & 1 else c)
        yield flip - 1, to


def greet(pos):
    y, z, x, c = pos
    peers = [device_at(y, lax.rem(z + k, NZ), x, c) for k in range(1, NZ)]
    peers += [device_at(*to) for _, to in plane_peers(pos)]
    barrier = pltpu.get_barrier_semaphore()
    for peer in peers:
        pl.semaphore_signal(barrier, inc=1, device_id=peer, device_id_type=MESH_ID)
    return lambda: pl.semaphore_wait(barrier, len(peers))


def at_step(index, events):
    for step, names in events.items():

        @pl.when(index == step)
        def _():
            for name in names:
                name()


def remote(src, dst, send, recv, index, peer):
    return pltpu.make_async_remote_copy(
        src_ref=src,
        dst_ref=dst,
        send_sem=send.at[index],
        recv_sem=recv.at[index],
        device_id=peer,
        device_id_type=MESH_ID,
    )


class Gather:
    def __init__(self, buf, cols, send, recv, pos):
        self.buf, self.cols, self.send, self.recv, self.pos = buf, cols, send, recv, pos

    def view(self, y, z, x, c):
        return self.buf.at[y, z, x, c, :, self.cols]

    def steps(self, step):
        y, z, x, c = self.pos
        lo, hi, both = pl.ds(0, 2), pl.ds(2, 2), pl.ds(0, 2)
        if step == 0:
            return [
                (k - 1, (y, z, x, c), (y, lax.rem(z + NZ - k, NZ), x, c), device_at(y, lax.rem(z + k, NZ), x, c))
                for k in range(1, NZ)
            ]
        x_peer, y_peer = device_at(y, z, 1 - x, c), device_at(1 - y, z, x, c)
        if step == 1:
            return [(3, (y, lo, x, c), (y, lo, 1 - x, c), x_peer), (4, (y, hi, x, c), (1 - y, hi, x, c), y_peer)]
        if step == 2:
            return [
                (5, (y, lo, both, c), (1 - y, lo, both, c), y_peer),
                (6, (both, hi, x, c), (both, hi, 1 - x, c), x_peer),
            ]
        return [(7, (both, pl.ds(0, NZ), both, c), (both, pl.ds(0, NZ), both, 1 - c), device_at(y, z, x, 1 - c))]

    def start(self, step):
        for sem, src, _, peer in self.steps(step):
            remote(self.view(*src), self.view(*src), self.send, self.recv, sem, peer).start()

    def wait(self, step):
        for sem, _, dst, peer in self.steps(step):
            remote(self.view(*dst), self.view(*dst), self.send, self.recv, sem, peer).wait_recv()

    def next(self, step):
        self.wait(step)
        self.start(step + 1)

    count = 4

    def drain(self):
        for step in range(self.count):
            for sem, src, _, peer in self.steps(step):
                remote(self.view(*src), self.view(*src), self.send, self.recv, sem, peer).wait_send()


class SmallGather(Gather):
    count = 2

    def __init__(self, buf, send, recv, pos):
        super().__init__(buf, None, send, recv, pos)

    def view(self, y, z, x, c):
        return self.buf.at[y, z, x, c]

    def steps(self, step):
        y, z, x, c = self.pos
        if step == 0:
            return super().steps(0)
        every = pl.ds(0, NZ)
        return [
            (3 + flip, (y, every, x, c), (to[0], every, to[2], to[3]), device_at(*to)) for flip, to in plane_peers(self.pos)
        ]


class SmallScatter:
    def __init__(self, source, acc, first, last, send, recv, pos):
        self.source, self.acc, self.first, self.last = source, acc, first, last
        self.send, self.recv, self.pos = send, recv, pos

    def copies(self, step):
        y, z, x, c = self.pos
        every = pl.ds(0, NZ)
        if step == 0:
            return [
                remote(
                    self.source.at[to[0], every, to[2], to[3]],
                    self.first.at[flip],
                    self.send,
                    self.recv,
                    3 + flip,
                    device_at(*to),
                )
                for flip, to in plane_peers(self.pos)
            ]
        return [
            remote(
                self.acc.at[lax.rem(z + k, NZ)],
                self.last.at[k - 1],
                self.send,
                self.recv,
                k - 1,
                device_at(y, lax.rem(z + k, NZ), x, c),
            )
            for k in range(1, NZ)
        ]

    def start(self, step):
        for copy in self.copies(step):
            copy.start()

    def next(self):
        y, z, x, c = self.pos
        total = self.source[y, :, x, c]
        for flip, copy in enumerate(self.copies(0)):
            copy.wait_recv()
            total = total + self.first[flip]
        self.acc[...] = total
        self.start(1)

    def final(self):
        total = self.acc[self.pos[1]]
        for k, copy in enumerate(self.copies(1)):
            copy.wait_recv()
            total = total + self.last[k]
        return total

    def drain(self):
        for step in range(2):
            for copy in self.copies(step):
                copy.wait_send()


def small_scratch():
    tile = (8, 128)
    return [
        pltpu.VMEM((NY, NZ, NX, NC, *tile), F32),
        pltpu.VMEM((NZ, *tile), F32),
        pltpu.VMEM((NY * NX * NC - 1, NZ, *tile), F32),
        pltpu.VMEM((NZ - 1, *tile), F32),
    ]


def fold(values):
    return values[0:8] + pltpu.roll(values[8:16], LINE, 1) + pltpu.roll(values[16:24], 2 * LINE, 1)


def unfold(tile):
    return jnp.concatenate([tile, pltpu.roll(tile, 128 - LINE, 1), pltpu.roll(tile, 128 - 2 * LINE, 1)], axis=0)


def gelu_parts(v):
    square = v * v
    half = 0.5 + 0.5 * jnp.tanh(v * (GELU_A + (GELU_A * GELU_B) * square))
    act = v * half
    slope = half + (2.0 * act) * (1.0 - half) * (GELU_A + (3 * GELU_A * GELU_B) * square)
    return act, slope


def moments(hidden):
    average = jnp.mean(hidden, axis=-1, keepdims=True)
    centered = hidden - average
    variance = jnp.mean(centered * centered, axis=-1, keepdims=True)
    scale = lax.rsqrt(variance + EPS)
    return centered * scale, scale


def norm_back(xhat, scale, grad):
    return (grad - jnp.mean(grad, axis=-1, keepdims=True) - xhat * jnp.mean(grad * xhat, axis=-1, keepdims=True)) * scale


def row_block(index, size):
    return pl.ds(pl.multiple_of(index * size, size), size)


def sum_rows_of(values):
    return jnp.sum(values.astype(F32), axis=0, keepdims=True)


def blocks():
    for z in range(NZ):
        for x in range(NX):
            for c in range(NC):
                for y in range(NY):
                    yield (z * NX + x) * NC * NY + c * NY + y, (y, z, x, c)


class Scatter:
    def __init__(self, source, own, bufs, send, recv, pos, loaded):
        self.source, self.own, self.bufs = source, own, bufs
        self.send, self.recv, self.pos, self.loaded = send, recv, pos, loaded

    def copies(self, step):
        y, z, x, c = self.pos
        first, second_x, second_y, third_y, third_x, last = self.bufs
        own = self.own
        lo, hi, both = pl.ds(0, 2), pl.ds(2, 2), pl.ds(0, 2)
        x_peer, y_peer = device_at(y, z, 1 - x, c), device_at(1 - y, z, x, c)
        if step == 0:
            return [(0, self.source.at[both, pl.ds(0, NZ), both, 1 - c], first, device_at(y, z, x, 1 - c))]
        if step == 1:
            return [(1, own.at[both, lo, 1 - x], second_x, x_peer), (2, own.at[1 - y, hi, both], second_y, y_peer)]
        if step == 2:
            return [(3, own.at[1 - y, lo, x], third_y, y_peer), (4, own.at[y, hi, 1 - x], third_x, x_peer)]
        return [
            (4 + k, own.at[y, lax.rem(z + k, NZ), x], last.at[k - 1], device_at(y, lax.rem(z + k, NZ), x, c))
            for k in range(1, NZ)
        ]

    def start(self, step):
        for sem, src, dst, peer in self.copies(step):
            remote(src, dst, self.send, self.recv, sem, peer).start()

    def wait(self, step):
        for sem, src, dst, peer in self.copies(step):
            remote(src, dst, self.send, self.recv, sem, peer).wait_recv()

    def add(self, step):
        y, z, x, c = self.pos
        own, source = self.own, self.source
        first, second_x, second_y, third_y, third_x, last = self.bufs
        kind = own.dtype

        def plus(left, right):
            return (left.astype(F32) + right.astype(F32)).astype(kind)

        def each(count, body):
            def run(i, _):
                body(i)
                return 0

            lax.fori_loop(0, count, run, 0)

        if step == 0:

            def body(i):
                iy, iz, ix = i // (NZ * NX), lax.rem(i // NX, NZ), lax.rem(i, NX)
                mine = own[iy, iz, ix] if self.loaded else source[iy, iz, ix, c]
                own[iy, iz, ix] = plus(mine, first[iy, iz, ix])

            each(NY * NZ * NX, body)
        elif step == 1:

            def body(i):
                a, b = i // 2, lax.rem(i, 2)
                own[a, b, x] = plus(own[a, b, x], second_x[a, b])
                own[y, 2 + a, b] = plus(own[y, 2 + a, b], second_y[a, b])

            each(4, body)
        else:

            def body(i):
                own[y, i, x] = plus(own[y, i, x], third_y[i])
                own[y, 2 + i, x] = plus(own[y, 2 + i, x], third_x[i])

            each(2, body)

    def next(self, step):
        self.wait(step)
        self.add(step)
        if step == 0:
            self.sent(0)
        self.start(step + 1)

    def sent(self, step):
        for sem, src, dst, peer in self.copies(step):
            remote(src, dst, self.send, self.recv, sem, peer).wait_send()

    def final(self):
        y, z, x, c = self.pos
        last = self.bufs[5]
        self.wait(3)
        total = self.own[y, z, x].astype(F32)
        for k in range(NZ - 1):
            total = total + last[k].astype(F32)
        return total

    def drain(self):
        for step in range(1, 4):
            self.sent(step)


def scatter_scratch(per, width, kind):
    return [
        pltpu.VMEM((NY, NZ, NX, per, width), kind),
        pltpu.VMEM((2, 2, per, width), kind),
        pltpu.VMEM((2, 2, per, width), kind),
        pltpu.VMEM((2, per, width), kind),
        pltpu.VMEM((2, per, width), kind),
        pltpu.VMEM((NZ - 1, per, width), kind),
    ]


def layer_kernel(
    dims,
    steps,
    gains,
    biases,
    shift2,
    hidden,
    table_t,
    tokens_in,
    qkv_in,
    outw_t,
    upw_in,
    downw_t,
    cot_in,
    gup_out,
    gdown_out,
    gout_out,
    gqkv_out,
    gpack_out,
    gtok_out,
    layer_out,
    middle_hbm,
    grads_hbm,
    small_out,
    lse_out,
    ghid_out,
    full,
    pack,
    lines,
    stage,
    tokens,
    cot,
    normed,
    queries,
    keys_all,
    values_all,
    mixed,
    second,
    second_t,
    cot_t,
    result,
    gsec,
    act,
    gpre,
    gtile,
    hid,
    acc,
    inner,
    sums,
    *rest,
):
    rows, width, per, half, ffh, ft = dims
    pos = position()
    y, z, x, c = pos
    me = device_at(y, z, x, c)[0] * NY + y
    share = width // (NZ * NX * NC * NY)
    n_ff = ffh // ft
    send, recv, local = rest[-3:]

    n_groups = half // 128
    groups = [f"g{i}" for i in range(n_groups)]
    names = ["pack", "hid", *groups, "o"] + [f"m{i}" for i in range(n_ff)]
    col = {"o": pl.ds(3 * half, half)}
    for i in range(n_groups):
        col[f"g{i}"] = pl.ds(i * 384, 384)
    for i in range(n_ff):
        col[f"m{i}"] = pl.ds(4 * half + 2 * ft * i, 2 * ft)
    flow = {}
    for i, name in enumerate(names):
        if name in col:
            flow[name] = Gather(full, col[name], send.at[i], recv.at[i], pos)
        else:
            flow[name] = SmallGather({"pack": pack, "hid": lines}[name], send.at[i], recv.at[i], pos)
    ready = greet(pos)
    copies = {}

    def copy(name, src, dst):
        copies[name] = pltpu.make_async_copy(src, dst, local.at[len(copies)])
        copies[name].start()

    def own(start, size):
        return full.at[y, z, x, c, :, pl.ds(start, size)]

    parts = {"pack": [], "hid": []}
    for g in range(n_groups):
        parts[f"g{g}"] = [f"g{g}{i}" for i in range(3)]
        for i in range(3):
            copy(f"g{g}{i}", qkv_in.at[i, :, pl.ds(128 * g, 128)], own(384 * g + 128 * i, 128))
    copy("cot", cot_in, cot)
    copy("tokens", tokens_in, tokens)
    copy("o", outw_t, own(3 * half, half))
    parts["o"] = ["o"]
    for i in range(n_ff):
        copy(f"u{i}", upw_in.at[:, pl.ds(ft * i, ft)], own(4 * half + 2 * ft * i, ft))
        copy(f"d{i}", downw_t.at[:, pl.ds(ft * i, ft)], own(4 * half + 2 * ft * i + ft, ft))
        parts[f"m{i}"] = [f"u{i}", f"d{i}"]

    def launch(name):
        for key in parts[name]:
            copies[key].wait()
        flow[name].start(0)

    stage[...] = jnp.zeros_like(stage)
    stage[0:2, 0:share] = gains[...].astype(F32)
    stage[2:7, 0:share] = biases[...].astype(F32)
    stage[7:8, 0:share] = shift2[...].astype(F32)
    n_steps, n_seq = table_t.shape[1], steps.shape[1]
    wanted = jnp.concatenate([steps[...], jnp.full((1, 128 - n_seq), -1, jnp.int32)], axis=1)
    picked = (wanted == lax.broadcasted_iota(jnp.int32, (n_steps, 128), 0)).astype(BF16)
    pack[y, z, x, c] = fold(stage[...].T[0:share] + pltpu.roll(nn(table_t[...], picked), 8, 1))
    hshare = hidden.shape[1]
    lane = lax.broadcasted_iota(jnp.int32, (hshare, NC * NY * hshare), 0) + hshare * (c * NY + y)
    place = (lane == lax.broadcasted_iota(jnp.int32, (hshare, NC * NY * hshare), 1)).astype(BF16)
    spread = nn(jnp.broadcast_to(hidden[...], (8, hshare)), place)
    n_hid = NC * NY * hshare // 128
    pieces = [spread[0:1, 128 * j : 128 * j + 128] for j in range(n_hid)]
    lines[y, z, x, c] = jnp.concatenate([*pieces, jnp.zeros((8 - n_hid, 128), F32)], axis=0)

    ready()
    launch("pack")
    launch("g0")
    copies["cot"].wait()

    def turn_cot(i, total):
        rb = row_block(i, 256)
        block = cot[rb, :]
        cot_t[:, rb] = block.T
        return total + sum_rows_of(block)

    csum = lax.fori_loop(0, rows // 256, turn_cot, jnp.zeros((1, width), F32))
    sums[...] = jnp.zeros_like(sums)
    sums[6:7, :] = csum
    flow["pack"].next(0)
    flow["g0"].next(0)
    launch("g1")
    flow["g0"].next(1)
    flow["pack"].wait(1)
    flow["g1"].next(0)
    launch("g2")
    launch("hid")
    launch("o")

    for d, (by, bz, bx, bc) in blocks():
        result[d * share : d * share + share, 0:128] = unfold(pack[by, bz, bx, bc])
    small_out[...] = result[0:width, 0:128].T
    embed = small_out[pl.ds(8 + me, 1), :]
    copies["tokens"].wait()

    def first_norm(i, _):
        rb = row_block(i, 128)
        xhat, _ = moments(tokens[rb, :].astype(F32) + embed)
        normed[rb, :] = (xhat * small_out[0:1, :] + small_out[2:3, :]).astype(BF16)
        return 0

    lax.fori_loop(0, rows // 128, first_norm, 0)
    flow["g0"].next(2)
    flow["g1"].next(1)
    flow["g2"].next(0)
    launch("m0")

    def whole(cols, size):
        return jnp.concatenate([full[by, :, :, :, :, cols].reshape(width, size) for by in range(NY)], axis=1)

    def project(group):
        cols = pl.ds(pl.multiple_of(group * 384, 128), 384)

        def body(i, _):
            rb = row_block(i, 512)
            value = nn(normed[rb, :], whole(cols, 384))
            for by in range(NY):
                to = pl.ds(pl.multiple_of((by * n_groups + group) * 128, 128), 128)
                piece = [value[:, by * 384 + 128 * j : by * 384 + 128 * j + 128] for j in range(3)]
                queries[rb, to] = (piece[0] + small_out[3:4, to]).astype(BF16) * jnp.asarray(HEAD_DIM**-0.5, BF16)
                keys_all[rb, to] = piece[1].astype(BF16)
                values_all[rb, to] = (piece[2] + small_out[4:5, to]).astype(BF16)
            return 0

        lax.fori_loop(0, rows // 512, body, 0)

    def then(name, step):
        return lambda: flow[name].next(step)

    def back(name, step):
        return lambda: sums_of[name].next(step)

    def arrived(name):
        return lambda: flow[name].wait(3)

    def off(name):
        return lambda: launch(name)

    events = {
        1: [then("g1", 2), then("g2", 1), then("o", 0), then("hid", 0)],
        3: [then("g2", 2), then("o", 1)],
        4: [then("m0", 1)],
        5: [then("o", 2), then("m1", 0), off("m2")],
    }
    between = {1: [then("m0", 0), off("m1")]}

    def attend(s, _):
        group, by = s // NY, lax.rem(s, NY)
        p = by * n_groups + group

        @pl.when(by == 0)
        def _():
            at_step(group, {g: [arrived(f"g{g}")] for g in range(n_groups)})
            project(group)
            at_step(group, between)

        at_step(s, events)
        cols = pl.ds(pl.multiple_of(p * 128, 128), 128)
        low = lax.broadcasted_iota(jnp.int32, (QB, 128), 1) < HEAD_DIM
        for i in range(rows // QB):
            n = (i + 1) * QB
            rb = slice(i * QB, n)
            key, value, query = keys_all[0:n, cols], values_all[0:n, cols], queries[rb, cols]
            outs, scales = [], []
            for h in range(2):
                scores = nt(key, jnp.where(low == (h == 0), query, jnp.zeros_like(query)))
                top = jnp.max(scores, axis=0, keepdims=True)
                expo = jnp.exp(scores - top)
                total = jnp.sum(expo, axis=0, keepdims=True)
                lse_out[pl.ds(2 * p + h, 1), rb] = top + jnp.log(total)
                scales.append(jnp.broadcast_to(1.0 / total, (HEAD_DIM, QB)))
                outs.append(tn(expo.astype(BF16), value))
            scale = jnp.concatenate(scales, axis=0).T
            mixed[rb, cols] = (jnp.where(low, outs[0], outs[1]) * scale).astype(BF16)
        return 0

    lax.fori_loop(0, width // 128, attend, 0)
    flow["o"].wait(3)
    flow["hid"].wait(1)
    for bz in range(NZ):
        for bx in range(NX):
            total = lines[0, bz, bx, 0] + lines[0, bz, bx, 1] + lines[1, bz, bx, 0] + lines[1, bz, bx, 1]
            for j in range(n_hid):
                at = ((bz * NX + bx) * n_hid + j) * 128
                hid[0:1, at : at + 128] = total[j : j + 1]

    def second_norm(i, _):
        at_step(i, {2: [then("m0", 2)]})
        rb = row_block(i, 256)
        start_h = tokens[rb, :].astype(F32) + embed
        value = start_h + (nt(mixed[rb, :], whole(col["o"], half)) + small_out[5:6, :])
        result[rb, :] = value
        gsec[rb, :] = jnp.zeros_like(value)
        xhat, _ = moments(value)
        block = (xhat * small_out[1:2, :] + small_out[7:8, :]).astype(BF16)
        second[rb, :] = block
        second_t[:, rb] = block.T
        return 0

    lax.fori_loop(0, rows // 256, second_norm, 0)
    copy("middle", result, middle_hbm)
    flow["m1"].next(1)
    flow["m0"].wait(3)
    copies["middle"].wait()
    at = len(copies)

    free = 4 * half
    half_f = 2 * ft
    places = {"m0": (0, free, half_f), "m1": (1, free, half_f), "m2": (0, free + half_f, half_f), "o": (1, free + half_f, half)}
    for g in range(n_groups):
        places[f"q{g}"] = (g % 2, free + 2 * half_f + 384 * (g // 2), 384)
    sums_of = {}
    for i, name in enumerate([*places, "pack", "hid"]):
        sems = (send.at[len(names) + i], recv.at[len(names) + i], pos)
        if name in places:
            core, start, size = places[name]
            own_view = full.at[:, :, :, core, :, pl.ds(start, size)]
            bufs = rest[6 * i : 6 * i + 6]
            if name[0] == "m":
                source = grads_hbm.at[:, :, :, :, :, pl.ds(half_f * i, half_f)]
            else:
                source = gtile.at[:, :, :, :, :, pl.ds(0 if name in ("o", "q1") else half, 384)]
            sums_of[name] = Scatter(source, own_view, bufs, *sems, name[0] == "m")
        else:
            sums_of[name] = SmallScatter(*(rest[-11:-7] if name == "pack" else rest[-7:-3]), *sems)
    loads = {
        name: pltpu.make_async_copy(sums_of[name].source.at[:, :, :, c], sums_of[name].own, local.at[at + 2 + i])
        for i, name in enumerate(["m0", "m1", "m2"])
    }

    def tile_copy(t, slot):
        ty, tm = lax.rem(t, NY), t // NY
        return pltpu.make_async_copy(
            gtile.at[slot],
            grads_hbm.at[ty, :, :, :, :, pl.ds(pl.multiple_of(tm * 2 * ft, 128), 2 * ft)],
            local.at[at + slot],
        )

    tiles = NY * n_ff

    def tile(t, _):
        ty, tm = lax.rem(t, NY), t // NY
        slot = lax.rem(t, 2)

        def begin(name):
            loads[name].start()
            sums_of[name].start(0)

        def first_sum(name):
            loads[name].wait()
            sums_of[name].next(0)

        def reuse():
            tile_copy(t - 2, slot).wait()

        def reuse_both():
            tile_copy(t - 2, slot).wait()
            tile_copy(t - 1, 1 - slot).wait()

        at_step(
            t,
            {
                1: [then("m2", 0)],
                2: [flow["m0"].drain, reuse_both, lambda: begin("m0"), then("m2", 1), arrived("m1")],
                3: [lambda: first_sum("m0")],
                4: [reuse_both, lambda: begin("m1"), arrived("m2")],
                5: [back("m0", 1), lambda: first_sum("m1")],
            },
        )

        up_at = pl.ds(pl.multiple_of(4 * half + tm * 2 * ft, 128), ft)
        down_at = pl.ds(pl.multiple_of(4 * half + tm * 2 * ft + ft, 128), ft)
        hid_at = pl.ds(pl.multiple_of(ty * ffh + tm * ft, 128), ft)

        def up():
            return full[ty, :, :, :, :, up_at].reshape(width, ft)

        def down():
            return full[ty, :, :, :, :, down_at].reshape(width, ft)

        pre = nn(second[...], up()) + hid[:, hid_at]
        gact = nn(cot[...], down())
        value, slope = gelu_parts(pre)
        act[...] = value.astype(BF16)
        grad = (gact * slope).astype(BF16)
        gpre[...] = grad
        ghid_out[:, hid_at] = sum_rows_of(grad)
        result[...] += nt(act[...], down())
        gsec[...] += nt(gpre[...], up())

        def results():
            second[...] = (result[...] + small_out[6:7, :]).astype(BF16)
            layer_save.start()
            middle_load.start()

        at_step(t, {1: [then("m1", 2)], 3: [then("m2", 2)], tiles - 1: [results]})

        turn = (NZ, NX, NC, per, ft)
        gtile[slot, :, :, :, :, 0:ft] = nn(second_t[...], gpre[...]).astype(BF16).reshape(turn)
        gtile[slot, :, :, :, :, ft : 2 * ft] = nn(cot_t[...], act[...]).astype(BF16).reshape(turn)
        tile_copy(t, slot).start()
        return 0

    layer_save = pltpu.make_async_copy(second, layer_out, local.at[at + 5])
    middle_load = pltpu.make_async_copy(middle_hbm, result, local.at[at + 6])
    lax.fori_loop(0, tiles, tile, 0)
    flow["m1"].drain()
    flow["m2"].drain()
    tile_copy(tiles - 2, 0).wait()
    tile_copy(tiles - 1, 1).wait()
    loads["m2"].start()
    sums_of["m2"].start(0)
    reload = [
        pltpu.make_async_copy(tokens_in.at[:, pl.ds(0, ft)], act, local.at[at + 7]),
        pltpu.make_async_copy(tokens_in.at[:, pl.ds(ft, width - ft)], gpre.at[:, pl.ds(0, width - ft)], local.at[at + 8]),
    ]
    for load in reload:
        load.start()
    for d, (by, bz, bx, bc) in blocks():
        start = (bz * NX + bx) * n_hid
        pieces = [ghid_out[:, 128 * (start + j) : 128 * (start + j + 1)] for j in range(n_hid)]
        sums_of["hid"].source[by, bz, bx, bc] = jnp.concatenate([*pieces, jnp.zeros((8 - n_hid, 128), F32)], axis=0)
    sums_of["hid"].start(0)
    layer_save.wait()
    middle_load.wait()
    gattn, gattn_t, normed_t, gmixed = second, cot_t, second_t, tokens
    gq, gk, gv = second, normed, cot
    def second_back(i, totals):
        rb = row_block(i, 128)
        xhat, scale = moments(result[rb, :])
        grad = gsec[rb, :]
        total = cot[rb, :].astype(F32) + norm_back(xhat, scale, grad * small_out[1:2, :])
        gsec[rb, :] = total
        low = total.astype(BF16)
        gattn[rb, :] = low
        gattn_t[:, rb] = low.T
        return (
            totals[0] + sum_rows_of(grad * xhat),
            totals[1] + sum_rows_of(grad),
            totals[2] + sum_rows_of(low),
        )

    zero = jnp.zeros((1, width), F32)
    ggain2, gshift2, gattn_sum = lax.fori_loop(0, rows // 128, second_back, (zero, zero, zero))
    sums[1:2, :] = ggain2
    sums[5:6, :] = gattn_sum
    sums[7:8, :] = gshift2

    def weight(index):
        picks = [
            full[by, :, :, :, :, pl.ds(384 * g + 128 * index, 128)].reshape(width, 128)
            for by in range(NY)
            for g in range(n_groups)
        ]
        return jnp.concatenate(picks, axis=1)

    for by in range(NY):
        def out_grad(i, _):
            rb = row_block(i, 384)
            part = nn(gattn_t[rb, :], mixed[:, by * half : by * half + half]).astype(BF16)
            gtile[by, pl.ds(i * 2, 2), :, :, :, 0:half] = part.reshape(2, NX, NC, per, half)
            return 0

        lax.fori_loop(0, width // 384, out_grad, 0)
    sums_of["o"].start(0)
    loads["m2"].wait()
    sums_of["m2"].next(0)
    sums_of["m0"].next(2)

    def mixed_grad(i, _):
        rb = row_block(i, 512)
        gmixed[rb, :] = nn(gattn[rb, :], whole(col["o"], half)).astype(BF16)
        return 0

    lax.fori_loop(0, rows // 512, mixed_grad, 0)
    sums_of["m1"].next(1)
    sums_of["o"].next(0)

    def turn_normed(i, _):
        rb = row_block(i, 256)
        normed_t[:, rb] = normed[rb, :].T
        return 0

    lax.fori_loop(0, rows // 256, turn_normed, 0)
    events_back = {
        2: [back("m1", 2)],
        3: [back("q0", 0), back("m2", 1)],
        4: [back("o", 1), back("m2", 2), sums_of["hid"].next],
        5: [back("q1", 0), back("q0", 1)],
    }

    def attend_back(s, _):
        group, by = s // NY, lax.rem(s, NY)
        p = by * n_groups + group
        at_step(s, events_back)
        cols = pl.ds(pl.multiple_of(p * 128, 128), 128)
        dots = (gmixed[:, cols].astype(F32) * mixed[:, cols].astype(F32)).T
        for h in range(2):
            inner[h : h + 1, :] = jnp.sum(dots[HEAD_DIM * h : HEAD_DIM * (h + 1)], axis=0, keepdims=True)
        for j in range(rows // QB):
            kb, first = slice(j * QB, (j + 1) * QB), j * QB
            later = rows - first
            key, value = keys_all[kb, cols], values_all[kb, cols]
            low = lax.broadcasted_iota(jnp.int32, (later, 128), 1) < HEAD_DIM

            def two(block):
                none = jnp.zeros_like(block)
                return jnp.concatenate([jnp.where(low, block, none), jnp.where(low, none, block)], axis=0)

            query, grad = two(queries[first:rows, cols]), two(gmixed[first:rows, cols])
            logs = jnp.concatenate([lse_out[pl.ds(2 * p + h, 1), first:rows] for h in range(2)], axis=1)
            inners = jnp.concatenate([inner[h : h + 1, first:rows] for h in range(2)], axis=1)
            probs = jnp.exp(nt(key, query) - logs)
            gscores = (probs * (nt(value, grad) - inners)).astype(BF16)
            gv[kb, cols] = nn(probs.astype(BF16), grad).astype(BF16)
            gk[kb, cols] = nn(gscores, query).astype(BF16)
            both = tn(gscores, key)
            more = jnp.where(low, both[:later], both[later:])
            if j == 0:
                acc[...] = more
            else:
                acc[first:rows] += more
        gq[:, cols] = (acc[...] * HEAD_DIM**-0.5).astype(BF16)

        @pl.when(by == NY - 1)
        def _():
            offset = lax.rem(group + 1, 2) * half
            for piece, source in enumerate((gq, gk, gv)):
                pick = jnp.concatenate(
                    [source[:, pl.ds(pl.multiple_of((b * n_groups + group) * 128, 128), 128)] for b in range(NY)], axis=1
                )
                part = nn(normed_t[...], pick).astype(BF16)
                for b in range(NY):
                    to = pl.ds(pl.multiple_of(offset + piece * 128, 128), 128)
                    gtile[b, :, :, :, :, to] = part[:, b * 128 : b * 128 + 128].reshape(NZ, NX, NC, per, 128)
            at_step(group, {g: [lambda g=g: sums_of[f"q{g}"].start(0)] for g in range(n_groups)})

        return 0

    lax.fori_loop(0, NY * n_groups, attend_back, 0)
    sums_of["o"].next(2)
    for load in reload:
        load.wait()

    def first_back(i, totals):
        rb = row_block(i, 256)
        block = jnp.concatenate([act[rb, :], gpre[rb, 0 : width - ft]], axis=1)
        xhat, scale = moments(block.astype(F32) + embed)
        q_rows, k_rows, v_rows = gq[rb, :], gk[rb, :], gv[rb, :]
        grad = nt(q_rows, weight(0)) + nt(k_rows, weight(1)) + nt(v_rows, weight(2))
        total = gsec[rb, :] + norm_back(xhat, scale, grad * small_out[0:1, :])
        result[rb, :] = total

        at_step(
            i,
            {0: [back("q0", 2)], 1: [back("q1", 1), back("q2", 0)], 2: [back("q1", 2)], 3: [back("q2", 1)]},
        )
        return (
            totals[0] + sum_rows_of(grad * xhat),
            totals[1] + sum_rows_of(grad),
            totals[2] + sum_rows_of(q_rows),
            totals[3] + sum_rows_of(v_rows),
            totals[4] + sum_rows_of(total),
        )

    ggain1, gshift1, q_sum, v_sum, seq_sum = lax.fori_loop(0, rows // 256, first_back, (zero,) * 5)
    sums[0:1, :] = ggain1
    sums[2:3, :] = gshift1
    sums[3:4, :] = q_sum
    sums[4:5, :] = v_sum
    sums[pl.ds(8 + me, 1), :] = seq_sum
    gtok = pltpu.make_async_copy(result, gtok_out, local.at[at + 9])
    gtok.start()
    turned = sums[...].T
    for d, (by, bz, bx, bc) in blocks():
        sums_of["pack"].source[by, bz, bx, bc] = fold(turned[d * share : d * share + share])
    sums_of["pack"].start(0)
    sums_of["q2"].next(2)
    for i in range(n_ff):
        total = sums_of[f"m{i}"].final()
        gup_out[:, ft * i : ft * i + ft] = total[:, 0:ft]
        gdown_out[:, ft * i : ft * i + ft] = total[:, ft:]
    sums_of["pack"].next()
    gout_out[...] = sums_of["o"].final()
    gpack_out[8:16] = sums_of["hid"].final()
    for g in range(n_groups):
        total = sums_of[f"q{g}"].final()
        for piece in range(3):
            gqkv_out[piece, :, 128 * g : 128 * g + 128] = total[:, 128 * piece : 128 * piece + 128]
    gpack_out[0:8] = sums_of["pack"].final()
    gtok.wait()
    for name in ["pack", "hid", *groups, "o"]:
        flow[name].drain()
    for each in sums_of.values():
        each.drain()


def finish_kernel(slots, count, steps, gpack, *refs):
    large, (gains_out, biases_out, shift_out, hidden_out, table_out) = refs[:count], refs[count : count + 5]
    outs, bufs, (load_sem, save_sem) = refs[count + 5 : 2 * count + 5], refs[2 * count + 5 : 3 * count + 5], refs[-2:]
    pieces = []
    for src, buf, out in zip(large, bufs, outs):
        cut = 4 if src.shape[0] % 512 == 0 else 1
        size = src.shape[0] // cut
        for k in range(cut):
            at, n = pl.ds(k * size, size), len(pieces)
            pieces.append(
                (
                    pltpu.make_async_copy(src.at[at], buf.at[at], load_sem.at[n]),
                    pltpu.make_async_copy(buf.at[at], out.at[at], save_sem.at[n]),
                )
            )
    for load, _ in pieces:
        load.start()
    share, hshare = gains_out.shape[1], hidden_out.shape[1]
    features = unfold(gpack[0:8, :])
    turned = jnp.concatenate([features, jnp.zeros((128 - share, 128), F32)], axis=0).T
    gains_out[...] = turned[0:2, 0:share]
    biases_out[...] = turned[2:7, 0:share]
    shift_out[...] = turned[7:8, 0:share]
    slot = lax.rem(lax.axis_index("dp"), NC) * NY + lax.axis_index("tensor")
    line = jnp.concatenate([gpack[8 + j : 9 + j, :] for j in range(slots * hshare // 128)], axis=1)
    value = line[:, 0:hshare]
    for k in range(1, slots):
        value = jnp.where(slot == k, line[:, hshare * k : hshare * k + hshare], value)
    hidden_out[...] = value
    n_steps, n_seq = table_out.shape[1], steps.shape[1]
    picked = (steps[...] == lax.broadcasted_iota(jnp.int32, (n_steps, n_seq), 0)).astype(F32)
    table_out[...] = lax.dot_general(
        features[:, 8 : 8 + n_seq], picked, (((1,), (1,)), ((), ())), precision=HIGH, preferred_element_type=F32
    )
    for load, save in pieces:
        load.wait()
        save.start()
    for _, save in pieces:
        save.wait()


def fast_shards(
    tokens,
    timesteps,
    norm_gains,
    biases,
    second_shift,
    hidden_bias,
    step_table,
    qkv_weight,
    out_weight,
    up_weight,
    down_weight,
    cotangent,
):
    rows, width = tokens.shape
    _, per, half = qkv_weight.shape
    ffh = up_weight.shape[1]
    ft = 512
    dims = (rows, width, per, half, ffh, ft)
    n_ff, n_groups = ffh // ft, half // 128
    total = 4 * half + 2 * ffh
    vmem, anywhere = pl.BlockSpec(memory_space=pltpu.VMEM), pl.BlockSpec(memory_space=pl.ANY)
    shape = jax.ShapeDtypeStruct
    low, wide = shape((rows, width), BF16), shape((rows, width), F32)
    vm = pltpu.VMEM
    hshare = hidden_bias.shape[0]
    steps = timesteps.reshape(1, -1)
    chunks = [2 * ft] * n_ff + [half] * (1 + n_groups)
    scratch = []
    for cols in chunks:
        scratch += scatter_scratch(per, cols, BF16)
    n_flows = 3 + n_groups + n_ff + len(chunks) + 2
    gup, gdown, gout, gqkv, gpack, gtok, layer, _, _ = pl.pallas_call(
        functools.partial(layer_kernel, dims),
        in_specs=[vmem] * 6 + [anywhere] * 6,
        out_specs=[vmem] * 5 + [anywhere] * 4,
        out_shape=[
            shape((per, ffh), F32),
            shape((per, ffh), F32),
            shape((per, half), F32),
            shape((3, per, half), F32),
            shape((16, 128), F32),
            wide,
            low,
            wide,
            shape((NY, NZ, NX, NC, per, 2 * ffh), BF16),
        ],
        scratch_shapes=[
            vm((128, width), F32),
            vm((16, rows), F32),
            vm((1, NY * ffh), F32),
            vm((NY, NZ, NX, NC, per, total), BF16),
            vm((NY, NZ, NX, NC, 8, 128), F32),
            vm((NY, NZ, NX, NC, 8, 128), F32),
            vm((128, 128), F32),
            vm((rows, width), BF16),
            vm((rows, width), BF16),
            vm((rows, width), BF16),
            vm((rows, width), BF16),
            vm((rows, width), BF16),
            vm((rows, width), BF16),
            vm((rows, width), BF16),
            vm((rows, width), BF16),
            vm((width, rows), BF16),
            vm((width, rows), BF16),
            vm((rows, width), F32),
            vm((rows, width), F32),
            vm((rows, ft), BF16),
            vm((rows, ft), BF16),
            vm((2, NZ, NX, NC, per, 2 * ft), BF16),
            vm((1, NY * ffh), F32),
            vm((rows, 128), F32),
            vm((8, rows), F32),
            vm((128, width), F32),
            *scratch,
            *small_scratch(),
            *small_scratch(),
            pltpu.SemaphoreType.DMA((n_flows, 10)),
            pltpu.SemaphoreType.DMA((n_flows, 10)),
            pltpu.SemaphoreType.DMA((14 + 3 * n_groups + 2 * n_ff,)),
        ],
        compiler_params=pltpu.CompilerParams(collective_id=0, has_side_effects=True, vmem_limit_bytes=VMEM_LIMIT),
        name="layer",
    )(
        steps,
        norm_gains,
        biases,
        second_shift.reshape(1, -1),
        hidden_bias.reshape(1, -1),
        step_table.T,
        tokens,
        qkv_weight,
        out_weight.T,
        up_weight,
        down_weight.T,
        cotangent,
    )
    share, n_steps = norm_gains.shape[1], step_table.shape[0]
    large = (gtok, layer, gqkv, gout, gup, gdown)
    pieces = sum(4 if array.shape[0] % 512 == 0 else 1 for array in large)
    small_shapes = [(2, share), (5, share), (1, share), (1, hshare), (share, n_steps)]
    large_shapes = [shape(array.shape, array.dtype) for array in large]
    grad_gains, grad_biases, grad_shift, grad_hidden, grad_table, gtok, layer, gqkv, gout, gup, gdown = pl.pallas_call(
        functools.partial(finish_kernel, NC * NY, len(large)),
        in_specs=[vmem] * 2 + [anywhere] * len(large),
        out_specs=[vmem] * 5 + [anywhere] * len(large),
        out_shape=[shape(dims, F32) for dims in small_shapes] + large_shapes,
        scratch_shapes=[vm(array.shape, array.dtype) for array in large] + [pltpu.SemaphoreType.DMA((pieces,))] * 2,
        name="finish",
    )(steps, gpack, *large)
    return (
        layer,
        gtok,
        grad_gains,
        grad_biases,
        grad_shift.reshape(share),
        grad_hidden.reshape(hshare),
        grad_table.T,
        gqkv,
        gout.T,
        gup,
        gdown.T,
    )


def solution(mesh):
    in_specs = (
        P(("dp", "tensor"), None),
        P(),
        P(None, ("dp", "tensor")),
        P(None, ("dp", "tensor")),
        P(("dp", "tensor")),
        P(("dp", "tensor")),
        P(None, ("dp", "tensor")),
        P(None, "dp", "tensor"),
        P("tensor", "dp"),
        P("dp", "tensor"),
        P("tensor", "dp"),
        P(("dp", "tensor"), None),
    )
    out_specs = (
        P(("dp", "tensor"), None),
        P(("dp", "tensor"), None),
        P(None, ("dp", "tensor")),
        P(None, ("dp", "tensor")),
        P(("dp", "tensor")),
        P(("dp", "tensor")),
        P(None, ("dp", "tensor")),
        P(None, "dp", "tensor"),
        P("tensor", "dp"),
        P("dp", "tensor"),
        P("tensor", "dp"),
    )
    fast = mesh.shape["dp"] == NZ * NX * NC and mesh.shape["tensor"] == NY
    return jax.shard_map(fast_shards if fast else shards, mesh=mesh, in_specs=in_specs, out_specs=out_specs, check_vma=False)
```

```python
import functools

import jax
import jax.numpy as jnp
from jax import lax
from jax.experimental import pallas as pl
from jax.experimental.pallas import tpu as pltpu
from jax.sharding import PartitionSpec as P

HEAD_DIM = 64
TSTEPS = 1000
LEN = 1024
BLOCK = 256
QBLK = 512


EPS = 1e-05
NEGATIVE = -1e30
HIGH = lax.Precision.HIGHEST
VMEM_LIMIT = 62 * 1024 * 1024


def layer_norm(hidden, gain, shift):
    average = jnp.mean(hidden, axis=-1, keepdims=True)
    centered = hidden - average
    variance = jnp.mean(centered * centered, axis=-1, keepdims=True)
    return centered * lax.rsqrt(variance + EPS) * gain + shift


def gather_rows(values):
    return lax.all_gather(values, "tensor", axis=0, tiled=True)


def sum_rows(values):
    return lax.psum_scatter(
        values.astype(jnp.bfloat16), "tensor", scatter_dimension=0, tiled=True
    ).astype(jnp.float32)


def fetch_attn(qkv_weight, out_weight):
    return (
        lax.all_gather(qkv_weight, "dp", axis=1, tiled=True),
        lax.all_gather(out_weight, "dp", axis=1, tiled=True),
    )


def fetch_mlp(up_weight, down_weight):
    return (
        lax.all_gather(up_weight, "dp", axis=0, tiled=True),
        lax.all_gather(down_weight, "dp", axis=1, tiled=True),
    )


def place_part(part, whole_len, offset):
    return lax.dynamic_update_slice_in_dim(jnp.zeros((whole_len,), jnp.float32), part, offset, 0)


def contract_rows(left, right):
    return lax.dot_general(
        left, right, (((0,), (0,)), ((), ())), preferred_element_type=jnp.float32
    )


def contract_cols(left, right):
    return lax.dot_general(
        left, right, (((1,), (1,)), ((), ())), preferred_element_type=jnp.float32
    )


def block_mask(start):
    query_pos = start + jnp.arange(QBLK)
    key_pos = jnp.arange(LEN)
    return query_pos[:, None] // BLOCK >= key_pos[None, :] // BLOCK


def split_heads(values):
    return values.reshape(values.shape[0], values.shape[1] // HEAD_DIM, HEAD_DIM)


def masked_scores(query_heads, key_heads, start, scale):
    scores = (
        jnp.einsum("qhd,khd->hqk", query_heads, key_heads, preferred_element_type=jnp.float32)
        * scale
    )
    return jnp.where(block_mask(start)[None], scores, NEGATIVE)


def block_slices(queries, keys_all, values_all, index):
    per_seq = LEN // QBLK
    seq_start = index // per_seq * LEN
    start = index % per_seq * QBLK
    query_blk = lax.dynamic_slice_in_dim(queries, seq_start + start, QBLK, 0)
    key_seq = lax.dynamic_slice_in_dim(keys_all, seq_start, LEN, 0)
    value_seq = lax.dynamic_slice_in_dim(values_all, seq_start, LEN, 0)
    return (seq_start, start, query_blk, key_seq, value_seq)


def run_attention(queries, keys_all, values_all, scale):
    total_rows = queries.shape[0]

    def run_advance(carry, index):
        seq_start, start, query_blk, key_seq, value_seq = block_slices(
            queries, keys_all, values_all, index
        )
        scores = masked_scores(split_heads(query_blk), split_heads(key_seq), start, scale)
        largest = jnp.max(scores, axis=-1, keepdims=True)
        expo = jnp.exp(scores - largest)
        totals = jnp.sum(expo, axis=-1, keepdims=True)
        chances = (expo / totals).astype(jnp.bfloat16)
        log_total = (largest + jnp.log(totals))[..., 0]
        mixed = jnp.einsum(
            "hqk,khd->qhd", chances, split_heads(value_seq), preferred_element_type=jnp.float32
        )
        return (carry, (mixed.reshape(QBLK, -1).astype(jnp.bfloat16), log_total))

    unused, (mixed, log_total) = lax.scan(run_advance, 0, jnp.arange(total_rows // QBLK))
    return (mixed.reshape(total_rows, -1), log_total)


def attention_back(queries, keys_all, values_all, grad_mixed, log_total, scale):
    total_rows = queries.shape[0]
    zeros = jnp.zeros(queries.shape, jnp.float32)

    def attention_advance(carry, inputs):
        grad_keys, grad_values = carry
        index, log_blk = inputs
        seq_start, start, query_blk, key_seq, value_seq = block_slices(
            queries, keys_all, values_all, index
        )
        grad_blk = lax.dynamic_slice_in_dim(grad_mixed, seq_start + start, QBLK, 0)
        query_heads = split_heads(query_blk)
        key_heads = split_heads(key_seq)
        grad_heads = split_heads(grad_blk)
        scores = masked_scores(query_heads, key_heads, start, scale)
        chances = jnp.exp(scores - log_blk[..., None])
        grad_probs = jnp.einsum(
            "qhd,khd->hqk", grad_heads, split_heads(value_seq), preferred_element_type=jnp.float32
        )
        inner = jnp.sum(chances * grad_probs, axis=-1, keepdims=True)
        grad_scores = (chances * (grad_probs - inner)).astype(jnp.bfloat16)
        grad_query = (
            jnp.einsum("hqk,khd->qhd", grad_scores, key_heads, preferred_element_type=jnp.float32)
            * scale
        )
        grad_key = (
            jnp.einsum("hqk,qhd->khd", grad_scores, query_heads, preferred_element_type=jnp.float32)
            * scale
        )
        grad_value = jnp.einsum(
            "hqk,qhd->khd",
            chances.astype(jnp.bfloat16),
            grad_heads,
            preferred_element_type=jnp.float32,
        )
        old_keys = lax.dynamic_slice_in_dim(grad_keys, seq_start, LEN, 0)
        old_values = lax.dynamic_slice_in_dim(grad_values, seq_start, LEN, 0)
        grad_keys = lax.dynamic_update_slice_in_dim(
            grad_keys, old_keys + grad_key.reshape(LEN, -1), seq_start, 0
        )
        grad_values = lax.dynamic_update_slice_in_dim(
            grad_values, old_values + grad_value.reshape(LEN, -1), seq_start, 0
        )
        return ((grad_keys, grad_values), grad_query.reshape(QBLK, -1))

    (grad_keys, grad_values), grad_queries = lax.scan(
        attention_advance, (zeros, zeros), (jnp.arange(total_rows // QBLK), log_total)
    )
    return (grad_queries.reshape(total_rows, -1), grad_keys, grad_values)


def shards(
    tokens,
    timesteps,
    norm_gains,
    biases,
    second_shift,
    hidden_bias,
    step_table,
    qkv_weight,
    out_weight,
    up_weight,
    down_weight,
    cotangent,
):
    width = tokens.shape[1]
    half_width = qkv_weight.shape[2]
    half_hidden = up_weight.shape[1]
    slot = lax.axis_index("tensor")
    device = lax.axis_index(("dp", "tensor"))
    scale = HEAD_DIM ** (-0.5)
    gains_all, biases_all, second_all, hidden_all, table_all = (
        lax.all_gather(norm_gains, ("dp", "tensor"), axis=1, tiled=True),
        lax.all_gather(biases, ("dp", "tensor"), axis=1, tiled=True),
        lax.all_gather(second_shift, ("dp", "tensor"), axis=0, tiled=True),
        lax.all_gather(hidden_bias, ("dp", "tensor"), axis=0, tiled=True),
        lax.all_gather(step_table, ("dp", "tensor"), axis=1, tiled=True),
    )
    gains_all = gains_all.astype(jnp.float32)
    biases_all = biases_all.astype(jnp.float32)
    second_all = second_all.astype(jnp.float32)
    hidden_local = lax.dynamic_slice_in_dim(
        hidden_all.astype(jnp.float32), slot * half_hidden, half_hidden, 0
    )
    query_bias = lax.dynamic_slice_in_dim(biases_all[1], slot * half_width, half_width, 0)
    value_bias = lax.dynamic_slice_in_dim(biases_all[2], slot * half_width, half_width, 0)
    step_id = lax.dynamic_slice_in_dim(timesteps, device, 1, 0)
    picker = (step_id[:, None] == jnp.arange(TSTEPS)[None, :]).astype(jnp.bfloat16)
    embed = jnp.dot(picker, table_all, preferred_element_type=jnp.float32)
    start_h = tokens.astype(jnp.float32) + embed
    qkv_full, out_full = fetch_attn(qkv_weight, out_weight)
    up_full, down_full = fetch_mlp(up_weight, down_weight)
    normed = gather_rows(layer_norm(start_h, gains_all[0], biases_all[0]).astype(jnp.bfloat16))
    projected = jnp.einsum("rd,jde->jre", normed, qkv_full, preferred_element_type=jnp.float32)
    queries = (projected[0] + query_bias).astype(jnp.bfloat16)
    keys_all = projected[1].astype(jnp.bfloat16)
    values_all = (projected[2] + value_bias).astype(jnp.bfloat16)
    mixed, log_total = run_attention(queries, keys_all, values_all, scale)
    attn_out = (
        sum_rows(jnp.dot(mixed, out_full, preferred_element_type=jnp.float32)) + biases_all[3]
    )
    middle = start_h + attn_out
    second = gather_rows(layer_norm(middle, gains_all[1], second_all).astype(jnp.bfloat16))
    pre_act = jnp.dot(second, up_full, preferred_element_type=jnp.float32) + hidden_local
    activated = jax.nn.gelu(pre_act).astype(jnp.bfloat16)
    mlp_out = (
        sum_rows(jnp.dot(activated, down_full, preferred_element_type=jnp.float32)) + biases_all[4]
    )
    layer_out = (middle + mlp_out).astype(jnp.bfloat16)
    grad_top = cotangent.astype(jnp.float32)
    up_full, down_full = fetch_mlp(up_weight, down_weight)
    grad_mlp_all = gather_rows(cotangent)
    grad_downw = contract_rows(activated, grad_mlp_all)
    grad_act = contract_cols(grad_mlp_all, down_full)
    unused, gelu_back = jax.vjp(jax.nn.gelu, pre_act)
    grad_pre = gelu_back(grad_act)[0].astype(jnp.bfloat16)
    grad_upw = contract_rows(second, grad_pre)
    grad_hidden_local = jnp.sum(grad_pre.astype(jnp.float32), axis=0)
    grad_second = sum_rows(contract_cols(grad_pre, up_full))
    unused, second_back = jax.vjp(layer_norm, middle, gains_all[1], second_all)
    grad_mid_part, grad_gain_two, grad_shift_two = second_back(grad_second)
    grad_middle = grad_top + grad_mid_part
    grad_up, grad_down = (
        lax.psum_scatter(grad_upw, "dp", scatter_dimension=0, tiled=True),
        lax.psum_scatter(grad_downw, "dp", scatter_dimension=1, tiled=True),
    )
    qkv_full, out_full = fetch_attn(qkv_weight, out_weight)
    grad_attn = grad_middle.astype(jnp.bfloat16)
    grad_attn_all = gather_rows(grad_attn)
    grad_outw = contract_rows(mixed, grad_attn_all)
    grad_mixed = contract_cols(grad_attn_all, out_full).astype(jnp.bfloat16)
    grad_queries, grad_keys, grad_values = attention_back(
        queries, keys_all, values_all, grad_mixed, log_total, scale
    )
    grad_rows = jnp.stack([grad_queries, grad_keys, grad_values]).astype(jnp.bfloat16)
    grad_qkvw = jnp.einsum("rd,jre->jde", normed, grad_rows, preferred_element_type=jnp.float32)
    grad_normed = sum_rows(
        jnp.einsum("jre,jde->rd", grad_rows, qkv_full, preferred_element_type=jnp.float32)
    )
    unused, first_back = jax.vjp(layer_norm, start_h, gains_all[0], biases_all[0])
    grad_start_part, grad_gain_one, grad_shift_one = first_back(grad_normed)
    grad_tokens = grad_middle + grad_start_part
    grad_qkv, grad_out = (
        lax.psum_scatter(grad_qkvw, "dp", scatter_dimension=1, tiled=True),
        lax.psum_scatter(grad_outw, "dp", scatter_dimension=1, tiled=True),
    )
    row_sums = jnp.sum(grad_rows.astype(jnp.float32), axis=1)
    gain_terms = jnp.stack([grad_gain_one, grad_gain_two])
    bias_terms = jnp.stack(
        [
            grad_shift_one,
            place_part(row_sums[0], width, slot * half_width),
            place_part(row_sums[2], width, slot * half_width),
            jnp.sum(grad_attn.astype(jnp.float32), axis=0),
            jnp.sum(grad_top, axis=0),
        ]
    )
    hidden_terms = place_part(
        grad_hidden_local,
        hidden_bias.shape[0] * lax.axis_size(("dp", "tensor")),
        slot * half_hidden,
    )
    seq_grad = jnp.sum(grad_tokens, axis=0, keepdims=True)
    table_terms = lax.dot_general(
        picker.astype(jnp.float32),
        seq_grad,
        (((0,), (0,)), ((), ())),
        precision=HIGH,
        preferred_element_type=jnp.float32,
    )
    grad_gains, grad_biases, grad_shift, grad_hidden, grad_table = (
        lax.psum_scatter(gain_terms, ("dp", "tensor"), scatter_dimension=1, tiled=True),
        lax.psum_scatter(bias_terms, ("dp", "tensor"), scatter_dimension=1, tiled=True),
        lax.psum_scatter(grad_shift_two, ("dp", "tensor"), scatter_dimension=0, tiled=True),
        lax.psum_scatter(hidden_terms, ("dp", "tensor"), scatter_dimension=0, tiled=True),
        lax.psum_scatter(table_terms, ("dp", "tensor"), scatter_dimension=1, tiled=True),
    )
    return (
        layer_out,
        grad_tokens,
        grad_gains,
        grad_biases,
        grad_shift,
        grad_hidden,
        grad_table,
        grad_qkv,
        grad_out,
        grad_up,
        grad_down,
    )


MESH_ID = pl.DeviceIdType.MESH
F32, BF16 = jnp.float32, jnp.bfloat16
NZ, NX, NC, NY = 4, 2, 2, 2
QB = 256
LINE = 40
GELU_A, GELU_B = 0.7978845608028654, 0.044715


def nt(left, right):
    return lax.dot_general(left, right, (((1,), (1,)), ((), ())), preferred_element_type=F32)


def nn(left, right):
    return lax.dot_general(left, right, (((1,), (0,)), ((), ())), preferred_element_type=F32)


def tn(left, right):
    return lax.dot_general(left, right, (((0,), (0,)), ((), ())), preferred_element_type=F32)


def position():
    dp = lax.axis_index("dp")
    return (lax.axis_index("tensor"), dp // (NX * NC), lax.rem(dp // NC, NX), lax.rem(dp, NC))


def device_at(y, z, x, c):
    return (z * (NX * NC) + x * NC + c, y)


def plane_peers(pos):
    y, z, x, c = pos
    for flip in range(1, NY * NX * NC):
        to = (1 - y if flip & 4 else y, z, 1 - x if flip & 2 else x, 1 - c if flip & 1 else c)
        yield flip - 1, to


def greet(pos):
    y, z, x, c = pos
    peers = [device_at(y, lax.rem(z + k, NZ), x, c) for k in range(1, NZ)]
    peers += [device_at(*to) for _, to in plane_peers(pos)]
    barrier = pltpu.get_barrier_semaphore()
    for peer in peers:
        pl.semaphore_signal(barrier, inc=1, device_id=peer, device_id_type=MESH_ID)
    return lambda: pl.semaphore_wait(barrier, len(peers))


def at_step(index, events):
    for step, names in events.items():

        @pl.when(index == step)
        def _():
            for name in names:
                name()


def remote(src, dst, send, recv, index, peer):
    return pltpu.make_async_remote_copy(
        src_ref=src,
        dst_ref=dst,
        send_sem=send.at[index],
        recv_sem=recv.at[index],
        device_id=peer,
        device_id_type=MESH_ID,
    )


class Gather:
    def __init__(self, buf, cols, send, recv, pos):
        self.buf, self.cols, self.send, self.recv, self.pos = buf, cols, send, recv, pos

    def view(self, y, z, x, c):
        return self.buf.at[y, z, x, c, :, self.cols]

    def steps(self, step):
        y, z, x, c = self.pos
        lo, hi, both = pl.ds(0, 2), pl.ds(2, 2), pl.ds(0, 2)
        if step == 0:
            return [
                (k - 1, (y, z, x, c), (y, lax.rem(z + NZ - k, NZ), x, c), device_at(y, lax.rem(z + k, NZ), x, c))
                for k in range(1, NZ)
            ]
        x_peer, y_peer = device_at(y, z, 1 - x, c), device_at(1 - y, z, x, c)
        if step == 1:
            return [(3, (y, lo, x, c), (y, lo, 1 - x, c), x_peer), (4, (y, hi, x, c), (1 - y, hi, x, c), y_peer)]
        if step == 2:
            return [
                (5, (y, lo, both, c), (1 - y, lo, both, c), y_peer),
                (6, (both, hi, x, c), (both, hi, 1 - x, c), x_peer),
            ]
        return [(7, (both, pl.ds(0, NZ), both, c), (both, pl.ds(0, NZ), both, 1 - c), device_at(y, z, x, 1 - c))]

    def start(self, step):
        for sem, src, _, peer in self.steps(step):
            remote(self.view(*src), self.view(*src), self.send, self.recv, sem, peer).start()

    def wait(self, step):
        for sem, _, dst, peer in self.steps(step):
            remote(self.view(*dst), self.view(*dst), self.send, self.recv, sem, peer).wait_recv()

    def next(self, step):
        self.wait(step)
        self.start(step + 1)

    count = 4
    order = (7, 3, 4, 5, 6, 0, 1, 2)

    def drain(self):
        for step in range(self.count):
            for sem, src, _, peer in self.steps(step):
                remote(self.view(*src), self.view(*src), self.send, self.recv, sem, peer).wait_send()


class PlaneGather(Gather):
    order = (10, 0, 1, 8, 9, 2, 4, 6)

    def view(self, y, z, x, c, part=2):
        start, size = self.cols
        if part < 2:
            start, size = start + part * (size // 2), size // 2
        return self.buf.at[y, z, x, c, :, pl.ds(start, size)]

    def steps(self, step):
        y, z, x, c = self.pos
        both, every = pl.ds(0, 2), pl.ds(0, NZ)
        x_peer, y_peer = device_at(y, z, 1 - x, c), device_at(1 - y, z, x, c)
        if step == 0:
            return [(0, (y, z, x, c, 0), (y, z, 1 - x, c, 0), x_peer), (1, (y, z, x, c, 1), (1 - y, z, x, c, 1), y_peer)]
        if step == 1:
            found = []
            for k in range(1, NZ):
                peer, other = device_at(y, lax.rem(z + k, NZ), x, c), lax.rem(z + NZ - k, NZ)
                found.append((2 * k, (y, z, both, c, 0), (y, other, both, c, 0), peer))
                found.append((2 * k + 1, (both, z, x, c, 1), (both, other, x, c, 1), peer))
            return found
        if step == 2:
            return [
                (8, (y, every, both, c, 0), (1 - y, every, both, c, 0), y_peer),
                (9, (both, every, x, c, 1), (both, every, 1 - x, c, 1), x_peer),
            ]
        return [(10, (both, every, both, c), (both, every, both, 1 - c), device_at(y, z, x, 1 - c))]


class SmallGather(Gather):
    count = 2

    def __init__(self, buf, send, recv, pos):
        super().__init__(buf, None, send, recv, pos)

    def view(self, y, z, x, c):
        return self.buf.at[y, z, x, c]

    def steps(self, step):
        y, z, x, c = self.pos
        if step == 0:
            return super().steps(0)
        every = pl.ds(0, NZ)
        return [
            (3 + flip, (y, every, x, c), (to[0], every, to[2], to[3]), device_at(*to)) for flip, to in plane_peers(self.pos)
        ]


class SmallScatter:
    def __init__(self, source, acc, first, last, send, recv, pos):
        self.source, self.acc, self.first, self.last = source, acc, first, last
        self.send, self.recv, self.pos = send, recv, pos

    def copies(self, step):
        y, z, x, c = self.pos
        every = pl.ds(0, NZ)
        if step == 0:
            return [
                remote(
                    self.source.at[to[0], every, to[2], to[3]],
                    self.first.at[flip],
                    self.send,
                    self.recv,
                    3 + flip,
                    device_at(*to),
                )
                for flip, to in plane_peers(self.pos)
            ]
        return [
            remote(
                self.acc.at[lax.rem(z + k, NZ)],
                self.last.at[k - 1],
                self.send,
                self.recv,
                k - 1,
                device_at(y, lax.rem(z + k, NZ), x, c),
            )
            for k in range(1, NZ)
        ]

    def start(self, step):
        for copy in self.copies(step):
            copy.start()

    def next(self):
        y, z, x, c = self.pos
        total = self.source[y, :, x, c]
        for flip, copy in enumerate(self.copies(0)):
            copy.wait_recv()
            total = total + self.first[flip]
        self.acc[...] = total
        self.start(1)

    def final(self):
        total = self.acc[self.pos[1]]
        for k, copy in enumerate(self.copies(1)):
            copy.wait_recv()
            total = total + self.last[k]
        return total

    def drain(self):
        for step in range(2):
            for copy in self.copies(step):
                copy.wait_send()


def small_scratch():
    tile = (8, 128)
    return [
        pltpu.VMEM((NY, NZ, NX, NC, *tile), F32),
        pltpu.VMEM((NZ, *tile), F32),
        pltpu.VMEM((NY * NX * NC - 1, NZ, *tile), F32),
        pltpu.VMEM((NZ - 1, *tile), F32),
    ]


def fold(values):
    return values[0:8] + pltpu.roll(values[8:16], LINE, 1) + pltpu.roll(values[16:24], 2 * LINE, 1)


def unfold(tile):
    return jnp.concatenate([tile, pltpu.roll(tile, 128 - LINE, 1), pltpu.roll(tile, 128 - 2 * LINE, 1)], axis=0)


def gelu_parts(v):
    square = v * v
    half = 0.5 + 0.5 * jnp.tanh(v * (GELU_A + (GELU_A * GELU_B) * square))
    act = v * half
    slope = half + (2.0 * act) * (1.0 - half) * (GELU_A + (3 * GELU_A * GELU_B) * square)
    return act, slope


def moments(hidden):
    average = jnp.mean(hidden, axis=-1, keepdims=True)
    centered = hidden - average
    variance = jnp.mean(centered * centered, axis=-1, keepdims=True)
    scale = lax.rsqrt(variance + EPS)
    return centered * scale, scale


def norm_back(xhat, scale, grad):
    return (grad - jnp.mean(grad, axis=-1, keepdims=True) - xhat * jnp.mean(grad * xhat, axis=-1, keepdims=True)) * scale


def row_block(index, size):
    return pl.ds(pl.multiple_of(index * size, size), size)


def sum_rows_of(values):
    return jnp.sum(values.astype(F32), axis=0, keepdims=True)


def blocks():
    for z in range(NZ):
        for x in range(NX):
            for c in range(NC):
                for y in range(NY):
                    yield (z * NX + x) * NC * NY + c * NY + y, (y, z, x, c)


class Scatter:
    def __init__(self, source, own, bufs, send, recv, pos, order):
        self.source, self.own, self.bufs = source, own, bufs
        self.send, self.recv, self.pos, self.order = send, recv, pos, order

    def copies(self, step):
        y, z, x, c = self.pos
        first, second_x, second_y, third_y, third_x, last = self.bufs
        own = self.own
        lo, hi, both = pl.ds(0, 2), pl.ds(2, 2), pl.ds(0, 2)
        x_peer, y_peer = device_at(y, z, 1 - x, c), device_at(1 - y, z, x, c)
        sem = self.order
        if step == 0:
            return [(sem[0], self.source.at[both, pl.ds(0, NZ), both, 1 - c], first, device_at(y, z, x, 1 - c))]
        if step == 1:
            return [
                (sem[1], own.at[both, lo, 1 - x], second_x, x_peer),
                (sem[2], own.at[1 - y, hi, both], second_y, y_peer),
            ]
        if step == 2:
            return [(sem[3], own.at[1 - y, lo, x], third_y, y_peer), (sem[4], own.at[y, hi, 1 - x], third_x, x_peer)]
        return [
            (sem[4 + k], own.at[y, lax.rem(z + k, NZ), x], last.at[k - 1], device_at(y, lax.rem(z + k, NZ), x, c))
            for k in range(1, NZ)
        ]

    def start(self, step):
        for sem, src, dst, peer in self.copies(step):
            remote(src, dst, self.send, self.recv, sem, peer).start()

    def wait(self, step):
        for sem, src, dst, peer in self.copies(step):
            remote(src, dst, self.send, self.recv, sem, peer).wait_recv()

    def add(self, step):
        y, z, x, c = self.pos
        own, source = self.own, self.source
        first, second_x, second_y, third_y, third_x, last = self.bufs
        kind = own.dtype

        def plus(left, right):
            return (left.astype(F32) + right.astype(F32)).astype(kind)

        def each(count, body):
            def run(i, _):
                body(i)
                return 0

            lax.fori_loop(0, count, run, 0)

        if step == 0:

            def body(i):
                iy, iz, ix = i // (NZ * NX), lax.rem(i // NX, NZ), lax.rem(i, NX)
                own[iy, iz, ix] = plus(source[iy, iz, ix, c], first[iy, iz, ix])

            each(NY * NZ * NX, body)
        elif step == 1:

            def body(i):
                a, b = i // 2, lax.rem(i, 2)
                own[a, b, x] = plus(own[a, b, x], second_x[a, b])
                own[y, 2 + a, b] = plus(own[y, 2 + a, b], second_y[a, b])

            each(4, body)
        else:

            def body(i):
                own[y, i, x] = plus(own[y, i, x], third_y[i])
                own[y, 2 + i, x] = plus(own[y, 2 + i, x], third_x[i])

            each(2, body)

    def first_sum(self):
        self.wait(0)
        self.add(0)
        self.sent(0)

    def next(self, step):
        if step == 0:
            self.first_sum()
        else:
            self.wait(step)
            self.add(step)
        self.start(step + 1)

    def sent(self, step):
        for sem, src, dst, peer in self.copies(step):
            remote(src, dst, self.send, self.recv, sem, peer).wait_send()

    def final(self):
        y, z, x, c = self.pos
        last = self.bufs[5]
        self.wait(3)
        total = self.own[y, z, x].astype(F32)
        for k in range(NZ - 1):
            total = total + last[k].astype(F32)
        return total

    def drain(self):
        for step in range(1, 4):
            self.sent(step)


def scatter_scratch(per, width, kind):
    return [
        pltpu.VMEM((NY, NZ, NX, per, width), kind),
        pltpu.VMEM((2, 2, per, width), kind),
        pltpu.VMEM((2, 2, per, width), kind),
        pltpu.VMEM((2, per, width), kind),
        pltpu.VMEM((2, per, width), kind),
        pltpu.VMEM((NZ - 1, per, width), kind),
    ]


def layer_kernel(
    dims,
    steps,
    gains,
    biases,
    shift2,
    hidden,
    table_t,
    tokens_in,
    qkv_in,
    outw_t,
    upw_in,
    downw_t,
    cot_in,
    gpack_out,
    gup_out,
    gdown_out,
    gout_out,
    gqkv_out,
    gtok_out,
    layer_out,
    middle_hbm,
    small_out,
    lse_out,
    ghid_out,
    full,
    pack,
    lines,
    stage,
    tokens,
    cot,
    normed,
    queries,
    keys_all,
    values_all,
    mixed,
    second,
    second_t,
    cot_t,
    result,
    gsec,
    act,
    gpre,
    gtile,
    hid,
    acc,
    inner,
    sums,
    gup,
    gdown,
    gout,
    gqkv,
    *rest,
):
    rows, width, per, half, ffh, ft = dims
    pos = position()
    y, z, x, c = pos
    me = device_at(y, z, x, c)[0] * NY + y
    share = width // (NZ * NX * NC * NY)
    n_ff = ffh // ft
    send, recv, local = rest[-3:]

    n_groups = half // 128
    groups = [f"g{i}" for i in range(n_groups)]
    names = ["pack", "hid", *groups, "o"] + [f"m{i}" for i in range(n_ff)]
    col = {"o": pl.ds(3 * half, half)}
    for i in range(n_groups):
        col[f"g{i}"] = pl.ds(i * 384, 384)
    for i in range(n_ff):
        col[f"m{i}"] = pl.ds(4 * half + 2 * ft * i, 2 * ft)
    flow, used = {}, 0
    for name in names:
        count = {"pack": 10, "hid": 10, "m1": 11}.get(name, 8)
        sems = (send.at[pl.ds(used, count)], recv.at[pl.ds(used, count)], pos)
        used += count
        if name == "m1":
            flow[name] = PlaneGather(full, (4 * half + 2 * ft, 2 * ft), *sems)
        elif name in col:
            flow[name] = Gather(full, col[name], *sems)
        else:
            flow[name] = SmallGather({"pack": pack, "hid": lines}[name], *sems)
    ready = greet(pos)
    copies = {}

    def copy(name, src, dst):
        copies[name] = pltpu.make_async_copy(src, dst, local.at[len(copies)])
        copies[name].start()

    def own(start, size):
        return full.at[y, z, x, c, :, pl.ds(start, size)]

    parts = {"pack": [], "hid": []}
    for g in range(n_groups):
        parts[f"g{g}"] = [f"g{g}{i}" for i in range(3)]
        for i in range(3):
            copy(f"g{g}{i}", qkv_in.at[i, :, pl.ds(128 * g, 128)], own(384 * g + 128 * i, 128))
    copy("cot", cot_in, cot)
    copy("tokens", tokens_in, tokens)
    copy("o", outw_t, own(3 * half, half))
    parts["o"] = ["o"]
    for i in range(n_ff):
        copy(f"u{i}", upw_in.at[:, pl.ds(ft * i, ft)], own(4 * half + 2 * ft * i, ft))
        copy(f"d{i}", downw_t.at[:, pl.ds(ft * i, ft)], own(4 * half + 2 * ft * i + ft, ft))
        parts[f"m{i}"] = [f"u{i}", f"d{i}"]

    def launch(name):
        for key in parts[name]:
            copies[key].wait()
        flow[name].start(0)

    stage[...] = jnp.zeros_like(stage)
    stage[0:2, 0:share] = gains[...].astype(F32)
    stage[2:7, 0:share] = biases[...].astype(F32)
    stage[7:8, 0:share] = shift2[...].astype(F32)
    n_steps, n_seq = table_t.shape[1], steps.shape[1]
    wanted = jnp.concatenate([steps[...], jnp.full((1, 128 - n_seq), -1, jnp.int32)], axis=1)
    picked = (wanted == lax.broadcasted_iota(jnp.int32, (n_steps, 128), 0)).astype(BF16)
    pack[y, z, x, c] = fold(stage[...].T[0:share] + pltpu.roll(nn(table_t[...], picked), 8, 1))
    hshare = hidden.shape[1]
    lane = lax.broadcasted_iota(jnp.int32, (hshare, NC * NY * hshare), 0) + hshare * (c * NY + y)
    place = (lane == lax.broadcasted_iota(jnp.int32, (hshare, NC * NY * hshare), 1)).astype(BF16)
    spread = nn(jnp.broadcast_to(hidden[...], (8, hshare)), place)
    n_hid = NC * NY * hshare // 128
    pieces = [spread[0:1, 128 * j : 128 * j + 128] for j in range(n_hid)]
    lines[y, z, x, c] = jnp.concatenate([*pieces, jnp.zeros((8 - n_hid, 128), F32)], axis=0)

    ready()
    launch("pack")
    launch("g0")
    copies["cot"].wait()

    def turn_cot(i, total):
        rb = row_block(i, 256)
        block = cot[rb, :]
        cot_t[:, rb] = block.T
        return total + sum_rows_of(block)

    csum = lax.fori_loop(0, rows // 256, turn_cot, jnp.zeros((1, width), F32))
    sums[...] = jnp.zeros_like(sums)
    sums[6:7, :] = csum
    flow["pack"].next(0)
    flow["g0"].next(0)
    launch("g1")
    flow["g0"].next(1)
    flow["pack"].wait(1)
    flow["g1"].next(0)
    launch("g2")
    launch("hid")
    launch("o")

    for d, (by, bz, bx, bc) in blocks():
        result[d * share : d * share + share, 0:128] = unfold(pack[by, bz, bx, bc])
    small_out[...] = result[0:width, 0:128].T
    embed = small_out[pl.ds(8 + me, 1), :]
    copies["tokens"].wait()

    def first_norm(i, _):
        rb = row_block(i, 128)
        xhat, _ = moments(tokens[rb, :].astype(F32) + embed)
        normed[rb, :] = (xhat * small_out[0:1, :] + small_out[2:3, :]).astype(BF16)
        return 0

    lax.fori_loop(0, rows // 128, first_norm, 0)
    flow["g0"].next(2)
    flow["g1"].next(1)
    flow["g2"].next(0)
    launch("m0")
    launch("m1")

    def whole(cols, size):
        return jnp.concatenate([full[by, :, :, :, :, cols].reshape(width, size) for by in range(NY)], axis=1)

    def project(group):
        cols = pl.ds(pl.multiple_of(group * 384, 128), 384)

        def body(i, _):
            rb = row_block(i, 512)
            value = nn(normed[rb, :], whole(cols, 384))
            for by in range(NY):
                to = pl.ds(pl.multiple_of((by * n_groups + group) * 128, 128), 128)
                piece = [value[:, by * 384 + 128 * j : by * 384 + 128 * j + 128] for j in range(3)]
                queries[rb, to] = (piece[0] + small_out[3:4, to]).astype(BF16) * jnp.asarray(HEAD_DIM**-0.5, BF16)
                keys_all[rb, to] = piece[1].astype(BF16)
                values_all[rb, to] = (piece[2] + small_out[4:5, to]).astype(BF16)
            return 0

        lax.fori_loop(0, rows // 512, body, 0)

    def then(name, step):
        return lambda: flow[name].next(step)

    def back(name, step):
        return lambda: sums_of[name].next(step)

    def arrived(name):
        return lambda: flow[name].wait(3)

    def off(name):
        return lambda: launch(name)

    events = {
        1: [then("g1", 2), then("g2", 1), then("o", 0), then("hid", 0)],
        3: [then("g2", 2), then("o", 1)],
        4: [then("m0", 1)],
        5: [then("o", 2)],
    }
    between = {1: [then("m0", 0), then("m1", 0)]}

    def attend(s, _):
        group, by = s // NY, lax.rem(s, NY)
        p = by * n_groups + group

        @pl.when(by == 0)
        def _():
            at_step(group, {g: [arrived(f"g{g}")] for g in range(n_groups)})
            project(group)
            at_step(group, between)

        at_step(s, events)
        cols = pl.ds(pl.multiple_of(p * 128, 128), 128)
        low = lax.broadcasted_iota(jnp.int32, (QB, 128), 1) < HEAD_DIM
        for i in range(rows // QB):
            n = (i + 1) * QB
            rb = slice(i * QB, n)
            key, value, query = keys_all[0:n, cols], values_all[0:n, cols], queries[rb, cols]
            outs, scales = [], []
            for h in range(2):
                scores = nt(key, jnp.where(low == (h == 0), query, jnp.zeros_like(query)))
                top = jnp.max(scores, axis=0, keepdims=True)
                expo = jnp.exp(scores - top)
                total = jnp.sum(expo, axis=0, keepdims=True)
                lse_out[pl.ds(2 * p + h, 1), rb] = top + jnp.log(total)
                scales.append(jnp.broadcast_to(1.0 / total, (HEAD_DIM, QB)))
                outs.append(tn(expo.astype(BF16), value))
            scale = jnp.concatenate(scales, axis=0).T
            mixed[rb, cols] = (jnp.where(low, outs[0], outs[1]) * scale).astype(BF16)
        return 0

    lax.fori_loop(0, width // 128, attend, 0)
    flow["o"].wait(3)
    launch("m2")
    flow["hid"].wait(1)
    for bz in range(NZ):
        for bx in range(NX):
            total = lines[0, bz, bx, 0] + lines[0, bz, bx, 1] + lines[1, bz, bx, 0] + lines[1, bz, bx, 1]
            for j in range(n_hid):
                at = ((bz * NX + bx) * n_hid + j) * 128
                hid[0:1, at : at + 128] = total[j : j + 1]

    at = len(copies)

    def middle_save(i):
        rb = row_block(i, 256)
        return pltpu.make_async_copy(result.at[rb], middle_hbm.at[rb], local.at[at + 10 + i])

    def second_norm(i, _):
        at_step(i, {2: [then("m0", 2)]})
        rb = row_block(i, 256)
        start_h = tokens[rb, :].astype(F32) + embed
        value = start_h + (nt(mixed[rb, :], whole(col["o"], half)) + small_out[5:6, :])
        result[rb, :] = value
        middle_save(i).start()
        gsec[rb, :] = jnp.zeros_like(value)
        xhat, _ = moments(value)
        block = (xhat * small_out[1:2, :] + small_out[7:8, :]).astype(BF16)
        second[rb, :] = block
        second_t[:, rb] = block.T
        return 0

    lax.fori_loop(0, rows // 256, second_norm, 0)
    flow["m1"].next(1)
    flow["m0"].wait(3)
    for i in range(rows // 256):
        middle_save(i).wait()

    free = 4 * half
    half_f = 2 * ft
    places = {"m0": (0, free, half_f), "m1": (1, free, half_f), "m2": (0, free + half_f, half_f), "o": (1, free + half_f, half)}
    for g in range(n_groups):
        places[f"q{g}"] = (g % 2, free + 2 * half_f + 384 * (g // 2), 384)
    sums_of = {}
    before = {"m0": "g0", "m1": "g1", "m2": "g2", "o": "o", "q0": "m0", "q1": "m2", "q2": "m1", "pack": "pack", "hid": "hid"}
    for i, name in enumerate([*places, "pack", "hid"]):
        gather = flow[before[name]]
        sems = (gather.send, gather.recv, pos)
        if name in places:
            core, start, size = places[name]
            own_view = full.at[:, :, :, core, :, pl.ds(start, size)]
            bufs = rest[6 * i : 6 * i + 6]
            if name[0] == "m":
                source = gtile
            else:
                source = gtile.at[:, :, :, :, :, pl.ds(0 if name in ("o", "q1") else half, 384)]
            sums_of[name] = Scatter(source, own_view, bufs, *sems, gather.order)
        else:
            sums_of[name] = SmallScatter(*(rest[-11:-7] if name == "pack" else rest[-7:-3]), *sems)
    tiles = NY * n_ff

    def tile(t, _):
        ty, tm = lax.rem(t, NY), t // NY
        slot = lax.rem(t, 2)

        def begin(name):
            return lambda: sums_of[name].start(0)

        def first_sum(name):
            return lambda: sums_of[name].first_sum()

        def second_step(name):
            return lambda: sums_of[name].start(1)

        at_step(
            t,
            {
                1: [then("m2", 0)],
                2: [flow["g0"].drain, begin("m0"), flow["m0"].drain, then("m2", 1), arrived("m1")],
                4: [flow["g1"].drain, begin("m1"), arrived("m2")],
            },
        )

        up_at = pl.ds(pl.multiple_of(4 * half + tm * 2 * ft, 128), ft)
        down_at = pl.ds(pl.multiple_of(4 * half + tm * 2 * ft + ft, 128), ft)
        hid_at = pl.ds(pl.multiple_of(ty * ffh + tm * ft, 128), ft)

        def up():
            return full[ty, :, :, :, :, up_at].reshape(width, ft)

        def down():
            return full[ty, :, :, :, :, down_at].reshape(width, ft)

        pre = nn(second[...], up()) + hid[:, hid_at]
        gact = nn(cot[...], down())
        value, slope = gelu_parts(pre)
        act[...] = value.astype(BF16)
        grad = (gact * slope).astype(BF16)
        gpre[...] = grad
        ghid_out[:, hid_at] = sum_rows_of(grad)
        result[...] += nt(act[...], down())
        gsec[...] += nt(gpre[...], up())

        def results():
            second[...] = (result[...] + small_out[6:7, :]).astype(BF16)
            layer_save.start()
            middle_load.start()

        at_step(
            t,
            {
                1: [then("m1", 2)],
                2: [first_sum("m0")],
                3: [then("m2", 2), second_step("m0")],
                4: [first_sum("m1"), second_step("m1")],
                tiles - 1: [results, back("m0", 1)],
            },
        )

        turn = (NZ, NX, NC, per, ft)
        gtile[slot, :, :, :, :, 0:ft] = nn(second_t[...], gpre[...]).astype(BF16).reshape(turn)
        gtile[slot, :, :, :, :, ft : 2 * ft] = nn(cot_t[...], act[...]).astype(BF16).reshape(turn)
        return 0

    layer_save = pltpu.make_async_copy(second, layer_out, local.at[at + 5])
    middle_load = pltpu.make_async_copy(middle_hbm, result, local.at[at + 6])
    lax.fori_loop(0, tiles, tile, 0)
    for name in ("g2", "m1", "m2", "hid"):
        flow[name].drain()
    sums_of["m2"].start(0)
    reload = [
        pltpu.make_async_copy(tokens_in.at[:, pl.ds(0, ft)], act, local.at[at + 7]),
        pltpu.make_async_copy(tokens_in.at[:, pl.ds(ft, width - ft)], gpre.at[:, pl.ds(0, width - ft)], local.at[at + 8]),
    ]
    for load in reload:
        load.start()
    for d, (by, bz, bx, bc) in blocks():
        start = (bz * NX + bx) * n_hid
        pieces = [ghid_out[:, 128 * (start + j) : 128 * (start + j + 1)] for j in range(n_hid)]
        sums_of["hid"].source[by, bz, bx, bc] = jnp.concatenate([*pieces, jnp.zeros((8 - n_hid, 128), F32)], axis=0)
    sums_of["hid"].start(0)
    layer_save.wait()
    middle_load.wait()
    gattn, gattn_t, normed_t, gmixed = second, cot_t, second_t, tokens
    gq, gk, gv = second, normed, cot
    def second_back(i, totals):
        rb = row_block(i, 128)
        xhat, scale = moments(result[rb, :])
        grad = gsec[rb, :]
        total = cot[rb, :].astype(F32) + norm_back(xhat, scale, grad * small_out[1:2, :])
        gsec[rb, :] = total
        low = total.astype(BF16)
        gattn[rb, :] = low
        gattn_t[:, rb] = low.T
        return (
            totals[0] + sum_rows_of(grad * xhat),
            totals[1] + sum_rows_of(grad),
            totals[2] + sum_rows_of(low),
        )

    zero = jnp.zeros((1, width), F32)
    ggain2, gshift2, gattn_sum = lax.fori_loop(0, rows // 128, second_back, (zero, zero, zero))
    sums[1:2, :] = ggain2
    sums[5:6, :] = gattn_sum
    sums[7:8, :] = gshift2

    def weight(index):
        picks = [
            full[by, :, :, :, :, pl.ds(384 * g + 128 * index, 128)].reshape(width, 128)
            for by in range(NY)
            for g in range(n_groups)
        ]
        return jnp.concatenate(picks, axis=1)

    flow["pack"].drain()
    flow["o"].drain()
    sums_of["m1"].next(1)
    sums_of["m2"].next(0)

    def out_grad(i, _):
        part = nn(gattn_t[row_block(i, 384), :], mixed[...]).astype(BF16)
        for by in range(NY):
            to = part[:, by * half : by * half + half].reshape(2, NX, NC, per, half)
            gtile[by, pl.ds(i * 2, 2), :, :, :, 0:half] = to
        return 0

    lax.fori_loop(0, width // 384, out_grad, 0)
    sums_of["o"].start(0)
    sums_of["m0"].next(2)

    def mixed_grad(i, _):
        rb = row_block(i, 512)
        gmixed[rb, :] = nn(gattn[rb, :], whole(col["o"], half)).astype(BF16)
        return 0

    lax.fori_loop(0, rows // 512, mixed_grad, 0)
    sums_of["o"].next(0)

    def turn_normed(i, _):
        rb = row_block(i, 256)
        normed_t[:, rb] = normed[rb, :].T
        return 0

    lax.fori_loop(0, rows // 256, turn_normed, 0)
    events_back = {
        1: [back("m1", 2)],
        2: [back("m2", 1)],
        3: [back("q0", 0), back("o", 1), sums_of["hid"].next],
        4: [back("m2", 2), back("q0", 1)],
        5: [back("o", 2), back("q0", 2), back("q1", 0)],
    }

    def attend_back(s, _):
        group, by = s // NY, lax.rem(s, NY)
        p = by * n_groups + group
        at_step(s, events_back)
        cols = pl.ds(pl.multiple_of(p * 128, 128), 128)
        dots = (gmixed[:, cols].astype(F32) * mixed[:, cols].astype(F32)).T
        for h in range(2):
            inner[h : h + 1, :] = jnp.sum(dots[HEAD_DIM * h : HEAD_DIM * (h + 1)], axis=0, keepdims=True)
        for j in range(rows // QB):
            kb, first = slice(j * QB, (j + 1) * QB), j * QB
            later = rows - first
            key, value = keys_all[kb, cols], values_all[kb, cols]
            low = lax.broadcasted_iota(jnp.int32, (later, 128), 1) < HEAD_DIM

            def two(block):
                none = jnp.zeros_like(block)
                return jnp.concatenate([jnp.where(low, block, none), jnp.where(low, none, block)], axis=0)

            query, grad = two(queries[first:rows, cols]), two(gmixed[first:rows, cols])
            logs = jnp.concatenate([lse_out[pl.ds(2 * p + h, 1), first:rows] for h in range(2)], axis=1)
            inners = jnp.concatenate([inner[h : h + 1, first:rows] for h in range(2)], axis=1)
            probs = jnp.exp(nt(key, query) - logs)
            gscores = (probs * (nt(value, grad) - inners)).astype(BF16)
            gv[kb, cols] = nn(probs.astype(BF16), grad).astype(BF16)
            gk[kb, cols] = nn(gscores, query).astype(BF16)
            both = tn(gscores, key)
            more = jnp.where(low, both[:later], both[later:])
            if j == 0:
                acc[...] = more
            else:
                acc[first:rows] += more
        gq[:, cols] = (acc[...] * HEAD_DIM**-0.5).astype(BF16)

        @pl.when(by == NY - 1)
        def _():
            offset = lax.rem(group + 1, 2) * half
            for piece, source in enumerate((gq, gk, gv)):
                pick = jnp.concatenate(
                    [source[:, pl.ds(pl.multiple_of((b * n_groups + group) * 128, 128), 128)] for b in range(NY)], axis=1
                )
                part = nn(normed_t[...], pick).astype(BF16)
                for b in range(NY):
                    to = pl.ds(pl.multiple_of(offset + piece * 128, 128), 128)
                    gtile[b, :, :, :, :, to] = part[:, b * 128 : b * 128 + 128].reshape(NZ, NX, NC, per, 128)
            at_step(group, {g: [lambda g=g: sums_of[f"q{g}"].start(0)] for g in range(n_groups)})
            at_step(group, {n_groups - 1: [back("q1", 1)]})

        return 0

    lax.fori_loop(0, NY * n_groups, attend_back, 0)
    for load in reload:
        load.wait()

    def m_final(i):
        def run():
            total = sums_of[f"m{i}"].final()
            gup[:, ft * i : ft * i + ft] = total[:, 0:ft]
            gdown[:, ft * i : ft * i + ft] = total[:, ft:]

        return run

    owners = {}
    for i, (name, src, dst) in enumerate([("gup", gup, gup_out), ("gdown", gdown, gdown_out), ("gout", gout, gout_out), ("gqkv", gqkv, gqkv_out)]):
        owners[name] = pltpu.make_async_copy(src, dst, local.at[at + 14 + i])

    def first_back(i, totals):
        rb = row_block(i, 256)
        block = jnp.concatenate([act[rb, :], gpre[rb, 0 : width - ft]], axis=1)
        xhat, scale = moments(block.astype(F32) + embed)
        q_rows, k_rows, v_rows = gq[rb, :], gk[rb, :], gv[rb, :]
        grad = nt(q_rows, weight(0)) + nt(k_rows, weight(1)) + nt(v_rows, weight(2))
        total = gsec[rb, :] + norm_back(xhat, scale, grad * small_out[0:1, :])
        result[rb, :] = total

        at_step(
            i,
            {0: [back("q2", 0)], 1: [m_final(0), back("q1", 2)], 2: [back("q2", 1), m_final(1)]},
        )
        return (
            totals[0] + sum_rows_of(grad * xhat),
            totals[1] + sum_rows_of(grad),
            totals[2] + sum_rows_of(q_rows),
            totals[3] + sum_rows_of(v_rows),
            totals[4] + sum_rows_of(total),
        )

    ggain1, gshift1, q_sum, v_sum, seq_sum = lax.fori_loop(0, rows // 256, first_back, (zero,) * 5)
    sums[0:1, :] = ggain1
    sums[2:3, :] = gshift1
    sums[3:4, :] = q_sum
    sums[4:5, :] = v_sum
    sums[pl.ds(8 + me, 1), :] = seq_sum
    gtok = pltpu.make_async_copy(result, gtok_out, local.at[at + 9])
    gtok.start()
    turned = sums[...].T
    for d, (by, bz, bx, bc) in blocks():
        sums_of["pack"].source[by, bz, bx, bc] = fold(turned[d * share : d * share + share])
    sums_of["pack"].start(0)
    last = f"q{n_groups - 1}"
    sums_of[last].next(2)
    for i in range(2, n_ff):
        m_final(i)()
    owners["gup"].start()
    owners["gdown"].start()
    sums_of["pack"].next()
    gout[...] = sums_of["o"].final()
    owners["gout"].start()
    gpack_out[8:16] = sums_of["hid"].final()

    def qkv_final(g):
        total = sums_of[f"q{g}"].final()
        for piece in range(3):
            gqkv[piece, :, 128 * g : 128 * g + 128] = total[:, 128 * piece : 128 * piece + 128]

    for g in range(n_groups - 1):
        qkv_final(g)
    for name, each in sums_of.items():
        if name not in ("pack", last):
            each.drain()
    qkv_final(n_groups - 1)
    owners["gqkv"].start()
    gpack_out[0:8] = sums_of["pack"].final()
    gtok.wait()
    sums_of[last].drain()
    sums_of["pack"].drain()
    for each in owners.values():
        each.wait()


def finish_kernel(slots, count, steps, gpack, *refs):
    large, (gains_out, biases_out, shift_out, hidden_out, table_out) = refs[:count], refs[count : count + 5]
    outs, bufs, (load_sem, save_sem) = refs[count + 5 : 2 * count + 5], refs[2 * count + 5 : 3 * count + 5], refs[-2:]
    pieces = []
    for src, buf, out in zip(large, bufs, outs):
        cut = 4 if src.shape[0] % 512 == 0 else 1
        size = src.shape[0] // cut
        for k in range(cut):
            at, n = pl.ds(k * size, size), len(pieces)
            pieces.append(
                (
                    pltpu.make_async_copy(src.at[at], buf.at[at], load_sem.at[n]),
                    pltpu.make_async_copy(buf.at[at], out.at[at], save_sem.at[n]),
                )
            )
    for load, _ in pieces:
        load.start()
    share, hshare = gains_out.shape[1], hidden_out.shape[1]
    features = unfold(gpack[0:8, :])
    turned = jnp.concatenate([features, jnp.zeros((128 - share, 128), F32)], axis=0).T
    gains_out[...] = turned[0:2, 0:share]
    biases_out[...] = turned[2:7, 0:share]
    shift_out[...] = turned[7:8, 0:share]
    slot = lax.rem(lax.axis_index("dp"), NC) * NY + lax.axis_index("tensor")
    line = jnp.concatenate([gpack[8 + j : 9 + j, :] for j in range(slots * hshare // 128)], axis=1)
    value = line[:, 0:hshare]
    for k in range(1, slots):
        value = jnp.where(slot == k, line[:, hshare * k : hshare * k + hshare], value)
    hidden_out[...] = value
    for load, save in pieces:
        load.wait()
        save.start()
    n_steps, n_seq = table_out.shape[1], steps.shape[1]
    picked = (steps[...] == lax.broadcasted_iota(jnp.int32, (n_steps, n_seq), 0)).astype(F32)
    table_out[...] = lax.dot_general(
        features[:, 8 : 8 + n_seq], picked, (((1,), (1,)), ((), ())), precision=HIGH, preferred_element_type=F32
    )
    for _, save in pieces:
        save.wait()


def fast_shards(
    tokens,
    timesteps,
    norm_gains,
    biases,
    second_shift,
    hidden_bias,
    step_table,
    qkv_weight,
    out_weight,
    up_weight,
    down_weight,
    cotangent,
):
    rows, width = tokens.shape
    _, per, half = qkv_weight.shape
    ffh = up_weight.shape[1]
    ft = 512
    dims = (rows, width, per, half, ffh, ft)
    n_ff, n_groups = ffh // ft, half // 128
    total = 4 * half + 2 * ffh
    vmem, anywhere = pl.BlockSpec(memory_space=pltpu.VMEM), pl.BlockSpec(memory_space=pl.ANY)
    shape = jax.ShapeDtypeStruct
    low, wide = shape((rows, width), BF16), shape((rows, width), F32)
    vm = pltpu.VMEM
    hshare = hidden_bias.shape[0]
    steps = timesteps.reshape(1, -1)
    chunks = [2 * ft] * n_ff + [half] * (1 + n_groups)
    scratch = []
    for cols in chunks:
        scratch += scatter_scratch(per, cols, BF16)
    n_sems = 2 * 10 + 8 * (n_groups + n_ff) + 11
    owned = [shape((per, ffh), F32), shape((per, ffh), F32), shape((per, half), F32), shape((3, per, half), F32)]
    gpack, gup, gdown, gout, gqkv, gtok, layer, _ = pl.pallas_call(
        functools.partial(layer_kernel, dims),
        in_specs=[vmem] * 6 + [anywhere] * 6,
        out_specs=[vmem] + [anywhere] * 7,
        out_shape=[
            shape((16, 128), F32),
            *owned,
            wide,
            low,
            wide,
        ],
        scratch_shapes=[
            vm((128, width), F32),
            vm((16, rows), F32),
            vm((1, NY * ffh), F32),
            vm((NY, NZ, NX, NC, per, total), BF16),
            vm((NY, NZ, NX, NC, 8, 128), F32),
            vm((NY, NZ, NX, NC, 8, 128), F32),
            vm((128, 128), F32),
            vm((rows, width), BF16),
            vm((rows, width), BF16),
            vm((rows, width), BF16),
            vm((rows, width), BF16),
            vm((rows, width), BF16),
            vm((rows, width), BF16),
            vm((rows, width), BF16),
            vm((rows, width), BF16),
            vm((width, rows), BF16),
            vm((width, rows), BF16),
            vm((rows, width), F32),
            vm((rows, width), F32),
            vm((rows, ft), BF16),
            vm((rows, ft), BF16),
            vm((2, NZ, NX, NC, per, 2 * ft), BF16),
            vm((1, NY * ffh), F32),
            vm((rows, 128), F32),
            vm((8, rows), F32),
            vm((128, width), F32),
            *[vm(each.shape, F32) for each in owned],
            *scratch,
            *small_scratch(),
            *small_scratch(),
            pltpu.SemaphoreType.DMA((n_sems,)),
            pltpu.SemaphoreType.DMA((n_sems,)),
            pltpu.SemaphoreType.DMA((24 + 3 * n_groups + 2 * n_ff,)),
        ],
        compiler_params=pltpu.CompilerParams(collective_id=0, has_side_effects=True, vmem_limit_bytes=VMEM_LIMIT),
        name="layer",
    )(
        steps,
        norm_gains,
        biases,
        second_shift.reshape(1, -1),
        hidden_bias.reshape(1, -1),
        step_table.T,
        tokens,
        qkv_weight,
        out_weight.T,
        up_weight,
        down_weight.T,
        cotangent,
    )
    share, n_steps = norm_gains.shape[1], step_table.shape[0]
    large = (gtok, layer, gqkv, gout, gup, gdown)
    pieces = sum(4 if array.shape[0] % 512 == 0 else 1 for array in large)
    small_shapes = [(2, share), (5, share), (1, share), (1, hshare), (share, n_steps)]
    large_shapes = [shape(array.shape, array.dtype) for array in large]
    grad_gains, grad_biases, grad_shift, grad_hidden, grad_table, gtok, layer, gqkv, gout, gup, gdown = pl.pallas_call(
        functools.partial(finish_kernel, NC * NY, len(large)),
        in_specs=[vmem] * 2 + [anywhere] * len(large),
        out_specs=[vmem] * 5 + [anywhere] * len(large),
        out_shape=[shape(dims, F32) for dims in small_shapes] + large_shapes,
        scratch_shapes=[vm(array.shape, array.dtype) for array in large] + [pltpu.SemaphoreType.DMA((pieces,))] * 2,
        name="finish",
    )(steps, gpack, *large)
    return (
        layer,
        gtok,
        grad_gains,
        grad_biases,
        grad_shift.reshape(share),
        grad_hidden.reshape(hshare),
        grad_table.T,
        gqkv,
        gout.T,
        gup,
        gdown.T,
    )


def solution(mesh):
    in_specs = (
        P(("dp", "tensor"), None),
        P(),
        P(None, ("dp", "tensor")),
        P(None, ("dp", "tensor")),
        P(("dp", "tensor")),
        P(("dp", "tensor")),
        P(None, ("dp", "tensor")),
        P(None, "dp", "tensor"),
        P("tensor", "dp"),
        P("dp", "tensor"),
        P("tensor", "dp"),
        P(("dp", "tensor"), None),
    )
    out_specs = (
        P(("dp", "tensor"), None),
        P(("dp", "tensor"), None),
        P(None, ("dp", "tensor")),
        P(None, ("dp", "tensor")),
        P(("dp", "tensor")),
        P(("dp", "tensor")),
        P(None, ("dp", "tensor")),
        P(None, "dp", "tensor"),
        P("tensor", "dp"),
        P("dp", "tensor"),
        P("tensor", "dp"),
    )
    fast = mesh.shape["dp"] == NZ * NX * NC and mesh.shape["tensor"] == NY
    return jax.shard_map(fast_shards if fast else shards, mesh=mesh, in_specs=in_specs, out_specs=out_specs, check_vma=False)
```

```python
import functools

import jax
import jax.numpy as jnp
from jax import lax
from jax.experimental import pallas as pl
from jax.experimental.pallas import tpu as pltpu
from jax.sharding import PartitionSpec as P

HEAD_DIM = 64
TSTEPS = 1000
LEN = 1024
BLOCK = 256
QBLK = 512


EPS = 1e-05
NEGATIVE = -1e30
HIGH = lax.Precision.HIGHEST
VMEM_LIMIT = 62 * 1024 * 1024


def layer_norm(hidden, gain, shift):
    average = jnp.mean(hidden, axis=-1, keepdims=True)
    centered = hidden - average
    variance = jnp.mean(centered * centered, axis=-1, keepdims=True)
    return centered * lax.rsqrt(variance + EPS) * gain + shift


def gather_rows(values):
    return lax.all_gather(values, "tensor", axis=0, tiled=True)


def sum_rows(values):
    return lax.psum_scatter(
        values.astype(jnp.bfloat16), "tensor", scatter_dimension=0, tiled=True
    ).astype(jnp.float32)


def fetch_attn(qkv_weight, out_weight):
    return (
        lax.all_gather(qkv_weight, "dp", axis=1, tiled=True),
        lax.all_gather(out_weight, "dp", axis=1, tiled=True),
    )


def fetch_mlp(up_weight, down_weight):
    return (
        lax.all_gather(up_weight, "dp", axis=0, tiled=True),
        lax.all_gather(down_weight, "dp", axis=1, tiled=True),
    )


def place_part(part, whole_len, offset):
    return lax.dynamic_update_slice_in_dim(jnp.zeros((whole_len,), jnp.float32), part, offset, 0)


def contract_rows(left, right):
    return lax.dot_general(
        left, right, (((0,), (0,)), ((), ())), preferred_element_type=jnp.float32
    )


def contract_cols(left, right):
    return lax.dot_general(
        left, right, (((1,), (1,)), ((), ())), preferred_element_type=jnp.float32
    )


def block_mask(start):
    query_pos = start + jnp.arange(QBLK)
    key_pos = jnp.arange(LEN)
    return query_pos[:, None] // BLOCK >= key_pos[None, :] // BLOCK


def split_heads(values):
    return values.reshape(values.shape[0], values.shape[1] // HEAD_DIM, HEAD_DIM)


def masked_scores(query_heads, key_heads, start, scale):
    scores = (
        jnp.einsum("qhd,khd->hqk", query_heads, key_heads, preferred_element_type=jnp.float32)
        * scale
    )
    return jnp.where(block_mask(start)[None], scores, NEGATIVE)


def block_slices(queries, keys_all, values_all, index):
    per_seq = LEN // QBLK
    seq_start = index // per_seq * LEN
    start = index % per_seq * QBLK
    query_blk = lax.dynamic_slice_in_dim(queries, seq_start + start, QBLK, 0)
    key_seq = lax.dynamic_slice_in_dim(keys_all, seq_start, LEN, 0)
    value_seq = lax.dynamic_slice_in_dim(values_all, seq_start, LEN, 0)
    return (seq_start, start, query_blk, key_seq, value_seq)


def run_attention(queries, keys_all, values_all, scale):
    total_rows = queries.shape[0]

    def run_advance(carry, index):
        seq_start, start, query_blk, key_seq, value_seq = block_slices(
            queries, keys_all, values_all, index
        )
        scores = masked_scores(split_heads(query_blk), split_heads(key_seq), start, scale)
        largest = jnp.max(scores, axis=-1, keepdims=True)
        expo = jnp.exp(scores - largest)
        totals = jnp.sum(expo, axis=-1, keepdims=True)
        chances = (expo / totals).astype(jnp.bfloat16)
        log_total = (largest + jnp.log(totals))[..., 0]
        mixed = jnp.einsum(
            "hqk,khd->qhd", chances, split_heads(value_seq), preferred_element_type=jnp.float32
        )
        return (carry, (mixed.reshape(QBLK, -1).astype(jnp.bfloat16), log_total))

    unused, (mixed, log_total) = lax.scan(run_advance, 0, jnp.arange(total_rows // QBLK))
    return (mixed.reshape(total_rows, -1), log_total)


def attention_back(queries, keys_all, values_all, grad_mixed, log_total, scale):
    total_rows = queries.shape[0]
    zeros = jnp.zeros(queries.shape, jnp.float32)

    def attention_advance(carry, inputs):
        grad_keys, grad_values = carry
        index, log_blk = inputs
        seq_start, start, query_blk, key_seq, value_seq = block_slices(
            queries, keys_all, values_all, index
        )
        grad_blk = lax.dynamic_slice_in_dim(grad_mixed, seq_start + start, QBLK, 0)
        query_heads = split_heads(query_blk)
        key_heads = split_heads(key_seq)
        grad_heads = split_heads(grad_blk)
        scores = masked_scores(query_heads, key_heads, start, scale)
        chances = jnp.exp(scores - log_blk[..., None])
        grad_probs = jnp.einsum(
            "qhd,khd->hqk", grad_heads, split_heads(value_seq), preferred_element_type=jnp.float32
        )
        inner = jnp.sum(chances * grad_probs, axis=-1, keepdims=True)
        grad_scores = (chances * (grad_probs - inner)).astype(jnp.bfloat16)
        grad_query = (
            jnp.einsum("hqk,khd->qhd", grad_scores, key_heads, preferred_element_type=jnp.float32)
            * scale
        )
        grad_key = (
            jnp.einsum("hqk,qhd->khd", grad_scores, query_heads, preferred_element_type=jnp.float32)
            * scale
        )
        grad_value = jnp.einsum(
            "hqk,qhd->khd",
            chances.astype(jnp.bfloat16),
            grad_heads,
            preferred_element_type=jnp.float32,
        )
        old_keys = lax.dynamic_slice_in_dim(grad_keys, seq_start, LEN, 0)
        old_values = lax.dynamic_slice_in_dim(grad_values, seq_start, LEN, 0)
        grad_keys = lax.dynamic_update_slice_in_dim(
            grad_keys, old_keys + grad_key.reshape(LEN, -1), seq_start, 0
        )
        grad_values = lax.dynamic_update_slice_in_dim(
            grad_values, old_values + grad_value.reshape(LEN, -1), seq_start, 0
        )
        return ((grad_keys, grad_values), grad_query.reshape(QBLK, -1))

    (grad_keys, grad_values), grad_queries = lax.scan(
        attention_advance, (zeros, zeros), (jnp.arange(total_rows // QBLK), log_total)
    )
    return (grad_queries.reshape(total_rows, -1), grad_keys, grad_values)


def shards(
    tokens,
    timesteps,
    norm_gains,
    biases,
    second_shift,
    hidden_bias,
    step_table,
    qkv_weight,
    out_weight,
    up_weight,
    down_weight,
    cotangent,
):
    width = tokens.shape[1]
    half_width = qkv_weight.shape[2]
    half_hidden = up_weight.shape[1]
    slot = lax.axis_index("tensor")
    device = lax.axis_index(("dp", "tensor"))
    scale = HEAD_DIM ** (-0.5)
    gains_all, biases_all, second_all, hidden_all, table_all = (
        lax.all_gather(norm_gains, ("dp", "tensor"), axis=1, tiled=True),
        lax.all_gather(biases, ("dp", "tensor"), axis=1, tiled=True),
        lax.all_gather(second_shift, ("dp", "tensor"), axis=0, tiled=True),
        lax.all_gather(hidden_bias, ("dp", "tensor"), axis=0, tiled=True),
        lax.all_gather(step_table, ("dp", "tensor"), axis=1, tiled=True),
    )
    gains_all = gains_all.astype(jnp.float32)
    biases_all = biases_all.astype(jnp.float32)
    second_all = second_all.astype(jnp.float32)
    hidden_local = lax.dynamic_slice_in_dim(
        hidden_all.astype(jnp.float32), slot * half_hidden, half_hidden, 0
    )
    query_bias = lax.dynamic_slice_in_dim(biases_all[1], slot * half_width, half_width, 0)
    value_bias = lax.dynamic_slice_in_dim(biases_all[2], slot * half_width, half_width, 0)
    step_id = lax.dynamic_slice_in_dim(timesteps, device, 1, 0)
    picker = (step_id[:, None] == jnp.arange(TSTEPS)[None, :]).astype(jnp.bfloat16)
    embed = jnp.dot(picker, table_all, preferred_element_type=jnp.float32)
    start_h = tokens.astype(jnp.float32) + embed
    qkv_full, out_full = fetch_attn(qkv_weight, out_weight)
    up_full, down_full = fetch_mlp(up_weight, down_weight)
    normed = gather_rows(layer_norm(start_h, gains_all[0], biases_all[0]).astype(jnp.bfloat16))
    projected = jnp.einsum("rd,jde->jre", normed, qkv_full, preferred_element_type=jnp.float32)
    queries = (projected[0] + query_bias).astype(jnp.bfloat16)
    keys_all = projected[1].astype(jnp.bfloat16)
    values_all = (projected[2] + value_bias).astype(jnp.bfloat16)
    mixed, log_total = run_attention(queries, keys_all, values_all, scale)
    attn_out = (
        sum_rows(jnp.dot(mixed, out_full, preferred_element_type=jnp.float32)) + biases_all[3]
    )
    middle = start_h + attn_out
    second = gather_rows(layer_norm(middle, gains_all[1], second_all).astype(jnp.bfloat16))
    pre_act = jnp.dot(second, up_full, preferred_element_type=jnp.float32) + hidden_local
    activated = jax.nn.gelu(pre_act).astype(jnp.bfloat16)
    mlp_out = (
        sum_rows(jnp.dot(activated, down_full, preferred_element_type=jnp.float32)) + biases_all[4]
    )
    layer_out = (middle + mlp_out).astype(jnp.bfloat16)
    grad_top = cotangent.astype(jnp.float32)
    up_full, down_full = fetch_mlp(up_weight, down_weight)
    grad_mlp_all = gather_rows(cotangent)
    grad_downw = contract_rows(activated, grad_mlp_all)
    grad_act = contract_cols(grad_mlp_all, down_full)
    unused, gelu_back = jax.vjp(jax.nn.gelu, pre_act)
    grad_pre = gelu_back(grad_act)[0].astype(jnp.bfloat16)
    grad_upw = contract_rows(second, grad_pre)
    grad_hidden_local = jnp.sum(grad_pre.astype(jnp.float32), axis=0)
    grad_second = sum_rows(contract_cols(grad_pre, up_full))
    unused, second_back = jax.vjp(layer_norm, middle, gains_all[1], second_all)
    grad_mid_part, grad_gain_two, grad_shift_two = second_back(grad_second)
    grad_middle = grad_top + grad_mid_part
    grad_up, grad_down = (
        lax.psum_scatter(grad_upw, "dp", scatter_dimension=0, tiled=True),
        lax.psum_scatter(grad_downw, "dp", scatter_dimension=1, tiled=True),
    )
    qkv_full, out_full = fetch_attn(qkv_weight, out_weight)
    grad_attn = grad_middle.astype(jnp.bfloat16)
    grad_attn_all = gather_rows(grad_attn)
    grad_outw = contract_rows(mixed, grad_attn_all)
    grad_mixed = contract_cols(grad_attn_all, out_full).astype(jnp.bfloat16)
    grad_queries, grad_keys, grad_values = attention_back(
        queries, keys_all, values_all, grad_mixed, log_total, scale
    )
    grad_rows = jnp.stack([grad_queries, grad_keys, grad_values]).astype(jnp.bfloat16)
    grad_qkvw = jnp.einsum("rd,jre->jde", normed, grad_rows, preferred_element_type=jnp.float32)
    grad_normed = sum_rows(
        jnp.einsum("jre,jde->rd", grad_rows, qkv_full, preferred_element_type=jnp.float32)
    )
    unused, first_back = jax.vjp(layer_norm, start_h, gains_all[0], biases_all[0])
    grad_start_part, grad_gain_one, grad_shift_one = first_back(grad_normed)
    grad_tokens = grad_middle + grad_start_part
    grad_qkv, grad_out = (
        lax.psum_scatter(grad_qkvw, "dp", scatter_dimension=1, tiled=True),
        lax.psum_scatter(grad_outw, "dp", scatter_dimension=1, tiled=True),
    )
    row_sums = jnp.sum(grad_rows.astype(jnp.float32), axis=1)
    gain_terms = jnp.stack([grad_gain_one, grad_gain_two])
    bias_terms = jnp.stack(
        [
            grad_shift_one,
            place_part(row_sums[0], width, slot * half_width),
            place_part(row_sums[2], width, slot * half_width),
            jnp.sum(grad_attn.astype(jnp.float32), axis=0),
            jnp.sum(grad_top, axis=0),
        ]
    )
    hidden_terms = place_part(
        grad_hidden_local,
        hidden_bias.shape[0] * lax.axis_size(("dp", "tensor")),
        slot * half_hidden,
    )
    seq_grad = jnp.sum(grad_tokens, axis=0, keepdims=True)
    table_terms = lax.dot_general(
        picker.astype(jnp.float32),
        seq_grad,
        (((0,), (0,)), ((), ())),
        precision=HIGH,
        preferred_element_type=jnp.float32,
    )
    grad_gains, grad_biases, grad_shift, grad_hidden, grad_table = (
        lax.psum_scatter(gain_terms, ("dp", "tensor"), scatter_dimension=1, tiled=True),
        lax.psum_scatter(bias_terms, ("dp", "tensor"), scatter_dimension=1, tiled=True),
        lax.psum_scatter(grad_shift_two, ("dp", "tensor"), scatter_dimension=0, tiled=True),
        lax.psum_scatter(hidden_terms, ("dp", "tensor"), scatter_dimension=0, tiled=True),
        lax.psum_scatter(table_terms, ("dp", "tensor"), scatter_dimension=1, tiled=True),
    )
    return (
        layer_out,
        grad_tokens,
        grad_gains,
        grad_biases,
        grad_shift,
        grad_hidden,
        grad_table,
        grad_qkv,
        grad_out,
        grad_up,
        grad_down,
    )


MESH_ID = pl.DeviceIdType.MESH
F32, BF16 = jnp.float32, jnp.bfloat16
NZ, NX, NC, NY = 4, 2, 2, 2
QB = 256
LINE = 40
GELU_A, GELU_B = 0.7978845608028654, 0.044715


def nt(left, right):
    return lax.dot_general(left, right, (((1,), (1,)), ((), ())), preferred_element_type=F32)


def nn(left, right):
    return lax.dot_general(left, right, (((1,), (0,)), ((), ())), preferred_element_type=F32)


def tn(left, right):
    return lax.dot_general(left, right, (((0,), (0,)), ((), ())), preferred_element_type=F32)


def position():
    dp = lax.axis_index("dp")
    return (lax.axis_index("tensor"), dp // (NX * NC), lax.rem(dp // NC, NX), lax.rem(dp, NC))


def device_at(y, z, x, c):
    return (z * (NX * NC) + x * NC + c, y)


def across(z, k):
    return {1: z + 1 - 2 * lax.rem(z, 2), 2: lax.rem(z + 2, NZ), 3: NZ - 1 - z}[k]


FAR_FIRST = (3, 2, 1)


def plane_peers(pos):
    y, z, x, c = pos
    for flip in range(1, NY * NX * NC):
        to = (1 - y if flip & 4 else y, z, 1 - x if flip & 2 else x, 1 - c if flip & 1 else c)
        yield flip - 1, to


def greet(pos):
    y, z, x, c = pos
    peers = [device_at(y, across(z, k), x, c) for k in FAR_FIRST]
    peers += [device_at(*to) for _, to in plane_peers(pos)]
    barrier = pltpu.get_barrier_semaphore()
    for peer in peers:
        pl.semaphore_signal(barrier, inc=1, device_id=peer, device_id_type=MESH_ID)
    return lambda: pl.semaphore_wait(barrier, len(peers))


def at_step(index, events):
    for step, names in events.items():

        @pl.when(index == step)
        def _():
            for name in names:
                name()


def remote(src, dst, send, recv, index, peer):
    return pltpu.make_async_remote_copy(
        src_ref=src,
        dst_ref=dst,
        send_sem=send.at[index],
        recv_sem=recv.at[index],
        device_id=peer,
        device_id_type=MESH_ID,
    )


class Gather:
    def __init__(self, buf, cols, send, recv, pos):
        self.buf, self.cols, self.send, self.recv, self.pos = buf, cols, send, recv, pos

    def view(self, y, z, x, c):
        return self.buf.at[y, z, x, c, :, self.cols]

    def steps(self, step):
        y, z, x, c = self.pos
        lo, hi, both = pl.ds(0, 2), pl.ds(2, 2), pl.ds(0, 2)
        if step == 0:
            return [
                (k - 1, (y, z, x, c), (y, across(z, k), x, c), device_at(y, across(z, k), x, c)) for k in FAR_FIRST
            ]
        x_peer, y_peer = device_at(y, z, 1 - x, c), device_at(1 - y, z, x, c)
        if step == 1:
            return [(3, (y, lo, x, c), (y, lo, 1 - x, c), x_peer), (4, (y, hi, x, c), (1 - y, hi, x, c), y_peer)]
        if step == 2:
            return [
                (5, (y, lo, both, c), (1 - y, lo, both, c), y_peer),
                (6, (both, hi, x, c), (both, hi, 1 - x, c), x_peer),
            ]
        return [(7, (both, pl.ds(0, NZ), both, c), (both, pl.ds(0, NZ), both, 1 - c), device_at(y, z, x, 1 - c))]

    def start(self, step):
        for sem, src, _, peer in self.steps(step):
            remote(self.view(*src), self.view(*src), self.send, self.recv, sem, peer).start()

    def wait(self, step):
        for sem, _, dst, peer in self.steps(step):
            remote(self.view(*dst), self.view(*dst), self.send, self.recv, sem, peer).wait_recv()

    def next(self, step):
        self.wait(step)
        self.start(step + 1)

    count = 4
    order = (7, 3, 4, 5, 6, 0, 1, 2)

    def drain(self):
        for step in range(self.count):
            for sem, src, _, peer in self.steps(step):
                remote(self.view(*src), self.view(*src), self.send, self.recv, sem, peer).wait_send()


class PlaneGather(Gather):
    order = (10, 0, 1, 8, 9, 2, 4, 6)

    def view(self, y, z, x, c, part=2):
        start, size = self.cols
        if part < 2:
            start, size = start + part * (size // 2), size // 2
        return self.buf.at[y, z, x, c, :, pl.ds(start, size)]

    def steps(self, step):
        y, z, x, c = self.pos
        both, every = pl.ds(0, 2), pl.ds(0, NZ)
        x_peer, y_peer = device_at(y, z, 1 - x, c), device_at(1 - y, z, x, c)
        if step == 0:
            return [(0, (y, z, x, c, 0), (y, z, 1 - x, c, 0), x_peer), (1, (y, z, x, c, 1), (1 - y, z, x, c, 1), y_peer)]
        if step == 1:
            found = []
            for k in FAR_FIRST:
                peer, other = device_at(y, across(z, k), x, c), across(z, k)
                found.append((2 * k, (y, z, both, c, 0), (y, other, both, c, 0), peer))
                found.append((2 * k + 1, (both, z, x, c, 1), (both, other, x, c, 1), peer))
            return found
        if step == 2:
            return [
                (8, (y, every, both, c, 0), (1 - y, every, both, c, 0), y_peer),
                (9, (both, every, x, c, 1), (both, every, 1 - x, c, 1), x_peer),
            ]
        return [(10, (both, every, both, c), (both, every, both, 1 - c), device_at(y, z, x, 1 - c))]


class SmallGather(Gather):
    count = 2

    def __init__(self, buf, send, recv, pos):
        super().__init__(buf, None, send, recv, pos)

    def view(self, y, z, x, c):
        return self.buf.at[y, z, x, c]

    def steps(self, step):
        y, z, x, c = self.pos
        if step == 0:
            return super().steps(0)
        every = pl.ds(0, NZ)
        return [
            (3 + flip, (y, every, x, c), (to[0], every, to[2], to[3]), device_at(*to)) for flip, to in plane_peers(self.pos)
        ]


class SmallScatter:
    def __init__(self, source, acc, first, last, send, recv, pos):
        self.source, self.acc, self.first, self.last = source, acc, first, last
        self.send, self.recv, self.pos = send, recv, pos

    def copies(self, step):
        y, z, x, c = self.pos
        every = pl.ds(0, NZ)
        if step == 0:
            return [
                remote(
                    self.source.at[to[0], every, to[2], to[3]],
                    self.first.at[flip],
                    self.send,
                    self.recv,
                    3 + flip,
                    device_at(*to),
                )
                for flip, to in plane_peers(self.pos)
            ]
        return [
            remote(
                self.acc.at[across(z, k)],
                self.last.at[k - 1],
                self.send,
                self.recv,
                k - 1,
                device_at(y, across(z, k), x, c),
            )
            for k in FAR_FIRST
        ]

    def start(self, step):
        for copy in self.copies(step):
            copy.start()

    def next(self):
        y, z, x, c = self.pos
        total = self.source[y, :, x, c]
        for flip, copy in enumerate(self.copies(0)):
            copy.wait_recv()
            total = total + self.first[flip]
        self.acc[...] = total
        self.start(1)

    def final(self):
        total = self.acc[self.pos[1]]
        for copy in self.copies(1):
            copy.wait_recv()
        for k in range(NZ - 1):
            total = total + self.last[k]
        return total

    def drain(self):
        for step in range(2):
            for copy in self.copies(step):
                copy.wait_send()


def small_scratch():
    tile = (8, 128)
    return [
        pltpu.VMEM((NY, NZ, NX, NC, *tile), F32),
        pltpu.VMEM((NZ, *tile), F32),
        pltpu.VMEM((NY * NX * NC - 1, NZ, *tile), F32),
        pltpu.VMEM((NZ - 1, *tile), F32),
    ]


def fold(values):
    return values[0:8] + pltpu.roll(values[8:16], LINE, 1) + pltpu.roll(values[16:24], 2 * LINE, 1)


def unfold(tile):
    return jnp.concatenate([tile, pltpu.roll(tile, 128 - LINE, 1), pltpu.roll(tile, 128 - 2 * LINE, 1)], axis=0)


def gelu_parts(v):
    square = v * v
    half = 0.5 + 0.5 * jnp.tanh(v * (GELU_A + (GELU_A * GELU_B) * square))
    act = v * half
    slope = half + (2.0 * act) * (1.0 - half) * (GELU_A + (3 * GELU_A * GELU_B) * square)
    return act, slope


def moments(hidden):
    average = jnp.mean(hidden, axis=-1, keepdims=True)
    centered = hidden - average
    variance = jnp.mean(centered * centered, axis=-1, keepdims=True)
    scale = lax.rsqrt(variance + EPS)
    return centered * scale, scale


def norm_back(xhat, scale, grad):
    return (grad - jnp.mean(grad, axis=-1, keepdims=True) - xhat * jnp.mean(grad * xhat, axis=-1, keepdims=True)) * scale


def row_block(index, size):
    return pl.ds(pl.multiple_of(index * size, size), size)


def sum_rows_of(values):
    return jnp.sum(values.astype(F32), axis=0, keepdims=True)


def blocks():
    for z in range(NZ):
        for x in range(NX):
            for c in range(NC):
                for y in range(NY):
                    yield (z * NX + x) * NC * NY + c * NY + y, (y, z, x, c)


class Scatter:
    def __init__(self, source, own, bufs, send, recv, pos, order):
        self.source, self.own, self.bufs = source, own, bufs
        self.send, self.recv, self.pos, self.order = send, recv, pos, order

    def copies(self, step):
        y, z, x, c = self.pos
        first, second_x, second_y, third_y, third_x, last = self.bufs
        own = self.own
        lo, hi, both = pl.ds(0, 2), pl.ds(2, 2), pl.ds(0, 2)
        x_peer, y_peer = device_at(y, z, 1 - x, c), device_at(1 - y, z, x, c)
        sem = self.order
        if step == 0:
            return [(sem[0], self.source.at[both, pl.ds(0, NZ), both, 1 - c], first, device_at(y, z, x, 1 - c))]
        if step == 1:
            return [
                (sem[1], own.at[both, lo, 1 - x], second_x, x_peer),
                (sem[2], own.at[1 - y, hi, both], second_y, y_peer),
            ]
        if step == 2:
            return [(sem[3], own.at[1 - y, lo, x], third_y, y_peer), (sem[4], own.at[y, hi, 1 - x], third_x, x_peer)]
        return [
            (sem[4 + k], own.at[y, across(z, k), x], last.at[k - 1], device_at(y, across(z, k), x, c))
            for k in FAR_FIRST
        ]

    def start(self, step):
        for sem, src, dst, peer in self.copies(step):
            remote(src, dst, self.send, self.recv, sem, peer).start()

    def wait(self, step):
        for sem, src, dst, peer in self.copies(step):
            remote(src, dst, self.send, self.recv, sem, peer).wait_recv()

    def add(self, step):
        y, z, x, c = self.pos
        own, source = self.own, self.source
        first, second_x, second_y, third_y, third_x, last = self.bufs
        kind = own.dtype

        def plus(left, right):
            return (left.astype(F32) + right.astype(F32)).astype(kind)

        def each(count, body):
            def run(i, _):
                body(i)
                return 0

            lax.fori_loop(0, count, run, 0)

        if step == 0:

            def body(i):
                iy, iz, ix = i // (NZ * NX), lax.rem(i // NX, NZ), lax.rem(i, NX)
                own[iy, iz, ix] = plus(source[iy, iz, ix, c], first[iy, iz, ix])

            each(NY * NZ * NX, body)
        elif step == 1:

            def body(i):
                a, b = i // 2, lax.rem(i, 2)
                own[a, b, x] = plus(own[a, b, x], second_x[a, b])
                own[y, 2 + a, b] = plus(own[y, 2 + a, b], second_y[a, b])

            each(4, body)
        else:

            def body(i):
                own[y, i, x] = plus(own[y, i, x], third_y[i])
                own[y, 2 + i, x] = plus(own[y, 2 + i, x], third_x[i])

            each(2, body)

    def first_sum(self):
        self.wait(0)
        self.add(0)
        self.sent(0)

    def next(self, step):
        if step == 0:
            self.first_sum()
        else:
            self.wait(step)
            self.add(step)
        self.start(step + 1)

    def sent(self, step):
        for sem, src, dst, peer in self.copies(step):
            remote(src, dst, self.send, self.recv, sem, peer).wait_send()

    def final(self):
        y, z, x, c = self.pos
        last = self.bufs[5]
        self.wait(3)
        total = self.own[y, z, x].astype(F32)
        for k in range(NZ - 1):
            total = total + last[k].astype(F32)
        return total

    def drain(self):
        for step in range(1, 4):
            self.sent(step)


def scatter_scratch(per, width, kind):
    return [
        pltpu.VMEM((NY, NZ, NX, per, width), kind),
        pltpu.VMEM((2, 2, per, width), kind),
        pltpu.VMEM((2, 2, per, width), kind),
        pltpu.VMEM((2, per, width), kind),
        pltpu.VMEM((2, per, width), kind),
        pltpu.VMEM((NZ - 1, per, width), kind),
    ]


def layer_kernel(
    dims,
    steps,
    gains,
    biases,
    shift2,
    hidden,
    table_t,
    tokens_in,
    qkv_in,
    outw_t,
    upw_in,
    downw_t,
    cot_in,
    gpack_out,
    gup_out,
    gdown_out,
    gout_out,
    gqkv_out,
    gtok_out,
    layer_out,
    middle_hbm,
    small_out,
    lse_out,
    ghid_out,
    full,
    pack,
    lines,
    stage,
    tokens,
    cot,
    normed,
    queries,
    keys_all,
    values_all,
    mixed,
    second,
    second_t,
    cot_t,
    result,
    gsec,
    act,
    gpre,
    gtile,
    hid,
    acc,
    inner,
    sums,
    gup,
    gdown,
    gout,
    gqkv,
    *rest,
):
    rows, width, per, half, ffh, ft = dims
    pos = position()
    y, z, x, c = pos
    me = device_at(y, z, x, c)[0] * NY + y
    share = width // (NZ * NX * NC * NY)
    n_ff = ffh // ft
    send, recv, local = rest[-3:]

    n_groups = half // 128
    groups = [f"g{i}" for i in range(n_groups)]
    names = ["pack", "hid", *groups, "o"] + [f"m{i}" for i in range(n_ff)]
    col = {"o": pl.ds(3 * half, half)}
    for i in range(n_groups):
        col[f"g{i}"] = pl.ds(i * 384, 384)
    for i in range(n_ff):
        col[f"m{i}"] = pl.ds(4 * half + 2 * ft * i, 2 * ft)
    flow, used = {}, 0
    for name in names:
        count = {"pack": 10, "hid": 10, "m1": 11}.get(name, 8)
        sems = (send.at[pl.ds(used, count)], recv.at[pl.ds(used, count)], pos)
        used += count
        if name == "m1":
            flow[name] = PlaneGather(full, (4 * half + 2 * ft, 2 * ft), *sems)
        elif name in col:
            flow[name] = Gather(full, col[name], *sems)
        else:
            flow[name] = SmallGather({"pack": pack, "hid": lines}[name], *sems)
    ready = greet(pos)
    copies = {}

    def copy(name, src, dst):
        copies[name] = pltpu.make_async_copy(src, dst, local.at[len(copies)])
        copies[name].start()

    def own(start, size):
        return full.at[y, z, x, c, :, pl.ds(start, size)]

    parts = {"pack": [], "hid": []}
    for g in range(n_groups):
        parts[f"g{g}"] = [f"g{g}{i}" for i in range(3)]
        for i in range(3):
            copy(f"g{g}{i}", qkv_in.at[i, :, pl.ds(128 * g, 128)], own(384 * g + 128 * i, 128))
    copy("cot", cot_in, cot)
    copy("tokens", tokens_in, tokens)
    copy("o", outw_t, own(3 * half, half))
    parts["o"] = ["o"]
    for i in range(n_ff):
        copy(f"u{i}", upw_in.at[:, pl.ds(ft * i, ft)], own(4 * half + 2 * ft * i, ft))
        copy(f"d{i}", downw_t.at[:, pl.ds(ft * i, ft)], own(4 * half + 2 * ft * i + ft, ft))
        parts[f"m{i}"] = [f"u{i}", f"d{i}"]

    def launch(name):
        for key in parts[name]:
            copies[key].wait()
        flow[name].start(0)

    stage[...] = jnp.zeros_like(stage)
    stage[0:2, 0:share] = gains[...].astype(F32)
    stage[2:7, 0:share] = biases[...].astype(F32)
    stage[7:8, 0:share] = shift2[...].astype(F32)
    n_steps, n_seq = table_t.shape[1], steps.shape[1]
    wanted = jnp.concatenate([steps[...], jnp.full((1, 128 - n_seq), -1, jnp.int32)], axis=1)
    picked = (wanted == lax.broadcasted_iota(jnp.int32, (n_steps, 128), 0)).astype(BF16)
    pack[y, z, x, c] = fold(stage[...].T[0:share] + pltpu.roll(nn(table_t[...], picked), 8, 1))
    hshare = hidden.shape[1]
    lane = lax.broadcasted_iota(jnp.int32, (hshare, NC * NY * hshare), 0) + hshare * (c * NY + y)
    place = (lane == lax.broadcasted_iota(jnp.int32, (hshare, NC * NY * hshare), 1)).astype(BF16)
    spread = nn(jnp.broadcast_to(hidden[...], (8, hshare)), place)
    n_hid = NC * NY * hshare // 128
    pieces = [spread[0:1, 128 * j : 128 * j + 128] for j in range(n_hid)]
    lines[y, z, x, c] = jnp.concatenate([*pieces, jnp.zeros((8 - n_hid, 128), F32)], axis=0)

    ready()
    launch("pack")
    launch("g0")
    copies["cot"].wait()

    def turn_cot(i, total):
        rb = row_block(i, 256)
        block = cot[rb, :]
        cot_t[:, rb] = block.T
        return total + sum_rows_of(block)

    csum = lax.fori_loop(0, rows // 256, turn_cot, jnp.zeros((1, width), F32))
    sums[...] = jnp.zeros_like(sums)
    sums[6:7, :] = csum
    flow["pack"].next(0)
    flow["g0"].next(0)
    launch("g1")
    flow["g0"].next(1)
    flow["pack"].wait(1)
    flow["g1"].next(0)
    launch("g2")
    launch("hid")
    launch("o")

    for d, (by, bz, bx, bc) in blocks():
        result[d * share : d * share + share, 0:128] = unfold(pack[by, bz, bx, bc])
    small_out[...] = result[0:width, 0:128].T
    embed = small_out[pl.ds(8 + me, 1), :]
    copies["tokens"].wait()

    def first_norm(i, _):
        rb = row_block(i, 128)
        xhat, _ = moments(tokens[rb, :].astype(F32) + embed)
        normed[rb, :] = (xhat * small_out[0:1, :] + small_out[2:3, :]).astype(BF16)
        return 0

    lax.fori_loop(0, rows // 128, first_norm, 0)
    flow["g0"].next(2)
    flow["g1"].next(1)
    flow["g2"].next(0)
    launch("m0")
    launch("m1")

    def whole(cols, size):
        return jnp.concatenate([full[by, :, :, :, :, cols].reshape(width, size) for by in range(NY)], axis=1)

    def project(group):
        cols = pl.ds(pl.multiple_of(group * 384, 128), 384)

        def body(i, _):
            rb = row_block(i, 512)
            value = nn(normed[rb, :], whole(cols, 384))
            for by in range(NY):
                to = pl.ds(pl.multiple_of((by * n_groups + group) * 128, 128), 128)
                piece = [value[:, by * 384 + 128 * j : by * 384 + 128 * j + 128] for j in range(3)]
                queries[rb, to] = (piece[0] + small_out[3:4, to]).astype(BF16) * jnp.asarray(HEAD_DIM**-0.5, BF16)
                keys_all[rb, to] = piece[1].astype(BF16)
                values_all[rb, to] = (piece[2] + small_out[4:5, to]).astype(BF16)
            return 0

        lax.fori_loop(0, rows // 512, body, 0)

    def then(name, step):
        return lambda: flow[name].next(step)

    def back(name, step):
        return lambda: sums_of[name].next(step)

    def arrived(name):
        return lambda: flow[name].wait(3)

    def off(name):
        return lambda: launch(name)

    events = {
        1: [then("g1", 2), then("g2", 1), then("o", 0), then("hid", 0)],
        3: [then("g2", 2), then("o", 1)],
        4: [then("m0", 1)],
        5: [then("o", 2)],
    }
    between = {1: [then("m0", 0)]}

    def attend(s, _):
        group, by = s // NY, lax.rem(s, NY)
        p = by * n_groups + group

        @pl.when(by == 0)
        def _():
            at_step(group, {1: [then("m1", 0)]})
            at_step(group, {g: [arrived(f"g{g}")] for g in range(n_groups)})
            project(group)
            at_step(group, between)

        at_step(s, events)
        cols = pl.ds(pl.multiple_of(p * 128, 128), 128)
        low = lax.broadcasted_iota(jnp.int32, (QB, 128), 1) < HEAD_DIM
        for i in range(rows // QB):
            n = (i + 1) * QB
            rb = slice(i * QB, n)
            key, value, query = keys_all[0:n, cols], values_all[0:n, cols], queries[rb, cols]
            outs, scales = [], []
            for h in range(2):
                scores = nt(key, jnp.where(low == (h == 0), query, jnp.zeros_like(query)))
                top = jnp.max(scores, axis=0, keepdims=True)
                expo = jnp.exp(scores - top)
                total = jnp.sum(expo, axis=0, keepdims=True)
                lse_out[pl.ds(2 * p + h, 1), rb] = top + jnp.log(total)
                scales.append(jnp.broadcast_to(1.0 / total, (HEAD_DIM, QB)))
                outs.append(tn(expo.astype(BF16), value))
            scale = jnp.concatenate(scales, axis=0).T
            mixed[rb, cols] = (jnp.where(low, outs[0], outs[1]) * scale).astype(BF16)
        return 0

    lax.fori_loop(0, width // 128, attend, 0)
    flow["o"].wait(3)
    launch("m2")
    flow["hid"].wait(1)
    for bz in range(NZ):
        for bx in range(NX):
            total = lines[0, bz, bx, 0] + lines[0, bz, bx, 1] + lines[1, bz, bx, 0] + lines[1, bz, bx, 1]
            for j in range(n_hid):
                at = ((bz * NX + bx) * n_hid + j) * 128
                hid[0:1, at : at + 128] = total[j : j + 1]

    at = len(copies)

    def middle_save(i):
        rb = row_block(i, 256)
        return pltpu.make_async_copy(result.at[rb], middle_hbm.at[rb], local.at[at + 10 + i])

    def second_norm(i, _):
        at_step(i, {2: [then("m0", 2)]})
        rb = row_block(i, 256)
        start_h = tokens[rb, :].astype(F32) + embed
        value = start_h + (nt(mixed[rb, :], whole(col["o"], half)) + small_out[5:6, :])
        result[rb, :] = value
        middle_save(i).start()
        gsec[rb, :] = jnp.zeros_like(value)
        xhat, _ = moments(value)
        block = (xhat * small_out[1:2, :] + small_out[7:8, :]).astype(BF16)
        second[rb, :] = block
        second_t[:, rb] = block.T
        return 0

    lax.fori_loop(0, rows // 256, second_norm, 0)
    flow["m1"].next(1)
    flow["m0"].wait(3)
    for i in range(rows // 256):
        middle_save(i).wait()

    free = 4 * half
    half_f = 2 * ft
    places = {"m0": (0, free, half_f), "m1": (1, free, half_f), "m2": (0, free + half_f, half_f), "o": (1, free + half_f, half)}
    for g in range(n_groups):
        places[f"q{g}"] = (g % 2, free + 2 * half_f + 384 * (g // 2), 384)
    sums_of = {}
    before = {"m0": "g0", "m1": "g1", "m2": "g2", "o": "o", "q0": "m0", "q1": "m2", "q2": "m1", "pack": "pack", "hid": "hid"}
    for i, name in enumerate([*places, "pack", "hid"]):
        gather = flow[before[name]]
        sems = (gather.send, gather.recv, pos)
        if name in places:
            core, start, size = places[name]
            own_view = full.at[:, :, :, core, :, pl.ds(start, size)]
            bufs = rest[6 * i : 6 * i + 6]
            if name[0] == "m":
                source = gtile
            else:
                source = gtile.at[:, :, :, :, :, pl.ds(0 if name in ("o", "q1") else half, 384)]
            sums_of[name] = Scatter(source, own_view, bufs, *sems, gather.order)
        else:
            sums_of[name] = SmallScatter(*(rest[-11:-7] if name == "pack" else rest[-7:-3]), *sems)
    tiles = NY * n_ff

    def tile(t, _):
        ty, tm = lax.rem(t, NY), t // NY
        slot = lax.rem(t, 2)

        def begin(name):
            return lambda: sums_of[name].start(0)

        def first_sum(name):
            return lambda: sums_of[name].first_sum()

        def second_step(name):
            return lambda: sums_of[name].start(1)

        at_step(
            t,
            {
                1: [then("m2", 0)],
                2: [flow["g0"].drain, begin("m0"), flow["m0"].drain, then("m2", 1), arrived("m1")],
                4: [flow["g1"].drain, begin("m1"), arrived("m2")],
            },
        )

        up_at = pl.ds(pl.multiple_of(4 * half + tm * 2 * ft, 128), ft)
        down_at = pl.ds(pl.multiple_of(4 * half + tm * 2 * ft + ft, 128), ft)
        hid_at = pl.ds(pl.multiple_of(ty * ffh + tm * ft, 128), ft)

        def up():
            return full[ty, :, :, :, :, up_at].reshape(width, ft)

        def down():
            return full[ty, :, :, :, :, down_at].reshape(width, ft)

        pre = nn(second[...], up()) + hid[:, hid_at]
        gact = nn(cot[...], down())
        value, slope = gelu_parts(pre)
        act[...] = value.astype(BF16)
        grad = (gact * slope).astype(BF16)
        gpre[...] = grad
        ghid_out[:, hid_at] = sum_rows_of(grad)
        result[...] += nt(act[...], down())
        gsec[...] += nt(gpre[...], up())

        def results():
            second[...] = (result[...] + small_out[6:7, :]).astype(BF16)
            layer_save.start()
            middle_load.start()

        at_step(
            t,
            {
                1: [then("m1", 2)],
                2: [first_sum("m0")],
                3: [then("m2", 2), second_step("m0")],
                4: [first_sum("m1"), second_step("m1")],
                tiles - 1: [results, back("m0", 1)],
            },
        )

        turn = (NZ, NX, NC, per, ft)
        gtile[slot, :, :, :, :, 0:ft] = nn(second_t[...], gpre[...]).astype(BF16).reshape(turn)
        gtile[slot, :, :, :, :, ft : 2 * ft] = nn(cot_t[...], act[...]).astype(BF16).reshape(turn)
        return 0

    layer_save = pltpu.make_async_copy(second, layer_out, local.at[at + 5])
    middle_load = pltpu.make_async_copy(middle_hbm, result, local.at[at + 6])
    lax.fori_loop(0, tiles, tile, 0)
    for name in ("g2", "m1", "m2", "hid"):
        flow[name].drain()
    sums_of["m2"].start(0)
    reload = [
        pltpu.make_async_copy(tokens_in.at[:, pl.ds(0, ft)], act, local.at[at + 7]),
        pltpu.make_async_copy(tokens_in.at[:, pl.ds(ft, width - ft)], gpre.at[:, pl.ds(0, width - ft)], local.at[at + 8]),
    ]
    for load in reload:
        load.start()
    for d, (by, bz, bx, bc) in blocks():
        start = (bz * NX + bx) * n_hid
        pieces = [ghid_out[:, 128 * (start + j) : 128 * (start + j + 1)] for j in range(n_hid)]
        sums_of["hid"].source[by, bz, bx, bc] = jnp.concatenate([*pieces, jnp.zeros((8 - n_hid, 128), F32)], axis=0)
    sums_of["hid"].start(0)
    layer_save.wait()
    middle_load.wait()
    gattn, gattn_t, normed_t, gmixed = second, cot_t, second_t, tokens
    gq, gk, gv = second, normed, cot
    def second_back(i, totals):
        rb = row_block(i, 128)
        xhat, scale = moments(result[rb, :])
        grad = gsec[rb, :]
        total = cot[rb, :].astype(F32) + norm_back(xhat, scale, grad * small_out[1:2, :])
        gsec[rb, :] = total
        low = total.astype(BF16)
        gattn[rb, :] = low
        gattn_t[:, rb] = low.T
        return (
            totals[0] + sum_rows_of(grad * xhat),
            totals[1] + sum_rows_of(grad),
            totals[2] + sum_rows_of(low),
        )

    zero = jnp.zeros((1, width), F32)
    ggain2, gshift2, gattn_sum = lax.fori_loop(0, rows // 128, second_back, (zero, zero, zero))
    sums[1:2, :] = ggain2
    sums[5:6, :] = gattn_sum
    sums[7:8, :] = gshift2

    def weight(index):
        picks = [
            full[by, :, :, :, :, pl.ds(384 * g + 128 * index, 128)].reshape(width, 128)
            for by in range(NY)
            for g in range(n_groups)
        ]
        return jnp.concatenate(picks, axis=1)

    flow["pack"].drain()
    flow["o"].drain()
    sums_of["m1"].next(1)
    sums_of["m2"].next(0)

    def out_grad(i, _):
        part = nn(gattn_t[row_block(i, 384), :], mixed[...]).astype(BF16)
        for by in range(NY):
            to = part[:, by * half : by * half + half].reshape(2, NX, NC, per, half)
            gtile[by, pl.ds(i * 2, 2), :, :, :, 0:half] = to
        return 0

    lax.fori_loop(0, width // 384, out_grad, 0)
    sums_of["o"].start(0)
    sums_of["m0"].next(2)

    def mixed_grad(i, _):
        rb = row_block(i, 512)
        gmixed[rb, :] = nn(gattn[rb, :], whole(col["o"], half)).astype(BF16)
        return 0

    lax.fori_loop(0, rows // 512, mixed_grad, 0)
    sums_of["o"].next(0)

    def turn_normed(i, _):
        rb = row_block(i, 256)
        normed_t[:, rb] = normed[rb, :].T
        return 0

    lax.fori_loop(0, rows // 256, turn_normed, 0)
    events_back = {
        1: [back("m1", 2)],
        2: [back("m2", 1)],
        3: [back("q0", 0), back("o", 1), sums_of["hid"].next],
        4: [back("m2", 2), back("q0", 1)],
        5: [back("o", 2), back("q0", 2), back("q1", 0)],
    }

    def attend_back(s, _):
        group, by = s // NY, lax.rem(s, NY)
        p = by * n_groups + group
        at_step(s, events_back)
        cols = pl.ds(pl.multiple_of(p * 128, 128), 128)
        dots = (gmixed[:, cols].astype(F32) * mixed[:, cols].astype(F32)).T
        for h in range(2):
            inner[h : h + 1, :] = jnp.sum(dots[HEAD_DIM * h : HEAD_DIM * (h + 1)], axis=0, keepdims=True)
        for j in range(rows // QB):
            kb, first = slice(j * QB, (j + 1) * QB), j * QB
            later = rows - first
            key, value = keys_all[kb, cols], values_all[kb, cols]
            low = lax.broadcasted_iota(jnp.int32, (later, 128), 1) < HEAD_DIM

            def two(block):
                none = jnp.zeros_like(block)
                return jnp.concatenate([jnp.where(low, block, none), jnp.where(low, none, block)], axis=0)

            query, grad = two(queries[first:rows, cols]), two(gmixed[first:rows, cols])
            logs = jnp.concatenate([lse_out[pl.ds(2 * p + h, 1), first:rows] for h in range(2)], axis=1)
            inners = jnp.concatenate([inner[h : h + 1, first:rows] for h in range(2)], axis=1)
            probs = jnp.exp(nt(key, query) - logs)
            gscores = (probs * (nt(value, grad) - inners)).astype(BF16)
            gv[kb, cols] = nn(probs.astype(BF16), grad).astype(BF16)
            gk[kb, cols] = nn(gscores, query).astype(BF16)
            both = tn(gscores, key)
            more = jnp.where(low, both[:later], both[later:])
            if j == 0:
                acc[...] = more
            else:
                acc[first:rows] += more
        gq[:, cols] = (acc[...] * HEAD_DIM**-0.5).astype(BF16)

        @pl.when(by == NY - 1)
        def _():
            offset = lax.rem(group + 1, 2) * half
            for piece, source in enumerate((gq, gk, gv)):
                pick = jnp.concatenate(
                    [source[:, pl.ds(pl.multiple_of((b * n_groups + group) * 128, 128), 128)] for b in range(NY)], axis=1
                )
                part = nn(normed_t[...], pick).astype(BF16)
                for b in range(NY):
                    to = pl.ds(pl.multiple_of(offset + piece * 128, 128), 128)
                    gtile[b, :, :, :, :, to] = part[:, b * 128 : b * 128 + 128].reshape(NZ, NX, NC, per, 128)
            at_step(group, {g: [lambda g=g: sums_of[f"q{g}"].start(0)] for g in range(n_groups)})
            at_step(group, {n_groups - 1: [back("q1", 1)]})

        return 0

    lax.fori_loop(0, NY * n_groups, attend_back, 0)
    for load in reload:
        load.wait()

    def m_final(i):
        def run():
            total = sums_of[f"m{i}"].final()
            gup[:, ft * i : ft * i + ft] = total[:, 0:ft]
            gdown[:, ft * i : ft * i + ft] = total[:, ft:]

        return run

    owners = {}
    for i, (name, src, dst) in enumerate([("gup", gup, gup_out), ("gdown", gdown, gdown_out), ("gout", gout, gout_out), ("gqkv", gqkv, gqkv_out)]):
        owners[name] = pltpu.make_async_copy(src, dst, local.at[at + 14 + i])

    def first_back(i, totals):
        rb = row_block(i, 256)
        block = jnp.concatenate([act[rb, :], gpre[rb, 0 : width - ft]], axis=1)
        xhat, scale = moments(block.astype(F32) + embed)
        q_rows, k_rows, v_rows = gq[rb, :], gk[rb, :], gv[rb, :]
        grad = nt(q_rows, weight(0)) + nt(k_rows, weight(1)) + nt(v_rows, weight(2))
        total = gsec[rb, :] + norm_back(xhat, scale, grad * small_out[0:1, :])
        mixed[rb, :] = total.astype(BF16)

        at_step(
            i,
            {0: [back("q2", 0)], 1: [m_final(0), back("q1", 2)], 2: [back("q2", 1), m_final(1)]},
        )
        return (
            totals[0] + sum_rows_of(grad * xhat),
            totals[1] + sum_rows_of(grad),
            totals[2] + sum_rows_of(q_rows),
            totals[3] + sum_rows_of(v_rows),
            totals[4] + sum_rows_of(total),
        )

    ggain1, gshift1, q_sum, v_sum, seq_sum = lax.fori_loop(0, rows // 256, first_back, (zero,) * 5)
    sums[0:1, :] = ggain1
    sums[2:3, :] = gshift1
    sums[3:4, :] = q_sum
    sums[4:5, :] = v_sum
    sums[pl.ds(8 + me, 1), :] = seq_sum
    gtok = pltpu.make_async_copy(mixed, gtok_out, local.at[at + 9])
    gtok.start()
    turned = sums[...].T
    for d, (by, bz, bx, bc) in blocks():
        sums_of["pack"].source[by, bz, bx, bc] = fold(turned[d * share : d * share + share])
    sums_of["pack"].start(0)
    last = f"q{n_groups - 1}"
    sums_of[last].next(2)
    for i in range(2, n_ff):
        m_final(i)()
    owners["gup"].start()
    owners["gdown"].start()
    sums_of["pack"].next()
    gout[...] = sums_of["o"].final()
    owners["gout"].start()
    gpack_out[8:16] = sums_of["hid"].final()

    def qkv_final(g):
        total = sums_of[f"q{g}"].final()
        for piece in range(3):
            gqkv[piece, :, 128 * g : 128 * g + 128] = total[:, 128 * piece : 128 * piece + 128]

    for g in range(n_groups - 1):
        qkv_final(g)
    for name, each in sums_of.items():
        if name not in ("pack", last):
            each.drain()
    qkv_final(n_groups - 1)
    owners["gqkv"].start()
    gpack_out[0:8] = sums_of["pack"].final()
    gtok.wait()
    sums_of[last].drain()
    sums_of["pack"].drain()
    for each in owners.values():
        each.wait()


def finish_kernel(slots, count, steps, gpack, *refs):
    large, (gains_out, biases_out, shift_out, hidden_out, table_out) = refs[:count], refs[count : count + 5]
    outs, rest = refs[count + 5 : 2 * count + 5], refs[2 * count + 5 :]
    bufs, wide, (load_sem, save_sem) = rest[:count], rest[count], rest[-2:]
    pieces = []
    for src, buf, out in zip(large, bufs, outs):
        cut = 4 if src.shape[0] % 512 == 0 else 1
        size = src.shape[0] // cut
        for k in range(cut):
            at, n = pl.ds(k * size, size), len(pieces)
            held = buf if src.dtype == out.dtype else wide
            load = pltpu.make_async_copy(src.at[at], buf.at[at], load_sem.at[n])
            pieces.append((load, pltpu.make_async_copy(held.at[at], out.at[at], save_sem.at[n]), held is wide and at))
    for load, _, _ in pieces:
        load.start()
    share, hshare = gains_out.shape[1], hidden_out.shape[1]
    features = unfold(gpack[0:8, :])
    turned = jnp.concatenate([features, jnp.zeros((128 - share, 128), F32)], axis=0).T
    gains_out[...] = turned[0:2, 0:share]
    biases_out[...] = turned[2:7, 0:share]
    shift_out[...] = turned[7:8, 0:share]
    slot = lax.rem(lax.axis_index("dp"), NC) * NY + lax.axis_index("tensor")
    line = jnp.concatenate([gpack[8 + j : 9 + j, :] for j in range(slots * hshare // 128)], axis=1)
    value = line[:, 0:hshare]
    for k in range(1, slots):
        value = jnp.where(slot == k, line[:, hshare * k : hshare * k + hshare], value)
    hidden_out[...] = value
    for load, save, at in pieces:
        load.wait()
        if at:
            wide[at, :] = bufs[0][at, :].astype(F32)
        save.start()
    n_steps, n_seq = table_out.shape[1], steps.shape[1]
    picked = (steps[...] == lax.broadcasted_iota(jnp.int32, (n_steps, n_seq), 0)).astype(F32)
    table_out[...] = lax.dot_general(
        features[:, 8 : 8 + n_seq], picked, (((1,), (1,)), ((), ())), precision=HIGH, preferred_element_type=F32
    )
    for _, save, _ in pieces:
        save.wait()


def fast_shards(
    tokens,
    timesteps,
    norm_gains,
    biases,
    second_shift,
    hidden_bias,
    step_table,
    qkv_weight,
    out_weight,
    up_weight,
    down_weight,
    cotangent,
):
    rows, width = tokens.shape
    _, per, half = qkv_weight.shape
    ffh = up_weight.shape[1]
    ft = 512
    dims = (rows, width, per, half, ffh, ft)
    n_ff, n_groups = ffh // ft, half // 128
    total = 4 * half + 2 * ffh
    vmem, anywhere = pl.BlockSpec(memory_space=pltpu.VMEM), pl.BlockSpec(memory_space=pl.ANY)
    shape = jax.ShapeDtypeStruct
    low, wide = shape((rows, width), BF16), shape((rows, width), F32)
    vm = pltpu.VMEM
    hshare = hidden_bias.shape[0]
    steps = timesteps.reshape(1, -1)
    chunks = [2 * ft] * n_ff + [half] * (1 + n_groups)
    scratch = []
    for cols in chunks:
        scratch += scatter_scratch(per, cols, BF16)
    n_sems = 2 * 10 + 8 * (n_groups + n_ff) + 11
    owned = [shape((per, ffh), F32), shape((per, ffh), F32), shape((per, half), F32), shape((3, per, half), F32)]
    gpack, gup, gdown, gout, gqkv, gtok, layer, _ = pl.pallas_call(
        functools.partial(layer_kernel, dims),
        in_specs=[vmem] * 6 + [anywhere] * 6,
        out_specs=[vmem] + [anywhere] * 7,
        out_shape=[
            shape((16, 128), F32),
            *owned,
            low,
            low,
            wide,
        ],
        scratch_shapes=[
            vm((128, width), F32),
            vm((16, rows), F32),
            vm((1, NY * ffh), F32),
            vm((NY, NZ, NX, NC, per, total), BF16),
            vm((NY, NZ, NX, NC, 8, 128), F32),
            vm((NY, NZ, NX, NC, 8, 128), F32),
            vm((128, 128), F32),
            vm((rows, width), BF16),
            vm((rows, width), BF16),
            vm((rows, width), BF16),
            vm((rows, width), BF16),
            vm((rows, width), BF16),
            vm((rows, width), BF16),
            vm((rows, width), BF16),
            vm((rows, width), BF16),
            vm((width, rows), BF16),
            vm((width, rows), BF16),
            vm((rows, width), F32),
            vm((rows, width), F32),
            vm((rows, ft), BF16),
            vm((rows, ft), BF16),
            vm((2, NZ, NX, NC, per, 2 * ft), BF16),
            vm((1, NY * ffh), F32),
            vm((rows, 128), F32),
            vm((8, rows), F32),
            vm((128, width), F32),
            *[vm(each.shape, F32) for each in owned],
            *scratch,
            *small_scratch(),
            *small_scratch(),
            pltpu.SemaphoreType.DMA((n_sems,)),
            pltpu.SemaphoreType.DMA((n_sems,)),
            pltpu.SemaphoreType.DMA((24 + 3 * n_groups + 2 * n_ff,)),
        ],
        compiler_params=pltpu.CompilerParams(collective_id=0, has_side_effects=True, vmem_limit_bytes=VMEM_LIMIT),
        name="layer",
    )(
        steps,
        norm_gains,
        biases,
        second_shift.reshape(1, -1),
        hidden_bias.reshape(1, -1),
        step_table.T,
        tokens,
        qkv_weight,
        out_weight.T,
        up_weight,
        down_weight.T,
        cotangent,
    )
    share, n_steps = norm_gains.shape[1], step_table.shape[0]
    large = (gtok, layer, gqkv, gout, gup, gdown)
    pieces = sum(4 if array.shape[0] % 512 == 0 else 1 for array in large)
    small_shapes = [(2, share), (5, share), (1, share), (1, hshare), (share, n_steps)]
    large_shapes = [wide, *[shape(array.shape, array.dtype) for array in large[1:]]]
    grad_gains, grad_biases, grad_shift, grad_hidden, grad_table, gtok, layer, gqkv, gout, gup, gdown = pl.pallas_call(
        functools.partial(finish_kernel, NC * NY, len(large)),
        in_specs=[vmem] * 2 + [anywhere] * len(large),
        out_specs=[vmem] * 5 + [anywhere] * len(large),
        out_shape=[shape(dims, F32) for dims in small_shapes] + large_shapes,
        scratch_shapes=[vm(array.shape, array.dtype) for array in large]
        + [vm(wide.shape, F32)]
        + [pltpu.SemaphoreType.DMA((pieces,))] * 2,
        name="finish",
    )(steps, gpack, *large)
    return (
        layer,
        gtok,
        grad_gains,
        grad_biases,
        grad_shift.reshape(share),
        grad_hidden.reshape(hshare),
        grad_table.T,
        gqkv,
        gout.T,
        gup,
        gdown.T,
    )


def solution(mesh):
    in_specs = (
        P(("dp", "tensor"), None),
        P(),
        P(None, ("dp", "tensor")),
        P(None, ("dp", "tensor")),
        P(("dp", "tensor")),
        P(("dp", "tensor")),
        P(None, ("dp", "tensor")),
        P(None, "dp", "tensor"),
        P("tensor", "dp"),
        P("dp", "tensor"),
        P("tensor", "dp"),
        P(("dp", "tensor"), None),
    )
    out_specs = (
        P(("dp", "tensor"), None),
        P(("dp", "tensor"), None),
        P(None, ("dp", "tensor")),
        P(None, ("dp", "tensor")),
        P(("dp", "tensor")),
        P(("dp", "tensor")),
        P(None, ("dp", "tensor")),
        P(None, "dp", "tensor"),
        P("tensor", "dp"),
        P("dp", "tensor"),
        P("tensor", "dp"),
    )
    fast = mesh.shape["dp"] == NZ * NX * NC and mesh.shape["tensor"] == NY
    return jax.shard_map(fast_shards if fast else shards, mesh=mesh, in_specs=in_specs, out_specs=out_specs, check_vma=False)
```

```python
import functools

import jax
import jax.numpy as jnp
from jax import lax
from jax.experimental import pallas as pl
from jax.experimental.pallas import tpu as pltpu
from jax.sharding import PartitionSpec as P

HEAD_DIM = 64
TSTEPS = 1000
LEN = 1024
BLOCK = 256
QBLK = 512


EPS = 1e-05
NEGATIVE = -1e30
HIGH = lax.Precision.HIGHEST
VMEM_LIMIT = 62 * 1024 * 1024


def layer_norm(hidden, gain, shift):
    average = jnp.mean(hidden, axis=-1, keepdims=True)
    centered = hidden - average
    variance = jnp.mean(centered * centered, axis=-1, keepdims=True)
    return centered * lax.rsqrt(variance + EPS) * gain + shift


def gather_rows(values):
    return lax.all_gather(values, "tensor", axis=0, tiled=True)


def sum_rows(values):
    return lax.psum_scatter(
        values.astype(jnp.bfloat16), "tensor", scatter_dimension=0, tiled=True
    ).astype(jnp.float32)


def fetch_attn(qkv_weight, out_weight):
    return (
        lax.all_gather(qkv_weight, "dp", axis=1, tiled=True),
        lax.all_gather(out_weight, "dp", axis=1, tiled=True),
    )


def fetch_mlp(up_weight, down_weight):
    return (
        lax.all_gather(up_weight, "dp", axis=0, tiled=True),
        lax.all_gather(down_weight, "dp", axis=1, tiled=True),
    )


def place_part(part, whole_len, offset):
    return lax.dynamic_update_slice_in_dim(jnp.zeros((whole_len,), jnp.float32), part, offset, 0)


def contract_rows(left, right):
    return lax.dot_general(
        left, right, (((0,), (0,)), ((), ())), preferred_element_type=jnp.float32
    )


def contract_cols(left, right):
    return lax.dot_general(
        left, right, (((1,), (1,)), ((), ())), preferred_element_type=jnp.float32
    )


def block_mask(start):
    query_pos = start + jnp.arange(QBLK)
    key_pos = jnp.arange(LEN)
    return query_pos[:, None] // BLOCK >= key_pos[None, :] // BLOCK


def split_heads(values):
    return values.reshape(values.shape[0], values.shape[1] // HEAD_DIM, HEAD_DIM)


def masked_scores(query_heads, key_heads, start, scale):
    scores = (
        jnp.einsum("qhd,khd->hqk", query_heads, key_heads, preferred_element_type=jnp.float32)
        * scale
    )
    return jnp.where(block_mask(start)[None], scores, NEGATIVE)


def block_slices(queries, keys_all, values_all, index):
    per_seq = LEN // QBLK
    seq_start = index // per_seq * LEN
    start = index % per_seq * QBLK
    query_blk = lax.dynamic_slice_in_dim(queries, seq_start + start, QBLK, 0)
    key_seq = lax.dynamic_slice_in_dim(keys_all, seq_start, LEN, 0)
    value_seq = lax.dynamic_slice_in_dim(values_all, seq_start, LEN, 0)
    return (seq_start, start, query_blk, key_seq, value_seq)


def run_attention(queries, keys_all, values_all, scale):
    total_rows = queries.shape[0]

    def run_advance(carry, index):
        seq_start, start, query_blk, key_seq, value_seq = block_slices(
            queries, keys_all, values_all, index
        )
        scores = masked_scores(split_heads(query_blk), split_heads(key_seq), start, scale)
        largest = jnp.max(scores, axis=-1, keepdims=True)
        expo = jnp.exp(scores - largest)
        totals = jnp.sum(expo, axis=-1, keepdims=True)
        chances = (expo / totals).astype(jnp.bfloat16)
        log_total = (largest + jnp.log(totals))[..., 0]
        mixed = jnp.einsum(
            "hqk,khd->qhd", chances, split_heads(value_seq), preferred_element_type=jnp.float32
        )
        return (carry, (mixed.reshape(QBLK, -1).astype(jnp.bfloat16), log_total))

    unused, (mixed, log_total) = lax.scan(run_advance, 0, jnp.arange(total_rows // QBLK))
    return (mixed.reshape(total_rows, -1), log_total)


def attention_back(queries, keys_all, values_all, grad_mixed, log_total, scale):
    total_rows = queries.shape[0]
    zeros = jnp.zeros(queries.shape, jnp.float32)

    def attention_advance(carry, inputs):
        grad_keys, grad_values = carry
        index, log_blk = inputs
        seq_start, start, query_blk, key_seq, value_seq = block_slices(
            queries, keys_all, values_all, index
        )
        grad_blk = lax.dynamic_slice_in_dim(grad_mixed, seq_start + start, QBLK, 0)
        query_heads = split_heads(query_blk)
        key_heads = split_heads(key_seq)
        grad_heads = split_heads(grad_blk)
        scores = masked_scores(query_heads, key_heads, start, scale)
        chances = jnp.exp(scores - log_blk[..., None])
        grad_probs = jnp.einsum(
            "qhd,khd->hqk", grad_heads, split_heads(value_seq), preferred_element_type=jnp.float32
        )
        inner = jnp.sum(chances * grad_probs, axis=-1, keepdims=True)
        grad_scores = (chances * (grad_probs - inner)).astype(jnp.bfloat16)
        grad_query = (
            jnp.einsum("hqk,khd->qhd", grad_scores, key_heads, preferred_element_type=jnp.float32)
            * scale
        )
        grad_key = (
            jnp.einsum("hqk,qhd->khd", grad_scores, query_heads, preferred_element_type=jnp.float32)
            * scale
        )
        grad_value = jnp.einsum(
            "hqk,qhd->khd",
            chances.astype(jnp.bfloat16),
            grad_heads,
            preferred_element_type=jnp.float32,
        )
        old_keys = lax.dynamic_slice_in_dim(grad_keys, seq_start, LEN, 0)
        old_values = lax.dynamic_slice_in_dim(grad_values, seq_start, LEN, 0)
        grad_keys = lax.dynamic_update_slice_in_dim(
            grad_keys, old_keys + grad_key.reshape(LEN, -1), seq_start, 0
        )
        grad_values = lax.dynamic_update_slice_in_dim(
            grad_values, old_values + grad_value.reshape(LEN, -1), seq_start, 0
        )
        return ((grad_keys, grad_values), grad_query.reshape(QBLK, -1))

    (grad_keys, grad_values), grad_queries = lax.scan(
        attention_advance, (zeros, zeros), (jnp.arange(total_rows // QBLK), log_total)
    )
    return (grad_queries.reshape(total_rows, -1), grad_keys, grad_values)


def shards(
    tokens,
    timesteps,
    norm_gains,
    biases,
    second_shift,
    hidden_bias,
    step_table,
    qkv_weight,
    out_weight,
    up_weight,
    down_weight,
    cotangent,
):
    width = tokens.shape[1]
    half_width = qkv_weight.shape[2]
    half_hidden = up_weight.shape[1]
    slot = lax.axis_index("tensor")
    device = lax.axis_index(("dp", "tensor"))
    scale = HEAD_DIM ** (-0.5)
    gains_all, biases_all, second_all, hidden_all, table_all = (
        lax.all_gather(norm_gains, ("dp", "tensor"), axis=1, tiled=True),
        lax.all_gather(biases, ("dp", "tensor"), axis=1, tiled=True),
        lax.all_gather(second_shift, ("dp", "tensor"), axis=0, tiled=True),
        lax.all_gather(hidden_bias, ("dp", "tensor"), axis=0, tiled=True),
        lax.all_gather(step_table, ("dp", "tensor"), axis=1, tiled=True),
    )
    gains_all = gains_all.astype(jnp.float32)
    biases_all = biases_all.astype(jnp.float32)
    second_all = second_all.astype(jnp.float32)
    hidden_local = lax.dynamic_slice_in_dim(
        hidden_all.astype(jnp.float32), slot * half_hidden, half_hidden, 0
    )
    query_bias = lax.dynamic_slice_in_dim(biases_all[1], slot * half_width, half_width, 0)
    value_bias = lax.dynamic_slice_in_dim(biases_all[2], slot * half_width, half_width, 0)
    step_id = lax.dynamic_slice_in_dim(timesteps, device, 1, 0)
    picker = (step_id[:, None] == jnp.arange(TSTEPS)[None, :]).astype(jnp.bfloat16)
    embed = jnp.dot(picker, table_all, preferred_element_type=jnp.float32)
    start_h = tokens.astype(jnp.float32) + embed
    qkv_full, out_full = fetch_attn(qkv_weight, out_weight)
    up_full, down_full = fetch_mlp(up_weight, down_weight)
    normed = gather_rows(layer_norm(start_h, gains_all[0], biases_all[0]).astype(jnp.bfloat16))
    projected = jnp.einsum("rd,jde->jre", normed, qkv_full, preferred_element_type=jnp.float32)
    queries = (projected[0] + query_bias).astype(jnp.bfloat16)
    keys_all = projected[1].astype(jnp.bfloat16)
    values_all = (projected[2] + value_bias).astype(jnp.bfloat16)
    mixed, log_total = run_attention(queries, keys_all, values_all, scale)
    attn_out = (
        sum_rows(jnp.dot(mixed, out_full, preferred_element_type=jnp.float32)) + biases_all[3]
    )
    middle = start_h + attn_out
    second = gather_rows(layer_norm(middle, gains_all[1], second_all).astype(jnp.bfloat16))
    pre_act = jnp.dot(second, up_full, preferred_element_type=jnp.float32) + hidden_local
    activated = jax.nn.gelu(pre_act).astype(jnp.bfloat16)
    mlp_out = (
        sum_rows(jnp.dot(activated, down_full, preferred_element_type=jnp.float32)) + biases_all[4]
    )
    layer_out = (middle + mlp_out).astype(jnp.bfloat16)
    grad_top = cotangent.astype(jnp.float32)
    up_full, down_full = fetch_mlp(up_weight, down_weight)
    grad_mlp_all = gather_rows(cotangent)
    grad_downw = contract_rows(activated, grad_mlp_all)
    grad_act = contract_cols(grad_mlp_all, down_full)
    unused, gelu_back = jax.vjp(jax.nn.gelu, pre_act)
    grad_pre = gelu_back(grad_act)[0].astype(jnp.bfloat16)
    grad_upw = contract_rows(second, grad_pre)
    grad_hidden_local = jnp.sum(grad_pre.astype(jnp.float32), axis=0)
    grad_second = sum_rows(contract_cols(grad_pre, up_full))
    unused, second_back = jax.vjp(layer_norm, middle, gains_all[1], second_all)
    grad_mid_part, grad_gain_two, grad_shift_two = second_back(grad_second)
    grad_middle = grad_top + grad_mid_part
    grad_up, grad_down = (
        lax.psum_scatter(grad_upw, "dp", scatter_dimension=0, tiled=True),
        lax.psum_scatter(grad_downw, "dp", scatter_dimension=1, tiled=True),
    )
    qkv_full, out_full = fetch_attn(qkv_weight, out_weight)
    grad_attn = grad_middle.astype(jnp.bfloat16)
    grad_attn_all = gather_rows(grad_attn)
    grad_outw = contract_rows(mixed, grad_attn_all)
    grad_mixed = contract_cols(grad_attn_all, out_full).astype(jnp.bfloat16)
    grad_queries, grad_keys, grad_values = attention_back(
        queries, keys_all, values_all, grad_mixed, log_total, scale
    )
    grad_rows = jnp.stack([grad_queries, grad_keys, grad_values]).astype(jnp.bfloat16)
    grad_qkvw = jnp.einsum("rd,jre->jde", normed, grad_rows, preferred_element_type=jnp.float32)
    grad_normed = sum_rows(
        jnp.einsum("jre,jde->rd", grad_rows, qkv_full, preferred_element_type=jnp.float32)
    )
    unused, first_back = jax.vjp(layer_norm, start_h, gains_all[0], biases_all[0])
    grad_start_part, grad_gain_one, grad_shift_one = first_back(grad_normed)
    grad_tokens = grad_middle + grad_start_part
    grad_qkv, grad_out = (
        lax.psum_scatter(grad_qkvw, "dp", scatter_dimension=1, tiled=True),
        lax.psum_scatter(grad_outw, "dp", scatter_dimension=1, tiled=True),
    )
    row_sums = jnp.sum(grad_rows.astype(jnp.float32), axis=1)
    gain_terms = jnp.stack([grad_gain_one, grad_gain_two])
    bias_terms = jnp.stack(
        [
            grad_shift_one,
            place_part(row_sums[0], width, slot * half_width),
            place_part(row_sums[2], width, slot * half_width),
            jnp.sum(grad_attn.astype(jnp.float32), axis=0),
            jnp.sum(grad_top, axis=0),
        ]
    )
    hidden_terms = place_part(
        grad_hidden_local,
        hidden_bias.shape[0] * lax.axis_size(("dp", "tensor")),
        slot * half_hidden,
    )
    seq_grad = jnp.sum(grad_tokens, axis=0, keepdims=True)
    table_terms = lax.dot_general(
        picker.astype(jnp.float32),
        seq_grad,
        (((0,), (0,)), ((), ())),
        precision=HIGH,
        preferred_element_type=jnp.float32,
    )
    grad_gains, grad_biases, grad_shift, grad_hidden, grad_table = (
        lax.psum_scatter(gain_terms, ("dp", "tensor"), scatter_dimension=1, tiled=True),
        lax.psum_scatter(bias_terms, ("dp", "tensor"), scatter_dimension=1, tiled=True),
        lax.psum_scatter(grad_shift_two, ("dp", "tensor"), scatter_dimension=0, tiled=True),
        lax.psum_scatter(hidden_terms, ("dp", "tensor"), scatter_dimension=0, tiled=True),
        lax.psum_scatter(table_terms, ("dp", "tensor"), scatter_dimension=1, tiled=True),
    )
    return (
        layer_out,
        grad_tokens,
        grad_gains,
        grad_biases,
        grad_shift,
        grad_hidden,
        grad_table,
        grad_qkv,
        grad_out,
        grad_up,
        grad_down,
    )


MESH_ID = pl.DeviceIdType.MESH
F32, BF16 = jnp.float32, jnp.bfloat16
NZ, NX, NC, NY = 4, 2, 2, 2
QB = 256
LINE = 40
GELU_A, GELU_B = 0.7978845608028654, 0.044715


def nt(left, right):
    return lax.dot_general(left, right, (((1,), (1,)), ((), ())), preferred_element_type=F32)


def nn(left, right):
    return lax.dot_general(left, right, (((1,), (0,)), ((), ())), preferred_element_type=F32)


def tn(left, right):
    return lax.dot_general(left, right, (((0,), (0,)), ((), ())), preferred_element_type=F32)


def position():
    dp = lax.axis_index("dp")
    return (lax.axis_index("tensor"), dp // (NX * NC), lax.rem(dp // NC, NX), lax.rem(dp, NC))


def device_at(y, z, x, c):
    return (z * (NX * NC) + x * NC + c, y)


def across(z, k):
    return {1: z + 1 - 2 * lax.rem(z, 2), 2: lax.rem(z + 2, NZ), 3: NZ - 1 - z}[k]


FAR_FIRST = (3, 2, 1)


def plane_peers(pos):
    y, z, x, c = pos
    for flip in range(1, NY * NX * NC):
        to = (1 - y if flip & 4 else y, z, 1 - x if flip & 2 else x, 1 - c if flip & 1 else c)
        yield flip - 1, to


def greet(pos):
    y, z, x, c = pos
    peers = [device_at(y, across(z, k), x, c) for k in FAR_FIRST]
    peers += [device_at(*to) for _, to in plane_peers(pos)]
    barrier = pltpu.get_barrier_semaphore()
    for peer in peers:
        pl.semaphore_signal(barrier, inc=1, device_id=peer, device_id_type=MESH_ID)
    return lambda: pl.semaphore_wait(barrier, len(peers))


def at_step(index, events):
    for step, names in events.items():

        @pl.when(index == step)
        def _():
            for name in names:
                name()


def remote(src, dst, send, recv, index, peer):
    return pltpu.make_async_remote_copy(
        src_ref=src,
        dst_ref=dst,
        send_sem=send.at[index],
        recv_sem=recv.at[index],
        device_id=peer,
        device_id_type=MESH_ID,
    )


class Gather:
    def __init__(self, buf, cols, send, recv, pos):
        self.buf, self.cols, self.send, self.recv, self.pos = buf, cols, send, recv, pos

    def view(self, y, z, x, c):
        return self.buf.at[y, z, x, c, :, self.cols]

    def steps(self, step):
        y, z, x, c = self.pos
        lo, hi, both = pl.ds(0, 2), pl.ds(2, 2), pl.ds(0, 2)
        if step == 0:
            return [
                (k - 1, (y, z, x, c), (y, across(z, k), x, c), device_at(y, across(z, k), x, c)) for k in FAR_FIRST
            ]
        x_peer, y_peer = device_at(y, z, 1 - x, c), device_at(1 - y, z, x, c)
        if step == 1:
            return [(3, (y, lo, x, c), (y, lo, 1 - x, c), x_peer), (4, (y, hi, x, c), (1 - y, hi, x, c), y_peer)]
        if step == 2:
            return [
                (5, (y, lo, both, c), (1 - y, lo, both, c), y_peer),
                (6, (both, hi, x, c), (both, hi, 1 - x, c), x_peer),
            ]
        return [(7, (both, pl.ds(0, NZ), both, c), (both, pl.ds(0, NZ), both, 1 - c), device_at(y, z, x, 1 - c))]

    def start(self, step):
        for sem, src, _, peer in self.steps(step):
            remote(self.view(*src), self.view(*src), self.send, self.recv, sem, peer).start()

    def wait(self, step):
        for sem, _, dst, peer in self.steps(step):
            remote(self.view(*dst), self.view(*dst), self.send, self.recv, sem, peer).wait_recv()

    def next(self, step):
        self.wait(step)
        self.start(step + 1)

    count = 4
    order = (7, 3, 4, 5, 6, 0, 1, 2)

    def drain(self):
        for step in range(self.count):
            for sem, src, _, peer in self.steps(step):
                remote(self.view(*src), self.view(*src), self.send, self.recv, sem, peer).wait_send()


class PlaneGather(Gather):
    order = (10, 0, 1, 8, 9, 2, 4, 6)

    def view(self, y, z, x, c, part=2):
        start, size = self.cols
        if part < 2:
            start, size = start + part * (size // 2), size // 2
        return self.buf.at[y, z, x, c, :, pl.ds(start, size)]

    def steps(self, step):
        y, z, x, c = self.pos
        both, every = pl.ds(0, 2), pl.ds(0, NZ)
        x_peer, y_peer = device_at(y, z, 1 - x, c), device_at(1 - y, z, x, c)
        if step == 0:
            return [(0, (y, z, x, c, 0), (y, z, 1 - x, c, 0), x_peer), (1, (y, z, x, c, 1), (1 - y, z, x, c, 1), y_peer)]
        if step == 1:
            found = []
            for k in FAR_FIRST:
                peer, other = device_at(y, across(z, k), x, c), across(z, k)
                found.append((2 * k, (y, z, both, c, 0), (y, other, both, c, 0), peer))
                found.append((2 * k + 1, (both, z, x, c, 1), (both, other, x, c, 1), peer))
            return found
        if step == 2:
            return [
                (8, (y, every, both, c, 0), (1 - y, every, both, c, 0), y_peer),
                (9, (both, every, x, c, 1), (both, every, 1 - x, c, 1), x_peer),
            ]
        return [(10, (both, every, both, c), (both, every, both, 1 - c), device_at(y, z, x, 1 - c))]


class SmallGather(Gather):
    count = 2

    def __init__(self, buf, send, recv, pos):
        super().__init__(buf, None, send, recv, pos)

    def view(self, y, z, x, c):
        return self.buf.at[y, z, x, c]

    def steps(self, step):
        y, z, x, c = self.pos
        if step == 0:
            return super().steps(0)
        every = pl.ds(0, NZ)
        return [
            (3 + flip, (y, every, x, c), (to[0], every, to[2], to[3]), device_at(*to)) for flip, to in plane_peers(self.pos)
        ]


class SmallScatter:
    def __init__(self, source, acc, first, last, send, recv, pos):
        self.source, self.acc, self.first, self.last = source, acc, first, last
        self.send, self.recv, self.pos = send, recv, pos

    def copies(self, step):
        y, z, x, c = self.pos
        every = pl.ds(0, NZ)
        if step == 0:
            return [
                remote(
                    self.source.at[to[0], every, to[2], to[3]],
                    self.first.at[flip],
                    self.send,
                    self.recv,
                    3 + flip,
                    device_at(*to),
                )
                for flip, to in plane_peers(self.pos)
            ]
        return [
            remote(
                self.acc.at[across(z, k)],
                self.last.at[k - 1],
                self.send,
                self.recv,
                k - 1,
                device_at(y, across(z, k), x, c),
            )
            for k in FAR_FIRST
        ]

    def start(self, step):
        for copy in self.copies(step):
            copy.start()

    def next(self):
        y, z, x, c = self.pos
        total = self.source[y, :, x, c]
        for flip, copy in enumerate(self.copies(0)):
            copy.wait_recv()
            total = total + self.first[flip]
        self.acc[...] = total
        self.start(1)

    def final(self):
        total = self.acc[self.pos[1]]
        for copy in self.copies(1):
            copy.wait_recv()
        for k in range(NZ - 1):
            total = total + self.last[k]
        return total

    def drain(self):
        for step in range(2):
            for copy in self.copies(step):
                copy.wait_send()


def small_scratch():
    tile = (8, 128)
    return [
        pltpu.VMEM((NY, NZ, NX, NC, *tile), F32),
        pltpu.VMEM((NZ, *tile), F32),
        pltpu.VMEM((NY * NX * NC - 1, NZ, *tile), F32),
        pltpu.VMEM((NZ - 1, *tile), F32),
    ]


def fold(values):
    return values[0:8] + pltpu.roll(values[8:16], LINE, 1) + pltpu.roll(values[16:24], 2 * LINE, 1)


def unfold(tile):
    return jnp.concatenate([tile, pltpu.roll(tile, 128 - LINE, 1), pltpu.roll(tile, 128 - 2 * LINE, 1)], axis=0)


def gelu_parts(v):
    square = v * v
    half = 0.5 + 0.5 * jnp.tanh(v * (GELU_A + (GELU_A * GELU_B) * square))
    act = v * half
    slope = half + (2.0 * act) * (1.0 - half) * (GELU_A + (3 * GELU_A * GELU_B) * square)
    return act, slope


def moments(hidden):
    average = jnp.mean(hidden, axis=-1, keepdims=True)
    centered = hidden - average
    variance = jnp.mean(centered * centered, axis=-1, keepdims=True)
    scale = lax.rsqrt(variance + EPS)
    return centered * scale, scale


def norm_back(xhat, scale, grad):
    return (grad - jnp.mean(grad, axis=-1, keepdims=True) - xhat * jnp.mean(grad * xhat, axis=-1, keepdims=True)) * scale


def row_block(index, size):
    return pl.ds(pl.multiple_of(index * size, size), size)


def sum_rows_of(values):
    return jnp.sum(values.astype(F32), axis=0, keepdims=True)


def blocks():
    for z in range(NZ):
        for x in range(NX):
            for c in range(NC):
                for y in range(NY):
                    yield (z * NX + x) * NC * NY + c * NY + y, (y, z, x, c)


class Scatter:
    def __init__(self, source, own, bufs, send, recv, pos, order):
        self.source, self.own, self.bufs = source, own, bufs
        self.send, self.recv, self.pos, self.order = send, recv, pos, order

    def copies(self, step):
        y, z, x, c = self.pos
        first, second_x, second_y, third_y, third_x, last = self.bufs
        own = self.own
        lo, hi, both = pl.ds(0, 2), pl.ds(2, 2), pl.ds(0, 2)
        x_peer, y_peer = device_at(y, z, 1 - x, c), device_at(1 - y, z, x, c)
        sem = self.order
        if step == 0:
            return [(sem[0], self.source.at[both, pl.ds(0, NZ), both, 1 - c], first, device_at(y, z, x, 1 - c))]
        if step == 1:
            return [
                (sem[1], own.at[both, lo, 1 - x], second_x, x_peer),
                (sem[2], own.at[1 - y, hi, both], second_y, y_peer),
            ]
        if step == 2:
            return [(sem[3], own.at[1 - y, lo, x], third_y, y_peer), (sem[4], own.at[y, hi, 1 - x], third_x, x_peer)]
        return [
            (sem[4 + k], own.at[y, across(z, k), x], last.at[k - 1], device_at(y, across(z, k), x, c))
            for k in FAR_FIRST
        ]

    def start(self, step):
        for sem, src, dst, peer in self.copies(step):
            remote(src, dst, self.send, self.recv, sem, peer).start()

    def wait(self, step):
        for sem, src, dst, peer in self.copies(step):
            remote(src, dst, self.send, self.recv, sem, peer).wait_recv()

    def add(self, step):
        y, z, x, c = self.pos
        own, source = self.own, self.source
        first, second_x, second_y, third_y, third_x, last = self.bufs
        kind = own.dtype

        def plus(left, right):
            return (left.astype(F32) + right.astype(F32)).astype(kind)

        def each(count, body):
            def run(i, _):
                body(i)
                return 0

            lax.fori_loop(0, count, run, 0)

        if step == 0:

            def body(i):
                iy, iz, ix = i // (NZ * NX), lax.rem(i // NX, NZ), lax.rem(i, NX)
                own[iy, iz, ix] = plus(source[iy, iz, ix, c], first[iy, iz, ix])

            each(NY * NZ * NX, body)
        elif step == 1:

            def body(i):
                a, b = i // 2, lax.rem(i, 2)
                own[a, b, x] = plus(own[a, b, x], second_x[a, b])
                own[y, 2 + a, b] = plus(own[y, 2 + a, b], second_y[a, b])

            each(4, body)
        else:

            def body(i):
                own[y, i, x] = plus(own[y, i, x], third_y[i])
                own[y, 2 + i, x] = plus(own[y, 2 + i, x], third_x[i])

            each(2, body)

    def first_sum(self):
        self.wait(0)
        self.add(0)
        self.sent(0)

    def next(self, step):
        if step == 0:
            self.first_sum()
        else:
            self.wait(step)
            self.add(step)
        self.start(step + 1)

    def sent(self, step):
        for sem, src, dst, peer in self.copies(step):
            remote(src, dst, self.send, self.recv, sem, peer).wait_send()

    def final(self):
        y, z, x, c = self.pos
        last = self.bufs[5]
        self.wait(3)
        total = self.own[y, z, x].astype(F32)
        for k in range(NZ - 1):
            total = total + last[k].astype(F32)
        return total

    def drain(self):
        for step in range(1, 4):
            self.sent(step)


def scatter_scratch(per, width, kind):
    return [
        pltpu.VMEM((NY, NZ, NX, per, width), kind),
        pltpu.VMEM((2, 2, per, width), kind),
        pltpu.VMEM((2, 2, per, width), kind),
        pltpu.VMEM((2, per, width), kind),
        pltpu.VMEM((2, per, width), kind),
        pltpu.VMEM((NZ - 1, per, width), kind),
    ]


def layer_kernel(
    dims,
    steps,
    gains,
    biases,
    shift2,
    hidden,
    table_t,
    tokens_in,
    qkv_in,
    outw_t,
    upw_in,
    downw_t,
    cot_in,
    gpack_out,
    gup_out,
    gdown_out,
    gout_out,
    gqkv_out,
    gtok_out,
    layer_out,
    middle_hbm,
    small_out,
    lse_out,
    ghid_out,
    full,
    pack,
    lines,
    stage,
    tokens,
    cot,
    normed,
    queries,
    keys_all,
    values_all,
    mixed,
    second,
    second_t,
    cot_t,
    result,
    gsec,
    act,
    gpre,
    gtile,
    hid,
    acc,
    inner,
    sums,
    gup,
    gdown,
    gout,
    gqkv,
    *rest,
):
    rows, width, per, half, ffh, ft = dims
    pos = position()
    y, z, x, c = pos
    me = device_at(y, z, x, c)[0] * NY + y
    share = width // (NZ * NX * NC * NY)
    n_ff = ffh // ft
    send, recv, local = rest[-3:]

    n_groups = half // 128
    groups = [f"g{i}" for i in range(n_groups)]
    names = ["pack", "hid", *groups, "o"] + [f"m{i}" for i in range(n_ff)]
    col = {"o": pl.ds(3 * half, half)}
    for i in range(n_groups):
        col[f"g{i}"] = pl.ds(i * 384, 384)
    for i in range(n_ff):
        col[f"m{i}"] = pl.ds(4 * half + 2 * ft * i, 2 * ft)
    flow, used = {}, 0
    for name in names:
        count = {"pack": 10, "hid": 10, "m1": 11}.get(name, 8)
        sems = (send.at[pl.ds(used, count)], recv.at[pl.ds(used, count)], pos)
        used += count
        if name == "m1":
            flow[name] = PlaneGather(full, (4 * half + 2 * ft, 2 * ft), *sems)
        elif name in col:
            flow[name] = Gather(full, col[name], *sems)
        else:
            flow[name] = SmallGather({"pack": pack, "hid": lines}[name], *sems)
    ready = greet(pos)
    copies = {}

    def copy(name, src, dst):
        copies[name] = pltpu.make_async_copy(src, dst, local.at[len(copies)])
        copies[name].start()

    def own(start, size):
        return full.at[y, z, x, c, :, pl.ds(start, size)]

    parts = {"pack": [], "hid": []}
    for g in range(n_groups):
        parts[f"g{g}"] = [f"g{g}{i}" for i in range(3)]
        for i in range(3):
            copy(f"g{g}{i}", qkv_in.at[i, :, pl.ds(128 * g, 128)], own(384 * g + 128 * i, 128))
    copy("cot", cot_in, cot)
    copy("tokens", tokens_in, tokens)
    copy("o", outw_t, own(3 * half, half))
    parts["o"] = ["o"]
    for i in range(n_ff):
        copy(f"u{i}", upw_in.at[:, pl.ds(ft * i, ft)], own(4 * half + 2 * ft * i, ft))
        copy(f"d{i}", downw_t.at[:, pl.ds(ft * i, ft)], own(4 * half + 2 * ft * i + ft, ft))
        parts[f"m{i}"] = [f"u{i}", f"d{i}"]

    def launch(name):
        for key in parts[name]:
            copies[key].wait()
        flow[name].start(0)

    stage[...] = jnp.zeros_like(stage)
    stage[0:2, 0:share] = gains[...].astype(F32)
    stage[2:7, 0:share] = biases[...].astype(F32)
    stage[7:8, 0:share] = shift2[...].astype(F32)
    n_steps, n_seq = table_t.shape[1], steps.shape[1]
    wanted = jnp.concatenate([steps[...], jnp.full((1, 128 - n_seq), -1, jnp.int32)], axis=1)
    picked = (wanted == lax.broadcasted_iota(jnp.int32, (n_steps, 128), 0)).astype(BF16)
    pack[y, z, x, c] = fold(stage[...].T[0:share] + pltpu.roll(nn(table_t[...], picked), 8, 1))
    hshare = hidden.shape[1]
    lane = lax.broadcasted_iota(jnp.int32, (hshare, NC * NY * hshare), 0) + hshare * (c * NY + y)
    place = (lane == lax.broadcasted_iota(jnp.int32, (hshare, NC * NY * hshare), 1)).astype(BF16)
    spread = nn(jnp.broadcast_to(hidden[...], (8, hshare)), place)
    n_hid = NC * NY * hshare // 128
    pieces = [spread[0:1, 128 * j : 128 * j + 128] for j in range(n_hid)]
    lines[y, z, x, c] = jnp.concatenate([*pieces, jnp.zeros((8 - n_hid, 128), F32)], axis=0)

    ready()
    launch("pack")
    launch("g0")
    copies["cot"].wait()

    def turn_cot(i, total):
        rb = row_block(i, 256)
        block = cot[rb, :]
        cot_t[:, rb] = block.T
        return total + sum_rows_of(block)

    csum = lax.fori_loop(0, rows // 256, turn_cot, jnp.zeros((1, width), F32))
    sums[...] = jnp.zeros_like(sums)
    sums[6:7, :] = csum
    flow["pack"].next(0)
    flow["g0"].next(0)
    launch("g1")
    flow["g0"].next(1)
    flow["pack"].wait(1)
    flow["g1"].next(0)
    launch("g2")
    launch("hid")
    launch("o")

    for d, (by, bz, bx, bc) in blocks():
        result[d * share : d * share + share, 0:128] = unfold(pack[by, bz, bx, bc])
    small_out[...] = result[0:width, 0:128].T
    embed = small_out[pl.ds(8 + me, 1), :]
    copies["tokens"].wait()

    def first_norm(i, _):
        rb = row_block(i, 128)
        xhat, _ = moments(tokens[rb, :].astype(F32) + embed)
        normed[rb, :] = (xhat * small_out[0:1, :] + small_out[2:3, :]).astype(BF16)
        return 0

    lax.fori_loop(0, rows // 128, first_norm, 0)
    flow["g0"].next(2)
    flow["g1"].next(1)
    flow["g2"].next(0)
    launch("m0")
    launch("m1")

    def whole(cols, size):
        return jnp.concatenate([full[by, :, :, :, :, cols].reshape(width, size) for by in range(NY)], axis=1)

    def project(group):
        cols = pl.ds(pl.multiple_of(group * 384, 128), 384)

        def body(i, _):
            rb = row_block(i, 512)
            value = nn(normed[rb, :], whole(cols, 384))
            for by in range(NY):
                to = pl.ds(pl.multiple_of((by * n_groups + group) * 128, 128), 128)
                piece = [value[:, by * 384 + 128 * j : by * 384 + 128 * j + 128] for j in range(3)]
                queries[rb, to] = (piece[0] + small_out[3:4, to]).astype(BF16) * jnp.asarray(HEAD_DIM**-0.5, BF16)
                keys_all[rb, to] = piece[1].astype(BF16)
                values_all[rb, to] = (piece[2] + small_out[4:5, to]).astype(BF16)
            return 0

        lax.fori_loop(0, rows // 512, body, 0)

    def then(name, step):
        return lambda: flow[name].next(step)

    def back(name, step):
        return lambda: sums_of[name].next(step)

    def arrived(name):
        return lambda: flow[name].wait(3)

    def off(name):
        return lambda: launch(name)

    events = {
        1: [then("g1", 2), then("g2", 1), then("o", 0), then("hid", 0)],
        3: [then("g2", 2), then("o", 1)],
        4: [then("m0", 1)],
        5: [then("o", 2)],
    }
    between = {1: [then("m0", 0)]}

    def attend(s, _):
        group, by = s // NY, lax.rem(s, NY)
        p = by * n_groups + group

        @pl.when(by == 0)
        def _():
            at_step(group, {1: [then("m1", 0)]})
            at_step(group, {g: [arrived(f"g{g}")] for g in range(n_groups)})
            project(group)
            at_step(group, between)

        at_step(s, events)
        cols = pl.ds(pl.multiple_of(p * 128, 128), 128)
        low = lax.broadcasted_iota(jnp.int32, (QB, 128), 1) < HEAD_DIM
        for i in range(rows // QB):
            n = (i + 1) * QB
            rb = slice(i * QB, n)
            key, value, query = keys_all[0:n, cols], values_all[0:n, cols], queries[rb, cols]
            outs, scales = [], []
            for h in range(2):
                scores = nt(key, jnp.where(low == (h == 0), query, jnp.zeros_like(query)))
                top = jnp.max(scores, axis=0, keepdims=True)
                expo = jnp.exp(scores - top)
                total = jnp.sum(expo, axis=0, keepdims=True)
                lse_out[pl.ds(2 * p + h, 1), rb] = top + jnp.log(total)
                scales.append(jnp.broadcast_to(1.0 / total, (HEAD_DIM, QB)))
                outs.append(tn(expo.astype(BF16), value))
            scale = jnp.concatenate(scales, axis=0).T
            mixed[rb, cols] = (jnp.where(low, outs[0], outs[1]) * scale).astype(BF16)
        return 0

    lax.fori_loop(0, width // 128, attend, 0)
    flow["o"].wait(3)
    launch("m2")
    flow["hid"].wait(1)
    for bz in range(NZ):
        for bx in range(NX):
            total = lines[0, bz, bx, 0] + lines[0, bz, bx, 1] + lines[1, bz, bx, 0] + lines[1, bz, bx, 1]
            for j in range(n_hid):
                at = ((bz * NX + bx) * n_hid + j) * 128
                hid[0:1, at : at + 128] = total[j : j + 1]

    at = len(copies)

    def middle_save(i):
        rb = row_block(i, 256)
        return pltpu.make_async_copy(result.at[rb], middle_hbm.at[rb], local.at[at + 10 + i])

    def second_norm(i, _):
        at_step(i, {2: [then("m0", 2)]})
        rb = row_block(i, 256)
        start_h = tokens[rb, :].astype(F32) + embed
        value = start_h + (nt(mixed[rb, :], whole(col["o"], half)) + small_out[5:6, :])
        result[rb, :] = value
        middle_save(i).start()
        gsec[rb, :] = jnp.zeros_like(value)
        xhat, _ = moments(value)
        block = (xhat * small_out[1:2, :] + small_out[7:8, :]).astype(BF16)
        second[rb, :] = block
        second_t[:, rb] = block.T
        return 0

    lax.fori_loop(0, rows // 256, second_norm, 0)
    flow["m1"].next(1)
    flow["m0"].wait(3)
    for i in range(rows // 256):
        middle_save(i).wait()

    free = 4 * half
    half_f = 2 * ft
    places = {"m0": (0, free, half_f), "m1": (1, free, half_f), "m2": (0, free + half_f, half_f), "o": (1, free + half_f, half)}
    for g in range(n_groups):
        places[f"q{g}"] = (g % 2, free + 2 * half_f + 384 * (g // 2), 384)
    sums_of = {}
    before = {"m0": "g0", "m1": "g1", "m2": "g2", "o": "o", "q0": "m0", "q1": "m2", "q2": "m1", "pack": "pack", "hid": "hid"}
    for i, name in enumerate([*places, "pack", "hid"]):
        gather = flow[before[name]]
        sems = (gather.send, gather.recv, pos)
        if name in places:
            core, start, size = places[name]
            own_view = full.at[:, :, :, core, :, pl.ds(start, size)]
            bufs = rest[6 * i : 6 * i + 6]
            if name[0] == "m":
                source = gtile
            else:
                source = gtile.at[:, :, :, :, :, pl.ds(0 if name in ("o", "q1") else half, 384)]
            sums_of[name] = Scatter(source, own_view, bufs, *sems, gather.order)
        else:
            sums_of[name] = SmallScatter(*(rest[-11:-7] if name == "pack" else rest[-7:-3]), *sems)
    tiles = NY * n_ff

    def tile(t, _):
        ty, tm = lax.rem(t, NY), t // NY
        slot = lax.rem(t, 2)

        def begin(name):
            return lambda: sums_of[name].start(0)

        def first_sum(name):
            return lambda: sums_of[name].first_sum()

        def second_step(name):
            return lambda: sums_of[name].start(1)

        at_step(
            t,
            {
                1: [then("m2", 0)],
                2: [flow["g0"].drain, begin("m0"), flow["m0"].drain, then("m2", 1), arrived("m1")],
                4: [flow["g1"].drain, begin("m1"), arrived("m2")],
            },
        )

        up_at = pl.ds(pl.multiple_of(4 * half + tm * 2 * ft, 128), ft)
        down_at = pl.ds(pl.multiple_of(4 * half + tm * 2 * ft + ft, 128), ft)
        hid_at = pl.ds(pl.multiple_of(ty * ffh + tm * ft, 128), ft)

        def up():
            return full[ty, :, :, :, :, up_at].reshape(width, ft)

        def down():
            return full[ty, :, :, :, :, down_at].reshape(width, ft)

        pre = nn(second[...], up()) + hid[:, hid_at]
        gact = nn(cot[...], down())
        value, slope = gelu_parts(pre)
        act[...] = value.astype(BF16)
        grad = (gact * slope).astype(BF16)
        gpre[...] = grad
        ghid_out[:, hid_at] = sum_rows_of(grad)
        result[...] += nt(act[...], down())
        gsec[...] += nt(gpre[...], up())

        def results():
            second[...] = (result[...] + small_out[6:7, :]).astype(BF16)
            layer_save.start()
            middle_load.start()

        at_step(
            t,
            {
                1: [then("m1", 2)],
                2: [first_sum("m0")],
                3: [then("m2", 2), second_step("m0")],
                4: [first_sum("m1"), second_step("m1")],
                tiles - 1: [results, back("m0", 1)],
            },
        )

        turn = (NZ, NX, NC, per, ft)
        gtile[slot, :, :, :, :, 0:ft] = nn(second_t[...], gpre[...]).astype(BF16).reshape(turn)
        gtile[slot, :, :, :, :, ft : 2 * ft] = nn(cot_t[...], act[...]).astype(BF16).reshape(turn)
        return 0

    layer_save = pltpu.make_async_copy(second, layer_out, local.at[at + 5])
    middle_load = pltpu.make_async_copy(middle_hbm, result, local.at[at + 6])
    lax.fori_loop(0, tiles, tile, 0)
    for name in ("g2", "m1", "m2", "hid"):
        flow[name].drain()
    sums_of["m2"].start(0)
    reload = [
        pltpu.make_async_copy(tokens_in.at[:, pl.ds(0, ft)], act, local.at[at + 7]),
        pltpu.make_async_copy(tokens_in.at[:, pl.ds(ft, width - ft)], gpre.at[:, pl.ds(0, width - ft)], local.at[at + 8]),
    ]
    for load in reload:
        load.start()
    for d, (by, bz, bx, bc) in blocks():
        start = (bz * NX + bx) * n_hid
        pieces = [ghid_out[:, 128 * (start + j) : 128 * (start + j + 1)] for j in range(n_hid)]
        sums_of["hid"].source[by, bz, bx, bc] = jnp.concatenate([*pieces, jnp.zeros((8 - n_hid, 128), F32)], axis=0)
    sums_of["hid"].start(0)
    layer_save.wait()
    middle_load.wait()
    gattn, gattn_t, normed_t, gmixed = second, cot_t, second_t, tokens
    gq, gk, gv = second, normed, cot
    def second_back(i, totals):
        rb = row_block(i, 128)
        xhat, scale = moments(result[rb, :])
        grad = gsec[rb, :]
        total = cot[rb, :].astype(F32) + norm_back(xhat, scale, grad * small_out[1:2, :])
        gsec[rb, :] = total
        low = total.astype(BF16)
        gattn[rb, :] = low
        gattn_t[:, rb] = low.T
        return (
            totals[0] + sum_rows_of(grad * xhat),
            totals[1] + sum_rows_of(grad),
            totals[2] + sum_rows_of(low),
        )

    zero = jnp.zeros((1, width), F32)
    ggain2, gshift2, gattn_sum = lax.fori_loop(0, rows // 128, second_back, (zero, zero, zero))
    sums[1:2, :] = ggain2
    sums[5:6, :] = gattn_sum
    sums[7:8, :] = gshift2

    def weight(index):
        picks = [
            full[by, :, :, :, :, pl.ds(384 * g + 128 * index, 128)].reshape(width, 128)
            for by in range(NY)
            for g in range(n_groups)
        ]
        return jnp.concatenate(picks, axis=1)

    flow["pack"].drain()
    flow["o"].drain()
    sums_of["m1"].next(1)
    sums_of["m2"].next(0)

    def out_grad(i, _):
        part = nn(gattn_t[row_block(i, 384), :], mixed[...]).astype(BF16)
        for by in range(NY):
            to = part[:, by * half : by * half + half].reshape(2, NX, NC, per, half)
            gtile[by, pl.ds(i * 2, 2), :, :, :, 0:half] = to
        return 0

    lax.fori_loop(0, width // 384, out_grad, 0)
    sums_of["o"].start(0)
    sums_of["m0"].next(2)

    def mixed_grad(i, _):
        rb = row_block(i, 512)
        gmixed[rb, :] = nn(gattn[rb, :], whole(col["o"], half)).astype(BF16)
        return 0

    lax.fori_loop(0, rows // 512, mixed_grad, 0)
    sums_of["o"].next(0)

    def turn_normed(i, _):
        rb = row_block(i, 256)
        normed_t[:, rb] = normed[rb, :].T
        return 0

    lax.fori_loop(0, rows // 256, turn_normed, 0)
    events_back = {
        1: [back("m1", 2)],
        3: [back("m2", 1), back("q0", 0), back("o", 1), sums_of["hid"].next],
        4: [back("m2", 2)],
        5: [back("q0", 1), back("o", 2), back("q1", 0)],
    }

    def attend_back(s, _):
        group, by = s // NY, lax.rem(s, NY)
        p = by * n_groups + group
        at_step(s, events_back)
        cols = pl.ds(pl.multiple_of(p * 128, 128), 128)
        dots = (gmixed[:, cols].astype(F32) * mixed[:, cols].astype(F32)).T
        for h in range(2):
            inner[h : h + 1, :] = jnp.sum(dots[HEAD_DIM * h : HEAD_DIM * (h + 1)], axis=0, keepdims=True)
        for j in range(rows // QB):
            kb, first = slice(j * QB, (j + 1) * QB), j * QB
            later = rows - first
            key, value = keys_all[kb, cols], values_all[kb, cols]
            low = lax.broadcasted_iota(jnp.int32, (later, 128), 1) < HEAD_DIM

            def two(block):
                none = jnp.zeros_like(block)
                return jnp.concatenate([jnp.where(low, block, none), jnp.where(low, none, block)], axis=0)

            query, grad = two(queries[first:rows, cols]), two(gmixed[first:rows, cols])
            logs = jnp.concatenate([lse_out[pl.ds(2 * p + h, 1), first:rows] for h in range(2)], axis=1)
            inners = jnp.concatenate([inner[h : h + 1, first:rows] for h in range(2)], axis=1)
            probs = jnp.exp(nt(key, query) - logs)
            gscores = (probs * (nt(value, grad) - inners)).astype(BF16)
            gv[kb, cols] = nn(probs.astype(BF16), grad).astype(BF16)
            gk[kb, cols] = nn(gscores, query).astype(BF16)
            both = tn(gscores, key)
            more = jnp.where(low, both[:later], both[later:])
            if j == 0:
                acc[...] = more
            else:
                acc[first:rows] += more
        gq[:, cols] = (acc[...] * HEAD_DIM**-0.5).astype(BF16)

        @pl.when(by == NY - 1)
        def _():
            offset = lax.rem(group + 1, 2) * half
            for piece, source in enumerate((gq, gk, gv)):
                pick = jnp.concatenate(
                    [source[:, pl.ds(pl.multiple_of((b * n_groups + group) * 128, 128), 128)] for b in range(NY)], axis=1
                )
                part = nn(normed_t[...], pick).astype(BF16)
                for b in range(NY):
                    to = pl.ds(pl.multiple_of(offset + piece * 128, 128), 128)
                    gtile[b, :, :, :, :, to] = part[:, b * 128 : b * 128 + 128].reshape(NZ, NX, NC, per, 128)
            at_step(group, {g: [lambda g=g: sums_of[f"q{g}"].start(0)] for g in range(n_groups)})
            at_step(group, {n_groups - 1: [back("q0", 2), back("q1", 1)]})

        return 0

    lax.fori_loop(0, NY * n_groups, attend_back, 0)
    for load in reload:
        load.wait()

    def m_final(i):
        def run():
            total = sums_of[f"m{i}"].final()
            gup[:, ft * i : ft * i + ft] = total[:, 0:ft]
            gdown[:, ft * i : ft * i + ft] = total[:, ft:]

        return run

    owners = {}
    for i, (name, src, dst) in enumerate([("gup", gup, gup_out), ("gdown", gdown, gdown_out), ("gout", gout, gout_out), ("gqkv", gqkv, gqkv_out)]):
        owners[name] = pltpu.make_async_copy(src, dst, local.at[at + 14 + i])

    def first_back(i, totals):
        rb = row_block(i, 256)
        block = jnp.concatenate([act[rb, :], gpre[rb, 0 : width - ft]], axis=1)
        xhat, scale = moments(block.astype(F32) + embed)
        q_rows, k_rows, v_rows = gq[rb, :], gk[rb, :], gv[rb, :]
        grad = nt(q_rows, weight(0)) + nt(k_rows, weight(1)) + nt(v_rows, weight(2))
        total = gsec[rb, :] + norm_back(xhat, scale, grad * small_out[0:1, :])
        mixed[rb, :] = total.astype(BF16)

        at_step(
            i,
            {0: [back("q2", 0)], 1: [m_final(0), back("q1", 2)], 2: [back("q2", 1), m_final(1)]},
        )
        return (
            totals[0] + sum_rows_of(grad * xhat),
            totals[1] + sum_rows_of(grad),
            totals[2] + sum_rows_of(q_rows),
            totals[3] + sum_rows_of(v_rows),
            totals[4] + sum_rows_of(total),
        )

    ggain1, gshift1, q_sum, v_sum, seq_sum = lax.fori_loop(0, rows // 256, first_back, (zero,) * 5)
    sums[0:1, :] = ggain1
    sums[2:3, :] = gshift1
    sums[3:4, :] = q_sum
    sums[4:5, :] = v_sum
    sums[pl.ds(8 + me, 1), :] = seq_sum
    gtok = pltpu.make_async_copy(mixed, gtok_out, local.at[at + 9])
    gtok.start()
    turned = sums[...].T
    for d, (by, bz, bx, bc) in blocks():
        sums_of["pack"].source[by, bz, bx, bc] = fold(turned[d * share : d * share + share])
    sums_of["pack"].start(0)
    last = f"q{n_groups - 1}"
    sums_of[last].next(2)
    for i in range(2, n_ff):
        m_final(i)()
    owners["gup"].start()
    owners["gdown"].start()
    sums_of["pack"].next()
    gout[...] = sums_of["o"].final()
    owners["gout"].start()
    gpack_out[8:16] = sums_of["hid"].final()

    def qkv_final(g):
        total = sums_of[f"q{g}"].final()
        for piece in range(3):
            gqkv[piece, :, 128 * g : 128 * g + 128] = total[:, 128 * piece : 128 * piece + 128]

    for g in range(n_groups - 1):
        qkv_final(g)
    for name, each in sums_of.items():
        if name not in ("pack", last):
            each.drain()
    qkv_final(n_groups - 1)
    owners["gqkv"].start()
    gpack_out[0:8] = sums_of["pack"].final()
    gtok.wait()
    sums_of[last].drain()
    sums_of["pack"].drain()
    for each in owners.values():
        each.wait()


def finish_kernel(slots, count, steps, gpack, *refs):
    large, (gains_out, biases_out, shift_out, hidden_out, table_out) = refs[:count], refs[count : count + 5]
    outs, rest = refs[count + 5 : 2 * count + 5], refs[2 * count + 5 :]
    bufs, wide, (load_sem, save_sem) = rest[:count], rest[count], rest[-2:]
    pieces = []
    for src, buf, out in zip(large, bufs, outs):
        cut = 4 if src.shape[0] % 512 == 0 else 1
        size = src.shape[0] // cut
        for k in range(cut):
            at, n = pl.ds(k * size, size), len(pieces)
            held = buf if src.dtype == out.dtype else wide
            load = pltpu.make_async_copy(src.at[at], buf.at[at], load_sem.at[n])
            pieces.append((load, pltpu.make_async_copy(held.at[at], out.at[at], save_sem.at[n]), held is wide and at))
    for load, _, _ in pieces:
        load.start()
    share, hshare = gains_out.shape[1], hidden_out.shape[1]
    features = unfold(gpack[0:8, :])
    turned = jnp.concatenate([features, jnp.zeros((128 - share, 128), F32)], axis=0).T
    gains_out[...] = turned[0:2, 0:share]
    biases_out[...] = turned[2:7, 0:share]
    shift_out[...] = turned[7:8, 0:share]
    slot = lax.rem(lax.axis_index("dp"), NC) * NY + lax.axis_index("tensor")
    line = jnp.concatenate([gpack[8 + j : 9 + j, :] for j in range(slots * hshare // 128)], axis=1)
    value = line[:, 0:hshare]
    for k in range(1, slots):
        value = jnp.where(slot == k, line[:, hshare * k : hshare * k + hshare], value)
    hidden_out[...] = value
    for load, save, at in pieces:
        load.wait()
        if at:
            wide[at, :] = bufs[0][at, :].astype(F32)
        save.start()
    n_steps, n_seq = table_out.shape[1], steps.shape[1]
    picked = (steps[...] == lax.broadcasted_iota(jnp.int32, (n_steps, n_seq), 0)).astype(F32)
    table_out[...] = lax.dot_general(
        features[:, 8 : 8 + n_seq], picked, (((1,), (1,)), ((), ())), precision=HIGH, preferred_element_type=F32
    )
    for _, save, _ in pieces:
        save.wait()


def fast_shards(
    tokens,
    timesteps,
    norm_gains,
    biases,
    second_shift,
    hidden_bias,
    step_table,
    qkv_weight,
    out_weight,
    up_weight,
    down_weight,
    cotangent,
):
    rows, width = tokens.shape
    _, per, half = qkv_weight.shape
    ffh = up_weight.shape[1]
    ft = 512
    dims = (rows, width, per, half, ffh, ft)
    n_ff, n_groups = ffh // ft, half // 128
    total = 4 * half + 2 * ffh
    vmem, anywhere = pl.BlockSpec(memory_space=pltpu.VMEM), pl.BlockSpec(memory_space=pl.ANY)
    shape = jax.ShapeDtypeStruct
    low, wide = shape((rows, width), BF16), shape((rows, width), F32)
    vm = pltpu.VMEM
    hshare = hidden_bias.shape[0]
    steps = timesteps.reshape(1, -1)
    chunks = [2 * ft] * n_ff + [half] * (1 + n_groups)
    scratch = []
    for cols in chunks:
        scratch += scatter_scratch(per, cols, BF16)
    n_sems = 2 * 10 + 8 * (n_groups + n_ff) + 11
    owned = [shape((per, ffh), F32), shape((per, ffh), F32), shape((per, half), F32), shape((3, per, half), F32)]
    gpack, gup, gdown, gout, gqkv, gtok, layer, _ = pl.pallas_call(
        functools.partial(layer_kernel, dims),
        in_specs=[vmem] * 6 + [anywhere] * 6,
        out_specs=[vmem] + [anywhere] * 7,
        out_shape=[
            shape((16, 128), F32),
            *owned,
            low,
            low,
            wide,
        ],
        scratch_shapes=[
            vm((128, width), F32),
            vm((16, rows), F32),
            vm((1, NY * ffh), F32),
            vm((NY, NZ, NX, NC, per, total), BF16),
            vm((NY, NZ, NX, NC, 8, 128), F32),
            vm((NY, NZ, NX, NC, 8, 128), F32),
            vm((128, 128), F32),
            vm((rows, width), BF16),
            vm((rows, width), BF16),
            vm((rows, width), BF16),
            vm((rows, width), BF16),
            vm((rows, width), BF16),
            vm((rows, width), BF16),
            vm((rows, width), BF16),
            vm((rows, width), BF16),
            vm((width, rows), BF16),
            vm((width, rows), BF16),
            vm((rows, width), F32),
            vm((rows, width), F32),
            vm((rows, ft), BF16),
            vm((rows, ft), BF16),
            vm((2, NZ, NX, NC, per, 2 * ft), BF16),
            vm((1, NY * ffh), F32),
            vm((rows, 128), F32),
            vm((8, rows), F32),
            vm((128, width), F32),
            *[vm(each.shape, F32) for each in owned],
            *scratch,
            *small_scratch(),
            *small_scratch(),
            pltpu.SemaphoreType.DMA((n_sems,)),
            pltpu.SemaphoreType.DMA((n_sems,)),
            pltpu.SemaphoreType.DMA((24 + 3 * n_groups + 2 * n_ff,)),
        ],
        compiler_params=pltpu.CompilerParams(collective_id=0, has_side_effects=True, vmem_limit_bytes=VMEM_LIMIT),
        name="layer",
    )(
        steps,
        norm_gains,
        biases,
        second_shift.reshape(1, -1),
        hidden_bias.reshape(1, -1),
        step_table.T,
        tokens,
        qkv_weight,
        out_weight.T,
        up_weight,
        down_weight.T,
        cotangent,
    )
    share, n_steps = norm_gains.shape[1], step_table.shape[0]
    large = (gtok, layer, gqkv, gout, gup, gdown)
    pieces = sum(4 if array.shape[0] % 512 == 0 else 1 for array in large)
    small_shapes = [(2, share), (5, share), (1, share), (1, hshare), (share, n_steps)]
    large_shapes = [wide, *[shape(array.shape, array.dtype) for array in large[1:]]]
    grad_gains, grad_biases, grad_shift, grad_hidden, grad_table, gtok, layer, gqkv, gout, gup, gdown = pl.pallas_call(
        functools.partial(finish_kernel, NC * NY, len(large)),
        in_specs=[vmem] * 2 + [anywhere] * len(large),
        out_specs=[vmem] * 5 + [anywhere] * len(large),
        out_shape=[shape(dims, F32) for dims in small_shapes] + large_shapes,
        scratch_shapes=[vm(array.shape, array.dtype) for array in large]
        + [vm(wide.shape, F32)]
        + [pltpu.SemaphoreType.DMA((pieces,))] * 2,
        name="finish",
    )(steps, gpack, *large)
    return (
        layer,
        gtok,
        grad_gains,
        grad_biases,
        grad_shift.reshape(share),
        grad_hidden.reshape(hshare),
        grad_table.T,
        gqkv,
        gout.T,
        gup,
        gdown.T,
    )


def solution(mesh):
    in_specs = (
        P(("dp", "tensor"), None),
        P(),
        P(None, ("dp", "tensor")),
        P(None, ("dp", "tensor")),
        P(("dp", "tensor")),
        P(("dp", "tensor")),
        P(None, ("dp", "tensor")),
        P(None, "dp", "tensor"),
        P("tensor", "dp"),
        P("dp", "tensor"),
        P("tensor", "dp"),
        P(("dp", "tensor"), None),
    )
    out_specs = (
        P(("dp", "tensor"), None),
        P(("dp", "tensor"), None),
        P(None, ("dp", "tensor")),
        P(None, ("dp", "tensor")),
        P(("dp", "tensor")),
        P(("dp", "tensor")),
        P(None, ("dp", "tensor")),
        P(None, "dp", "tensor"),
        P("tensor", "dp"),
        P("dp", "tensor"),
        P("tensor", "dp"),
    )
    fast = mesh.shape["dp"] == NZ * NX * NC and mesh.shape["tensor"] == NY
    return jax.shard_map(fast_shards if fast else shards, mesh=mesh, in_specs=in_specs, out_specs=out_specs, check_vma=False)
```
